32 devices in a mesh: expert: 8 (over z, y), hidden: 4 (over x, core).
Axes of the slice: x: 2, y: 2, z: 4, core: 2. Of those that a mesh axis runs over, the one named last changes fastest.
Arguments:
- tokens: bfloat16 [2, 6144, 768], P(None, 'expert'), may hold values from -6 to 6
- doc_ids: int32 [2, 8, 768], P(None, 'expert'), may hold values from 0 to 3, never falling along the last dimension, each value on 1 to 384 neighbouring positions
- pad_mask: int32 [2, 6144], P(None, 'expert'), may hold values 0 or 1
- norm1_gain: float32 [768], replicated, may hold values from 0.5 to 1.5
- norm1_bias: float32 [768], replicated, may hold values from -1 to 1
- qkv_weight: bfloat16 [3, 768, 768], P(None, None, 'hidden'), may hold values from -0.3125 to 0.3125
- out_weight: bfloat16 [768, 768], P('hidden'), may hold values from -0.875 to 0.875
- norm2_gain: float32 [768], replicated, may hold values from 0.5 to 1.5
- norm2_bias: float32 [768], replicated, may hold values from -1 to 1
- router: bfloat16 [768, 8], replicated, may hold values from -0.15625 to 0.15625
- routes: int32 [2, 6144, 2], P(None, 'expert'), may hold values from 0 to 7, all different within a row; in each aligned block of 768 rows (0 to 767, 768 to 1535, ..., all dimensions but the last counted through in order) at most 384 rows name the same one
- up_weight: bfloat16 [8, 768, 3072], P('expert', None, 'hidden'), may hold values from -0.21875 to 0.21875
- down_weight: bfloat16 [8, 768, 3072], P('expert', None, 'hidden'), may hold values from -0.15625 to 0.15625
- cotangent: bfloat16 [2, 6144, 768], P(None, 'expert'), may hold values from -6 to 6
Outputs:
- block_out: float32 [2, 6144, 768], P(None, 'expert')
- grad_tokens: float32 [2, 6144, 768], P(None, 'expert')
- grad_norm1_gain: float32 [768], replicated
- grad_norm1_bias: float32 [768], replicated
- grad_qkv: float32 [3, 768, 768], P(None, None, 'hidden')
- grad_out: float32 [768, 768], P('hidden')
- grad_norm2_gain: float32 [768], replicated
- grad_norm2_bias: float32 [768], replicated
- grad_router: float32 [768, 8], replicated
- grad_up: float32 [4, 768, 3072], P(None, 'expert', 'hidden')
- grad_down: float32 [4, 768, 3072], P(None, 'expert', 'hidden')
The draws below stay inside these ranges and needn't reach their ends.
Inputs may be any that keep to these rules, and one draw needn't show every extreme that they name: `routes`: each token names 2 different experts. In each micro-batch the tokens of one pack name any one expert at most 384 times, a bound that some block reaches. `doc_ids`: within a pack document numbers never fall; each document covers 1 to 384 consecutive tokens, and some covers exactly 384. `pad_mask`: 1 marks a real token, 0 a padding token.
All inputs are finite; a program needn't handle non-finite values. No bound on the sum of `pad_mask` on one device may be relied on, other than what follows from the above.
Results may differ from the reference program's by a relative error of at most 0.028.
Values may be sent and summed in bfloat16 or wider, within the bound.
No kernel may reach another device: no remote copies, remote signals or barrier semaphores. Data moves between devices by JAX's collectives and lax.ppermute only.
A program may use at most 256 MiB of HBM per device.

```python
import math
from functools import partial
import jax
import jax.numpy as jnp
import numpy as np
from jax import lax

D = 768
FF = 3072
HEADS = 12
HEAD_DIM = 64
TOP = 2
MB = 2
DOCS = 4
ROWS = 768
EXPERTS = 8
TRAIN = 4
PACKS = 8
TOKENS = 6144
CAP = 384
LONGEST = 384
N_HIDDEN = 4


def plant(array, key, low, high):
    longest = array.shape.index(max(array.shape))
    spots = []
    for shift in (0, 1):
        where = [jax.random.randint(jax.random.fold_in(key, axis), (), 0, length) for axis, length in enumerate(array.shape)]
        where[longest] = (where[longest] + shift) % array.shape[longest]
        spots.append(tuple(where))
    return array.at[spots[0]].set(low).at[spots[1]].set(high)


def shard_levels(key, dims, shards, least, top_value):
    factor_of = 1.0
    for dim, parts in shards:
        draws = jax.random.uniform(jax.random.fold_in(jax.random.fold_in(key, 6), dim), (parts,), jnp.float32, least / len(shards), top_value / len(shards))
        factor_of = factor_of * jnp.repeat(jnp.exp(draws), dims[dim] // parts).reshape((-1,) + (1,) * (len(dims) - 1 - dim))
    return factor_of


def length_profile(count, total, reach, lean):
    weights = [(1 << 20) // math.isqrt(standing ** lean) + 1 for standing in range(2, count + 1)]
    surplus, given = total - reach - (count - 1), [1] * (count - 1)
    while surplus > 0:
        movable = [i for i in range(count - 1) if given[i] < reach]
        mass, left = sum([weights[i] for i in movable]), surplus
        for i in movable:
            extra = min(reach - given[i], max(1, left * weights[i] // mass), surplus)
            given[i] = given[i] + extra
            surplus = surplus - extra
    return np.array([reach] + given)


def ragged(stream_key, count, total, limit, skew):
    if count == 2:
        one = jax.random.randint(stream_key, (), max(1, total - limit), min(limit, total - 1) + 1)
        return jnp.stack([one, total - one])
    sizes = jnp.asarray(length_profile(count, total, limit, skew), jnp.int32)
    twos = (count - 1) // 2
    donor, receiver = sizes[1:1 + 2 * twos:2], sizes[2:2 + 2 * twos:2]
    room = jnp.minimum(donor - 1, limit - receiver)
    moved = jax.random.randint(jax.random.fold_in(stream_key, 1), (twos,), 0, 1 << 20) % (room + 1)
    sizes = sizes.at[1:1 + 2 * twos:2].set(donor - moved).at[2:2 + 2 * twos:2].set(receiver + moved)
    return sizes[jax.random.permutation(jax.random.fold_in(stream_key, 2), count)]


def assign_block(stream_key, own, number, rows, amount, top, reach, slope):
    ranking = jax.random.permutation(stream_key, amount)
    heavy_load, ordinary = shares(amount, rows * top, reach, slope, True), shares(amount, rows * top, reach, slope, False)
    places = jnp.arange(amount)

    def named(tallies, turn):
        used = int((tallies > 0).sum())
        fixed = max(1, used // 4)
        moved = fixed + (places - fixed + turn * (used - fixed)) % max(1, amount - fixed)
        return jnp.zeros((amount,), jnp.int32).at[ranking[jnp.where(places < fixed, places, moved)]].set(jnp.asarray(tallies, jnp.int32))

    tallies = jnp.where(number % 4 == 0, named(heavy_load, number // 4), named(ordinary, number - number // 4 - 1))
    mixed = jax.random.permutation(jax.random.fold_in(own, 3), amount)
    donor, sink = mixed[0:amount // 2 * 2:2], mixed[1:amount // 2 * 2:2]
    margin = jnp.minimum(tallies[donor] - 1, reach - tallies[sink]) // 2
    margin = jnp.where((donor == ranking[0]) | (sink == ranking[0]) | (tallies[sink] == 0), 0, jnp.maximum(margin, 0))
    moved = jax.random.randint(jax.random.fold_in(own, 4), (amount // 2,), 0, 1 << 20) % (margin + 1)
    tallies = tallies.at[donor].add(-moved).at[sink].add(moved)
    items = jnp.searchsorted(jnp.cumsum(tallies), jnp.arange(rows * top), side="right").astype(jnp.int32)
    listing = items.reshape(top, rows).T
    listing = listing[jax.random.permutation(jax.random.fold_in(own, 1), rows)]
    turn = jax.random.randint(jax.random.fold_in(own, 2), (rows, 1), 0, top)
    return jnp.take_along_axis(listing, (jnp.arange(top)[None, :] + turn) % top, axis=1)


def shares(amount, total, limit, slope, full):
    weights = [(1 << 20) // math.isqrt(standing ** slope) + 1 for standing in range(1, amount + 1)]
    largest = limit if full else min(limit, max(-(-total // amount), total * weights[0] // sum(weights)))
    least = 1 if total - largest >= amount - 1 else 0
    given, rest = [largest] + [least] * (amount - 1), total - largest - least * (amount - 1)
    while rest > 0:
        movable = [i for i in range(1, amount) if given[i] < largest] or [i for i in range(1, amount) if given[i] < limit]
        whole, remaining = sum([weights[i] for i in movable]), rest
        for i in movable:
            more = min(limit - given[i], max(1, remaining * weights[i] // whole), rest)
            given[i] = given[i] + more
            rest = rest - more
    return np.array(given)


def noise(stream_key, shape, deviation, reach, cuts=(), held_as=jnp.bfloat16):
    loudness = shard_levels(stream_key, shape, cuts, -0.22, 0.18) if cuts else 1.0
    values = jax.random.normal(stream_key, shape, jnp.float32) * deviation * loudness
    return jnp.minimum(jnp.maximum(values, -reach), reach).astype(held_as)


def setup_inputs(seed: int = 0) -> dict:
    arg_keys = jax.random.split(jax.random.key(seed), 15)
    tokens = noise(arg_keys[0], (MB, TOKENS, D), 1.0, 6.0, ((1, 8),))
    doc_ids = jax.vmap(lambda own: jnp.searchsorted(jnp.cumsum(ragged(own, DOCS, ROWS, LONGEST, 2)), jnp.arange(ROWS), side="right"))(jax.random.split(arg_keys[1], MB * PACKS)).reshape((MB, PACKS, ROWS)).astype(jnp.int32)
    pad_mask = plant((jax.random.randint(arg_keys[2], (MB, TOKENS), 0, 8) < 7).astype(jnp.int32), jax.random.fold_in(arg_keys[2], 1), 0, 1)
    norm1_gain = jnp.clip(1.0 + 0.1 * jax.random.normal(arg_keys[3], (D,), jnp.float32), 0.5, 1.5)
    norm1_bias = noise(arg_keys[4], (D,), 0.2, 1.0, (), jnp.float32)
    qkv_weight = noise(arg_keys[5], (3, D, D), (D // 2) ** -0.5, 0.3125, ((2, 4),))
    out_weight = noise(arg_keys[6], (D, D), (D // 16) ** -0.5, 0.875, ((0, 4),))
    norm2_gain = jnp.clip(1.0 + 0.1 * jax.random.normal(arg_keys[7], (D,), jnp.float32), 0.5, 1.5)
    norm2_bias = noise(arg_keys[8], (D,), 0.2, 1.0, (), jnp.float32)
    router = noise(arg_keys[9], (D, EXPERTS), (2 * D) ** -0.5, 0.15625)
    routes_keys = jax.random.split(jax.random.fold_in(arg_keys[10], 1), MB * TOKENS // ROWS)
    routes_turns = jax.random.permutation(jax.random.fold_in(arg_keys[10], 3), MB * TOKENS // ROWS)
    routes = jax.vmap(lambda own, number: assign_block(jax.random.fold_in(arg_keys[10], 2), own, number, ROWS, EXPERTS, TOP, CAP, 2))(routes_keys, routes_turns).reshape((MB, TOKENS, TOP))
    up_weight = noise(arg_keys[11], (EXPERTS, D, FF), D ** -0.5, 0.21875, ((0, 8), (2, 4)))
    down_weight = noise(arg_keys[12], (EXPERTS, D, FF), (FF // 2) ** -0.5, 0.15625, ((0, 8), (2, 4)))
    cotangent = noise(arg_keys[13], (MB, TOKENS, D), 1.0, 6.0, ((1, 8),))
    return {"tokens": tokens, "doc_ids": doc_ids, "pad_mask": pad_mask, "norm1_gain": norm1_gain, "norm1_bias": norm1_bias, "qkv_weight": qkv_weight, "out_weight": out_weight, "norm2_gain": norm2_gain, "norm2_bias": norm2_bias, "router": router, "routes": routes, "up_weight": up_weight, "down_weight": down_weight, "cotangent": cotangent}


@jax.custom_vjp
def low(v):
    return lax.optimization_barrier(v.astype(jnp.bfloat16)).astype(jnp.float32)

@jax.custom_vjp
def low_back(v):
    return v

def low_keep(v):
    return (low(v), None)

def low_pass(kept, grad):
    return (grad,)

def back_keep(v):
    return (v, None)

def back_low(kept, grad):
    return (low(grad),)
low.defvjp(low_keep, low_pass)
low_back.defvjp(back_keep, back_low)
EPSILON = 1e-05
PRECISE = lax.Precision.HIGHEST
MASKED = -1e+30

def layer_norm(values, norm_gain, norm_bias):
    centre = values - lax.optimization_barrier(jnp.mean(values, -1, keepdims=True))
    spread = lax.optimization_barrier(jnp.mean(centre * centre, -1, keepdims=True))
    return centre * lax.rsqrt(spread + EPSILON) * norm_gain + norm_bias

def visible(doc_row, pad_row):
    total_rows = doc_row.shape[0]
    query_pos = jnp.arange(total_rows)[:, None]
    key_pos = jnp.arange(total_rows)[None, :]
    same_doc = doc_row[:, None] == doc_row[None, :]
    is_real = (pad_row[None, :] == 1) | (query_pos == key_pos)
    return (key_pos <= query_pos) & same_doc & is_real

def slot_tables(route_rows, experts, capacity):
    flat_routes = route_rows.reshape(-1)
    onehot = (flat_routes[:, None] == jnp.arange(experts, dtype=jnp.int32)[None, :]).astype(jnp.int32)
    before = jnp.cumsum(onehot, 0) - onehot
    placed = lax.optimization_barrier(jnp.sum(before * onehot, 1))
    slot_index = flat_routes * capacity + placed
    total_rows = flat_routes.shape[0]
    source = jnp.full((experts * capacity,), total_rows, jnp.int32).at[slot_index].set(jnp.arange(total_rows, dtype=jnp.int32))
    return (slot_index, source)

def take_rows(row_table, row_index):
    return row_table[row_index]

def attend_pack(pieces):
    queries, key_rows, value_rows, doc_row, pad_row = pieces
    allowed = visible(doc_row, pad_row)
    scores = jnp.einsum('qhd,khd->hqk', queries, key_rows, precision=PRECISE) * HEAD_DIM ** (-0.5)
    scores = low_back(scores)
    scores = jnp.where(allowed[None], scores, MASKED)
    exponent = jnp.exp(scores - lax.optimization_barrier(jnp.max(scores, -1, keepdims=True)))
    attn_weights = exponent / lax.optimization_barrier(jnp.sum(exponent, -1, keepdims=True))
    return jnp.einsum('hqk,khd->qhd', low(attn_weights), value_rows, precision=PRECISE)

def block_forward(params, inputs, doc_rows, pad_rows, route_rows, slot_index, source):
    norm1_gain, norm1_bias, qkv_weight, out_weight, norm2_gain, norm2_bias, router, up_weight, down_weight = params
    attn_in = low(layer_norm(inputs, norm1_gain, norm1_bias))
    projected = jnp.einsum('td,cdf->ctf', attn_in, qkv_weight, precision=PRECISE)
    projected = low_back(low(projected))
    head_view = projected.reshape(3, PACKS, ROWS, HEADS, HEAD_DIM)
    heads_out = lax.map(jax.checkpoint(attend_pack), (head_view[0], head_view[1], head_view[2], doc_rows, pad_rows))
    heads_low = low_back(low(heads_out.reshape(TOKENS, D)))
    attention = low_back(jnp.dot(heads_low, out_weight, precision=PRECISE))
    residual = inputs + attention
    moe_in = low(layer_norm(residual, norm2_gain, norm2_bias))
    logits = jnp.dot(moe_in, router, precision=PRECISE)
    chosen = jnp.take_along_axis(logits, route_rows, axis=1)
    shifted = jnp.exp(chosen - lax.optimization_barrier(jnp.max(chosen, -1, keepdims=True)))
    gate_vals = shifted / lax.optimization_barrier(jnp.sum(shifted, -1, keepdims=True))
    copies = low_back(jnp.broadcast_to(moe_in[:, None, :], (TOKENS, TOP, D)))
    padded = jnp.concatenate([copies.reshape(PACKS, ROWS * TOP, D), jnp.zeros((PACKS, 1, D), jnp.float32)], 1)
    buffer = jax.vmap(take_rows)(padded, source)
    buffer = buffer.reshape(PACKS, EXPERTS, CAP, D).transpose(1, 0, 2, 3).reshape(EXPERTS, PACKS * CAP, D)
    width_slice = FF // N_HIDDEN
    summed = jnp.zeros((EXPERTS, PACKS * CAP, D), jnp.float32)
    for slice_idx in range(N_HIDDEN):
        col_start = slice_idx * width_slice
        slice_in = low_back(buffer)
        hidden_pre = jnp.einsum('erd,edf->erf', slice_in, up_weight[:, :, col_start:col_start + width_slice], precision=PRECISE)
        hidden_pre = low_back(hidden_pre)
        hidden_act = low(jax.nn.gelu(hidden_pre, approximate=True))
        slice_out = jnp.einsum('erf,edf->erd', hidden_act, down_weight[:, :, col_start:col_start + width_slice], precision=PRECISE)
        summed = summed + low(slice_out)
    returned = low_back(low(summed))
    returned = returned.reshape(EXPERTS, PACKS, CAP, D).transpose(1, 0, 2, 3).reshape(PACKS, EXPERTS * CAP, D)
    returned = jnp.concatenate([returned, jnp.zeros((PACKS, 1, D), jnp.float32)], 1)
    expert_rows = jax.vmap(take_rows)(returned, slot_index).reshape(TOKENS, TOP, D)
    mixture = lax.optimization_barrier(jnp.sum(gate_vals[:, :, None] * expert_rows, 1))
    return residual + mixture

def reference(tokens, doc_ids, pad_mask, norm1_gain, norm1_bias, qkv_weight, out_weight, norm2_gain, norm2_bias, router, routes, up_weight, down_weight, cotangent):
    params = tuple((item.astype(jnp.float32) for item in (norm1_gain, norm1_bias, qkv_weight, out_weight, norm2_gain, norm2_bias, router, up_weight, down_weight)))
    outputs = []
    input_grads = []
    totals = jax.tree.map(jnp.zeros_like, params)
    for micro_idx in range(MB):
        inputs = tokens[micro_idx].astype(jnp.float32)
        route_rows = routes[micro_idx]
        per_pack = route_rows.reshape(PACKS, ROWS, TOP)
        slot_index, source = jax.vmap(partial(slot_tables, experts=EXPERTS, capacity=CAP))(per_pack)
        forward = partial(block_forward, doc_rows=doc_ids[micro_idx], pad_rows=pad_mask[micro_idx].reshape(PACKS, ROWS), route_rows=route_rows, slot_index=slot_index, source=source)
        result, pullback = jax.vjp(forward, params, inputs)
        param_grads, input_grad = pullback(cotangent[micro_idx].astype(jnp.float32))
        totals = jax.tree.map(jnp.add, totals, param_grads)
        outputs.append(result)
        input_grads.append(input_grad)
    return (jnp.stack(outputs), jnp.stack(input_grads), totals[0], totals[1], totals[2], totals[3], totals[4], totals[5], totals[6], totals[7][TRAIN:], totals[8][TRAIN:])
```

```python
import jax
import jax.numpy as jnp
from jax import lax
from jax.sharding import PartitionSpec as P

HEAD_DIM = 64
EPSILON = 1e-05
PRECISE = lax.Precision.HIGHEST
MASKED = -1e30
EXTRA = 8
BF = jnp.bfloat16
F32 = jnp.float32


def round_up(value, step):
    return -(-value // step) * step


def swap(values, axis, bit):
    size = lax.axis_size(axis)
    return lax.ppermute(values, axis, [(i, i ^ bit) for i in range(size)])


def ordered(flag, mine, other):
    return jnp.where(
        flag == 0, jnp.concatenate([mine, other], 0), jnp.concatenate([other, mine], 0)
    )


def normalize(values):
    centre = values - jnp.mean(values, -1, keepdims=True)
    spread = jnp.mean(centre * centre, -1, keepdims=True)
    scale = lax.rsqrt(spread + EPSILON)
    return centre * scale, scale


def normalize_pull(normed, scale, gain, grad):
    wide = grad * gain
    return scale * (
        wide
        - jnp.mean(wide, -1, keepdims=True)
        - normed * jnp.mean(wide * normed, -1, keepdims=True)
    )


def gelu_pair(v):
    c0 = 0.7978845608028654
    inner = c0 * (v + 0.044715 * v * v * v)
    t = jnp.tanh(inner)
    act = 0.5 * v * (1.0 + t)
    slope = 0.5 * (1.0 + t) + 0.5 * v * (1.0 - t * t) * (c0 * (1.0 + 3 * 0.044715 * v * v))
    return act, slope


def visible(doc_row, pad_row):
    total_rows = doc_row.shape[0]
    query_pos = jnp.arange(total_rows)[:, None]
    key_pos = jnp.arange(total_rows)[None, :]
    same_doc = doc_row[:, None] == doc_row[None, :]
    is_real = (pad_row[None, :] == 1) | (query_pos == key_pos)
    return (key_pos <= query_pos) & same_doc & is_real


def masked_scores(queries, key_rows, allowed):
    scores = jnp.einsum("qhd,khd->hqk", queries, key_rows, preferred_element_type=F32)
    return jnp.where(allowed[None], scores * HEAD_DIM**-0.5, MASKED)


def attend_forward(queries, key_rows, value_rows, allowed):
    scores = masked_scores(queries, key_rows, allowed)
    row_peak = jnp.max(scores, -1, keepdims=True)
    exponent = jnp.exp(scores - row_peak)
    row_total = jnp.sum(exponent, -1, keepdims=True)
    weights = (exponent / row_total).astype(BF)
    output = jnp.einsum("hqk,khd->qhd", weights, value_rows, preferred_element_type=F32)
    return output, row_peak + jnp.log(row_total)


def attend_backward(queries, key_rows, value_rows, allowed, log_total, heads_grad):
    scale = HEAD_DIM**-0.5
    scores = masked_scores(queries, key_rows, allowed)
    weights = jnp.exp(scores - log_total)
    weight_grad = jnp.einsum("qhd,khd->hqk", heads_grad, value_rows, preferred_element_type=F32)
    row_delta = jnp.sum(weights * weight_grad, -1, keepdims=True)
    score_grad = (weights * (weight_grad - row_delta)).astype(BF)
    query_grad = scale * jnp.einsum("hqk,khd->qhd", score_grad, key_rows, preferred_element_type=F32)
    key_grad = scale * jnp.einsum("hqk,qhd->khd", score_grad, queries, preferred_element_type=F32)
    value_grad = jnp.einsum(
        "hqk,qhd->khd", weights.astype(BF), heads_grad, preferred_element_type=F32
    )
    return query_grad, key_grad, value_grad


def make_shards(ne, nh):
    def to_experts(blocks):
        return lax.all_to_all(blocks, "expert", split_axis=0, concat_axis=0, tiled=True)

    def reduce_quarters(rows):
        blocks = rows.reshape(nh, -1, rows.shape[-1])
        bit = 1
        while bit < nh:
            keep = [r for r in range(blocks.shape[0]) if r % 2 == 0]
            send = [r for r in range(blocks.shape[0]) if r % 2 == 1]
            got = swap(jnp.concatenate([blocks[r] for r in send], 0), "hidden", bit)
            blocks = (
                jnp.stack([blocks[r] for r in keep]).astype(F32)
                + got.reshape(len(keep), -1, rows.shape[-1]).astype(F32)
            ).astype(BF)
            bit *= 2
        return blocks[0]

    def gather_quarters(rows):
        bit = nh // 2
        while bit >= 1:
            rows = jnp.concatenate([rows, swap(rows, "hidden", bit)], 0)
            bit //= 2
        return rows

    def quarter_order():
        order = [0]
        bit = nh // 2
        while bit >= 1:
            order = order + [r ^ bit for r in order]
            bit //= 2
        return order

    def sum_hidden(rows):
        h = lax.axis_index("hidden")
        count = rows.shape[0] // 2
        flag = h % 2
        kept = lax.dynamic_slice_in_dim(rows, flag * count, count, 0)
        sent = lax.dynamic_slice_in_dim(rows, (1 - flag) * count, count, 0)
        kept = (kept.astype(F32) + swap(sent, "hidden", 1).astype(F32)).astype(BF)
        bit = 2
        while bit < nh:
            kept = (kept.astype(F32) + swap(kept, "hidden", bit).astype(F32)).astype(BF)
            bit *= 2
        return ordered(flag, kept, swap(kept, "hidden", 1))

    def shards(
        tokens,
        doc_ids,
        pad_mask,
        norm1_gain,
        norm1_bias,
        qkv_weight,
        out_weight,
        norm2_gain,
        norm2_bias,
        router,
        routes,
        up_weight,
        down_weight,
        cotangent,
    ):
        micro_count, row_count, width = tokens.shape
        expert_count = router.shape[1]
        top_count = routes.shape[2]
        pack_cap = 2 * row_count * top_count // expert_count
        quarter = row_count // nh
        cap = round_up((pack_cap + (nh - 1) * (expert_count - 1)) // nh, 8)
        local_heads = qkv_weight.shape[2] // HEAD_DIM
        e_idx = lax.axis_index("expert")
        h_idx = lax.axis_index("hidden")
        micros = range(micro_count)

        ups, downs = [up_weight[0]], [down_weight[0]]
        bit = nh // 2
        while bit >= 1:
            pair = jnp.stack(ups + downs)
            got = swap(pair, "hidden", bit)
            ups = ups + [got[i] for i in range(len(ups))]
            downs = downs + [got[len(downs) + i] for i in range(len(downs))]
            bit //= 2
        slice_order = quarter_order()
        ups = [ups[slice_order.index(r)] for r in range(nh)]
        downs = [downs[slice_order.index(r)] for r in range(nh)]
        up_all = jnp.concatenate(ups, 1)
        down_all = jnp.concatenate(downs, 1)

        perms, places, tables = [], [], []
        for m in micros:
            low = jnp.min(routes[m], -1)
            high = jnp.max(routes[m], -1)
            key = (low * expert_count + high) * row_count + jnp.arange(row_count, dtype=jnp.int32)
            rank = jnp.sum((key[:, None] < key[None, :]).astype(jnp.int32), 0)
            targets = jnp.concatenate(
                [jnp.arange(quarter, dtype=jnp.int32) * nh + (h_idx ^ r) for r in range(nh)]
            )
            perm = (targets[:, None] == rank[None, :]).astype(BF)
            perms.append(perm)
            mine = jnp.dot(perm[:quarter], routes[m].astype(BF), preferred_element_type=F32)
            first, second = mine[:, 0], mine[:, 1]
            names = jnp.arange(expert_count, dtype=F32)[:, None]
            member = (first[None, :] == names) | (second[None, :] == names)
            before = (
                jnp.arange(quarter)[:, None] < jnp.arange(quarter)[None, :]
            ).astype(BF)
            place = jnp.dot(member.astype(BF), before, preferred_element_type=F32)
            slot = jnp.arange(cap, dtype=F32)[None, :, None]
            table = (slot == place[:, None, :]) & member[:, None, :]
            tables.append(table.astype(BF))
            others = (first + second)[None, :] - names
            places.append((member, others))

        def dispatch(m, rows):
            return jnp.einsum("ejt,td->ejd", tables[m], rows, preferred_element_type=F32).astype(BF)

        upstream_mine, upstream_slots, other_slots = [], [], []
        for m in micros:
            up_rows = jnp.dot(perms[m][:quarter], cotangent[m], preferred_element_type=F32)
            upstream_mine.append(up_rows)
            other = jnp.sum(tables[m].astype(F32) * places[m][1][:, None, :], -1)
            other_row = jnp.pad(
                other[:, None, :], ((0, 0), (0, EXTRA - 1), (0, width - cap))
            ).astype(BF)
            sent = jnp.concatenate([dispatch(m, up_rows.astype(BF)), other_row], 1)
            got = to_experts(sent)
            upstream_slots.append(got[:, :cap].reshape(-1, width))
            other_slots.append(got[:, cap, :cap].astype(F32).reshape(-1, 1))

        state = []
        for m in micros:
            inputs = tokens[m].astype(F32)
            allowed = visible(doc_ids[m, 0], pad_mask[m])
            normed1, scale1 = normalize(inputs)
            attn_in = (normed1 * norm1_gain + norm1_bias).astype(BF)
            projected = jnp.einsum(
                "rd,cdf->crf", attn_in, qkv_weight, preferred_element_type=F32
            ).astype(BF)
            heads = projected.reshape(3, row_count, local_heads, HEAD_DIM)
            heads_out, log_total = attend_forward(heads[0], heads[1], heads[2], allowed)
            heads_low = heads_out.reshape(row_count, -1).astype(BF)
            heads_sorted = jnp.dot(perms[m], heads_low, preferred_element_type=F32).astype(BF)
            term = jnp.dot(heads_sorted, out_weight, preferred_element_type=F32).astype(BF)
            attention = reduce_quarters(term).astype(F32)
            inputs_mine = jnp.dot(perms[m][:quarter], tokens[m], preferred_element_type=F32)
            residual = inputs_mine + attention
            normed2, scale2 = normalize(residual)
            moe_in = (normed2 * norm2_gain + norm2_bias).astype(BF)
            logits = jnp.dot(moe_in, router, preferred_element_type=F32).T
            member = places[m][0]
            masked = jnp.where(member, logits, MASKED)
            raised = jnp.where(member, jnp.exp(masked - jnp.max(masked, 0, keepdims=True)), 0.0)
            gates = raised / jnp.sum(raised, 0, keepdims=True)
            received = to_experts(dispatch(m, moe_in)).reshape(-1, width)
            state.append(
                dict(
                    inputs=inputs,
                    allowed=allowed,
                    normed1=normed1,
                    scale1=scale1,
                    attn_in=attn_in,
                    heads=heads,
                    log_total=log_total,
                    heads_sorted=heads_sorted,
                    attention=attention,
                    normed2=normed2,
                    scale2=scale2,
                    moe_in=moe_in,
                    gates=gates,
                    received=received,
                )
            )

        ordinals = jnp.arange(expert_count, dtype=F32)[None, :]
        for m in micros:
            s = state[m]
            rows = s["received"]
            logits = jnp.dot(rows, router, preferred_element_type=F32)
            picks = (ordinals == e_idx.astype(F32)).astype(F32) - (
                ordinals == other_slots[m]
            ).astype(F32)
            gate = jax.nn.sigmoid(jnp.sum(logits * picks, -1, keepdims=True))
            grad_rows = (gate * upstream_slots[m].astype(F32)).astype(BF)
            hidden_pre = jnp.dot(rows, up_all, preferred_element_type=F32)
            act, slope = gelu_pair(hidden_pre)
            hidden_act = act.astype(BF)
            expert_out = jnp.einsum(
                "rf,df->rd", hidden_act, down_all, preferred_element_type=F32
            ).astype(BF)
            act_grad = jnp.dot(grad_rows, down_all, preferred_element_type=F32)
            pre_grad = (act_grad * slope).astype(BF)
            copies = jnp.einsum("rf,df->rd", pre_grad, up_all, preferred_element_type=F32).astype(BF)
            gate_grad = jnp.sum(upstream_slots[m].astype(F32) * expert_out.astype(F32), -1)
            gate_grad = gate_grad.reshape(expert_count, 1, cap)
            coarse = gate_grad.astype(BF)
            fine = (gate_grad - coarse.astype(F32)).astype(BF)
            extra = jnp.pad(
                jnp.concatenate([coarse, fine], 1), ((0, 0), (0, EXTRA - 2), (0, width - cap))
            )
            sent = jnp.concatenate([copies.reshape(expert_count, cap, width), extra], 1)
            s["copies_back"] = to_experts(sent)
            s["out_back"] = to_experts(expert_out.reshape(expert_count, cap, width))
            s["grad_rows"] = grad_rows
            s["hidden_act"] = hidden_act
            s["pre_grad"] = pre_grad

        grad_up = sum(
            jnp.einsum("rd,rf->df", s["received"], s["pre_grad"], preferred_element_type=F32)
            for s in state
        )
        grad_down = sum(
            jnp.einsum("rd,rf->df", s["grad_rows"], s["hidden_act"], preferred_element_type=F32)
            for s in state
        )
        part = jnp.concatenate([grad_up, grad_down], 0).astype(BF)
        part = part.reshape(2 * width, nh, -1).transpose(1, 0, 2).reshape(nh * 2 * width, -1)
        own = reduce_quarters(part)
        own = own.reshape(2, ne, width // ne, -1).transpose(1, 0, 2, 3)
        parts = to_experts(own)[ne // 2 :].astype(F32)

        grad_router = 0.0
        gain2_total, bias2_total = 0.0, 0.0
        for m in micros:
            s = state[m]
            back = s["copies_back"]
            table = tables[m]
            copies_sum = jnp.einsum("ejt,ejd->td", table, back[:, :cap], preferred_element_type=F32)
            slot_grad = back[:, cap, :cap].astype(F32) + back[:, cap + 1, :cap].astype(F32)
            gate_grad = jnp.sum(table.astype(F32) * slot_grad[:, :, None], 1)
            gates = s["gates"]
            logit_grad = gates * (gate_grad - jnp.sum(gates * gate_grad, 0, keepdims=True))
            normed2_grad = copies_sum + jnp.einsum(
                "et,de->td", logit_grad, router.astype(F32), precision=PRECISE
            )
            grad_router = grad_router + jnp.einsum(
                "et,td->ed", logit_grad, s["moe_in"].astype(F32), precision=PRECISE
            )
            gain2_total = gain2_total + jnp.sum(normed2_grad * s["normed2"], 0)
            bias2_total = bias2_total + jnp.sum(normed2_grad, 0)
            resid_grad = upstream_mine[m] + normalize_pull(
                s["normed2"], s["scale2"], norm2_gain, normed2_grad
            )
            s["resid_all"] = gather_quarters(resid_grad.astype(BF))
            weighted = (table.astype(F32) * gates[:, None, :]).astype(BF)
            mixture = jnp.einsum("ejt,ejd->td", weighted, s["out_back"], preferred_element_type=F32)
            s["delta_all"] = gather_quarters((s["attention"] + mixture).astype(BF))

        small = jnp.concatenate([gain2_total[None], bias2_total[None], grad_router], 0)
        small_rows = round_up(small.shape[0], 16)
        small = jnp.pad(small, ((0, small_rows - small.shape[0]), (0, 0))).astype(BF)

        order = quarter_order()
        grad_qkv, grad_proj = 0.0, 0.0
        gain1_total, bias1_total = 0.0, 0.0
        outputs, input_grads = [], []
        for m in micros:
            s = state[m]
            perm = perms[m].reshape(nh, quarter, row_count)
            perm_all = jnp.concatenate([perm[r] for r in order], 0)
            heads_sorted = s["heads_sorted"].reshape(nh, quarter, -1)
            heads_sorted = jnp.concatenate([heads_sorted[r] for r in order], 0)
            resid_all = s["resid_all"]
            grad_proj = grad_proj + jnp.einsum(
                "rf,rd->fd", heads_sorted, resid_all, preferred_element_type=F32
            )
            heads_grad = jnp.einsum(
                "rd,fd->rf", resid_all, out_weight, preferred_element_type=F32
            ).astype(BF)
            heads_grad = jnp.einsum(
                "rt,rf->tf", perm_all, heads_grad, preferred_element_type=F32
            ).astype(BF)
            heads = s["heads"]
            grads = attend_backward(
                heads[0],
                heads[1],
                heads[2],
                s["allowed"],
                s["log_total"],
                heads_grad.reshape(row_count, local_heads, HEAD_DIM),
            )
            qkv_grad = jnp.stack(grads).reshape(3, row_count, -1).astype(BF)
            grad_qkv = grad_qkv + jnp.einsum(
                "rd,crf->cdf", s["attn_in"], qkv_grad, preferred_element_type=F32
            )
            term = jnp.einsum(
                "crf,cdf->rd", qkv_grad, qkv_weight, preferred_element_type=F32
            ).astype(BF)
            if m == micro_count - 1:
                total = sum_hidden(jnp.concatenate([term, small], 0))
                small_sum = total[row_count:]
                normed1_grad = total[:row_count].astype(F32)
            else:
                normed1_grad = sum_hidden(term).astype(F32)
            gain1_total = gain1_total + jnp.sum(normed1_grad * s["normed1"], 0)
            bias1_total = bias1_total + jnp.sum(normed1_grad, 0)
            resid_grad = jnp.einsum("rt,rd->td", perm_all, resid_all, preferred_element_type=F32)
            input_grads.append(
                resid_grad + normalize_pull(s["normed1"], s["scale1"], norm1_gain, normed1_grad)
            )
            delta = jnp.einsum("rt,rd->td", perm_all, s["delta_all"], preferred_element_type=F32)
            outputs.append(s["inputs"] + delta)

        flat = jnp.concatenate([grad_qkv.reshape(-1), grad_proj.reshape(-1)]).astype(BF)
        flat = flat.reshape(ne, -1, width)
        share = jnp.sum(to_experts(flat).astype(F32), 0).astype(BF)
        share_rows = share.shape[0]
        extra = jnp.concatenate([gain1_total[None], bias1_total[None]], 0).astype(BF)
        extra = jnp.concatenate([extra, small_sum], 0)
        extra = jnp.pad(extra, ((0, round_up(extra.shape[0], 16) - extra.shape[0]), (0, 0)))
        gathered = jnp.concatenate([share, extra], 0)[None]
        bit = ne // 2
        while bit >= 1:
            gathered = jnp.concatenate([gathered, swap(gathered, "expert", bit)], 0)
            bit //= 2
        bits = []
        bit = ne // 2
        found = [0]
        while bit >= 1:
            found = found + [r ^ bit for r in found]
            bit //= 2
        sums = jnp.sum(gathered[:, share_rows:].astype(F32), 0)
        where = jnp.zeros((ne,), jnp.int32)
        slots = jnp.array([found.index(r) for r in range(ne)], jnp.int32)
        where = slots[jnp.arange(ne, dtype=jnp.int32) ^ e_idx]
        flat = gathered[:, :share_rows][where].astype(F32).reshape(-1)
        split = grad_qkv.size
        return (
            jnp.stack(outputs),
            jnp.stack(input_grads),
            sums[0],
            sums[1],
            flat[:split].reshape(grad_qkv.shape),
            flat[split:].reshape(grad_proj.shape),
            sums[2],
            sums[3],
            sums[4 : 4 + expert_count].T,
            parts[:, 0],
            parts[:, 1],
        )

    return shards


def solution(mesh):
    placed = (
        P(None, "expert", None),
        P(None, "expert", None),
        P(None, "expert"),
        P(),
        P(),
        P(None, None, "hidden"),
        P("hidden", None),
        P(),
        P(),
        P(),
        P(None, "expert", None),
        P("expert", None, "hidden"),
        P("expert", None, "hidden"),
        P(None, "expert", None),
    )
    return jax.shard_map(
        make_shards(mesh.shape["expert"], mesh.shape["hidden"]),
        mesh=mesh,
        in_specs=placed,
        out_specs=(
            P(None, "expert", None),
            P(None, "expert", None),
            P(),
            P(),
            P(None, None, "hidden"),
            P("hidden", None),
            P(),
            P(),
            P(),
            P(None, "expert", "hidden"),
            P(None, "expert", "hidden"),
        ),
        check_vma=False,
    )
```

```python
import jax
import jax.numpy as jnp
from jax import lax
from jax.experimental import pallas as pl
from jax.experimental.pallas import tpu as pltpu
from jax.sharding import PartitionSpec as P

HEAD_DIM = 64
EPSILON = 1e-05
PRECISE = lax.Precision.HIGHEST
MASKED = -1e30
TILE = 16
BF = jnp.bfloat16
F32 = jnp.float32


def round_up(value, step):
    return -(-value // step) * step


def swap(values, axis, bit):
    size = lax.axis_size(axis)
    return lax.ppermute(values, axis, [(i, i ^ bit) for i in range(size)])


def ordered(flag, mine, other):
    return jnp.where(
        flag == 0, jnp.concatenate([mine, other], 0), jnp.concatenate([other, mine], 0)
    )


def normalize(values):
    centre = values - jnp.mean(values, -1, keepdims=True)
    spread = jnp.mean(centre * centre, -1, keepdims=True)
    scale = lax.rsqrt(spread + EPSILON)
    return centre * scale, scale


def normalize_pull(normed, scale, gain, grad):
    wide = grad * gain
    return scale * (
        wide
        - jnp.mean(wide, -1, keepdims=True)
        - normed * jnp.mean(wide * normed, -1, keepdims=True)
    )


def gelu_pair(v):
    c0 = 0.7978845608028654
    inner = c0 * (v + 0.044715 * v * v * v)
    t = jnp.tanh(inner)
    act = 0.5 * v * (1.0 + t)
    slope = 0.5 * (1.0 + t) + 0.5 * v * (1.0 - t * t) * (c0 * (1.0 + 3 * 0.044715 * v * v))
    return act, slope


def after(values, *others):
    return lax.optimization_barrier((values, others))[0]


def diagonal(count):
    return lax.broadcasted_iota(jnp.int32, (count, count), 0) == lax.broadcasted_iota(
        jnp.int32, (count, count), 1
    )


def expert_body(slices, packs, cap, width, aliased):
    rows_n = packs * cap

    def body(own_ref, rows_ref, cot_ref, router_ref, *refs):
        ups, downs = refs[:slices], refs[slices : 2 * slices]
        refs = refs[2 * slices + (4 if aliased else 0) :]
        (out_ref, copies_ref, rows_all, grads_all, act_all, pre_all) = refs[:6]
        up_v, down_v, grad_rows, acc_out, acc_copies, sems = refs[6:]
        i, s = pl.program_id(0), pl.program_id(1)

        def fetch(r):
            return (
                pltpu.make_async_copy(ups[r], up_v.at[r], sems.at[0, r]),
                pltpu.make_async_copy(downs[r], down_v.at[r], sems.at[1, r]),
            )

        @pl.when((i == 0) & (s == 0))
        def _():
            for r in range(slices):
                for copy in fetch(r):
                    copy.start()

        for r in range(slices):

            @pl.when((i == 0) & (s == r))
            def _():
                for copy in fetch(r):
                    copy.wait()

        @pl.when(s == 0)
        def _():
            rows = rows_ref[...].reshape(rows_n, width)
            rows_all[...] = rows
            logits = jnp.dot(rows, router_ref[...], preferred_element_type=F32)
            ordinals = lax.broadcasted_iota(jnp.int32, logits.shape, 1).astype(F32)
            eye = diagonal(cap)
            other = []
            for p in range(packs):
                line = cot_ref[p, cap - TILE :, :][TILE - 1 :, :cap].astype(F32)
                other.append(jnp.sum(jnp.where(eye, line, 0.0), 1, keepdims=True))
            other = jnp.concatenate(other, 0)
            own = own_ref[0].astype(F32)
            picks = jnp.where(ordinals == own, 1.0, 0.0) - jnp.where(ordinals == other, 1.0, 0.0)
            gate = jax.nn.sigmoid(jnp.sum(logits * picks, -1, keepdims=True))
            cot = cot_ref[...].reshape(rows_n, width).astype(F32)
            low = (gate * cot).astype(BF)
            grad_rows[...] = low
            grads_all[...] = low

        up, down = up_v[s], down_v[s]
        pre = jnp.dot(rows_ref[...].reshape(rows_n, width), up, preferred_element_type=F32)
        act_grad = jnp.dot(grad_rows[...], down, preferred_element_type=F32)
        act, slope = gelu_pair(pre)
        act = act.astype(BF)
        act_all[...] = act
        pre_grad = (act_grad * slope).astype(BF)
        pre_all[...] = pre_grad
        along = (((1,), (1,)), ((), ()))
        out = lax.dot_general(act, down, along, preferred_element_type=F32)
        copies = lax.dot_general(pre_grad, up, along, preferred_element_type=F32)

        @pl.when(s == 0)
        def _():
            acc_out[...] = out
            acc_copies[...] = copies

        @pl.when(s > 0)
        def _():
            acc_out[...] += out
            acc_copies[...] += copies

        @pl.when(s == slices - 1)
        def _():
            low = acc_out[...].astype(BF)
            out_ref[...] = low.reshape(packs, cap, width)
            copies_ref[...] = acc_copies[...].astype(BF).reshape(packs, cap, width)
            cot = cot_ref[...].reshape(rows_n, width).astype(F32)
            gate_grad = jnp.sum(cot * low.astype(F32), -1, keepdims=True)
            eye = diagonal(cap)
            index = lax.broadcasted_iota(jnp.int32, (TILE, width), 0)
            for p in range(packs):
                column = gate_grad[p * cap : (p + 1) * cap]
                line = jnp.sum(jnp.where(eye, column, 0.0), 0, keepdims=True)
                line = jnp.concatenate([line, jnp.zeros((1, width - cap), F32)], 1)
                coarse = line.astype(BF).astype(F32)
                tail = copies_ref[p, cap - TILE :, :].astype(F32)
                tail = jnp.where(index == TILE - 1, coarse, tail)
                tail = jnp.where(index == TILE - 2, line - coarse, tail)
                copies_ref[p, cap - TILE :, :] = tail.astype(BF)

    return body


def run_expert(own, rows, cot, router, ups, downs, held, m, micro_count):
    blocks, cap, width = rows.shape
    slices = len(ups)
    hidden = ups[0].shape[1]
    packs = max(p for p in range(1, blocks + 1) if blocks % p == 0 and p * cap <= 448)
    steps = blocks // packs
    total = micro_count * blocks * cap
    aliased = held is not None
    rows_n = packs * cap
    block = pl.BlockSpec((packs, cap, width), lambda i, s: (i, 0, 0))
    any_spec = pl.BlockSpec(memory_space=pl.ANY)
    whole_rows = pl.BlockSpec((rows_n, width), lambda i, s: (m * steps + i, 0))
    whole_hidden = pl.BlockSpec((rows_n, hidden), lambda i, s: (m * steps + i, s))
    inputs = [own, rows, cot, router, *ups, *downs]
    in_specs = [
        pl.BlockSpec(memory_space=pltpu.SMEM),
        block,
        block,
        pl.BlockSpec(router.shape, lambda i, s: (0, 0)),
    ] + [any_spec] * (2 * slices)
    aliases = {}
    if aliased:
        aliases = {len(inputs) + k: 2 + k for k in range(4)}
        inputs += list(held)
        in_specs += [any_spec] * 4
    return pl.pallas_call(
        expert_body(slices, packs, cap, width, aliased),
        grid=(steps, slices),
        in_specs=in_specs,
        out_specs=[block, block, whole_rows, whole_rows, whole_hidden, whole_hidden],
        out_shape=[
            jax.ShapeDtypeStruct((blocks, cap, width), BF),
            jax.ShapeDtypeStruct((blocks, cap, width), BF),
            jax.ShapeDtypeStruct((total, width), BF),
            jax.ShapeDtypeStruct((total, width), BF),
            jax.ShapeDtypeStruct((total, slices * hidden), BF),
            jax.ShapeDtypeStruct((total, slices * hidden), BF),
        ],
        scratch_shapes=[
            pltpu.VMEM((slices,) + ups[0].shape, BF),
            pltpu.VMEM((slices,) + downs[0].shape, BF),
            pltpu.VMEM((rows_n, width), BF),
            pltpu.VMEM((rows_n, width), F32),
            pltpu.VMEM((rows_n, width), F32),
            pltpu.SemaphoreType.DMA((2, slices)),
        ],
        input_output_aliases=aliases,
        compiler_params=pltpu.CompilerParams(vmem_limit_bytes=48 * 1024 * 1024),
        name="expert",
    )(*inputs)


def visible(doc_row, pad_row):
    total_rows = doc_row.shape[0]
    query_pos = jnp.arange(total_rows)[:, None]
    key_pos = jnp.arange(total_rows)[None, :]
    same_doc = doc_row[:, None] == doc_row[None, :]
    is_real = (pad_row[None, :] == 1) | (query_pos == key_pos)
    return (key_pos <= query_pos) & same_doc & is_real


def masked_scores(queries, key_rows, allowed):
    scores = jnp.einsum("qhd,khd->hqk", queries, key_rows, preferred_element_type=F32)
    return jnp.where(allowed[None], scores * HEAD_DIM**-0.5, MASKED)


def attend_forward(queries, key_rows, value_rows, allowed):
    scores = masked_scores(queries, key_rows, allowed)
    row_peak = jnp.max(scores, -1, keepdims=True)
    exponent = jnp.exp(scores - row_peak)
    row_total = jnp.sum(exponent, -1, keepdims=True)
    weights = (exponent / row_total).astype(BF)
    output = jnp.einsum("hqk,khd->qhd", weights, value_rows, preferred_element_type=F32)
    return output, row_peak + jnp.log(row_total)


def attend_backward(queries, key_rows, value_rows, allowed, log_total, heads_grad):
    scale = HEAD_DIM**-0.5
    scores = masked_scores(queries, key_rows, allowed)
    weights = jnp.exp(scores - log_total)
    weight_grad = jnp.einsum("qhd,khd->hqk", heads_grad, value_rows, preferred_element_type=F32)
    row_delta = jnp.sum(weights * weight_grad, -1, keepdims=True)
    score_grad = (weights * (weight_grad - row_delta)).astype(BF)
    query_grad = scale * jnp.einsum("hqk,khd->qhd", score_grad, key_rows, preferred_element_type=F32)
    key_grad = scale * jnp.einsum("hqk,qhd->khd", score_grad, queries, preferred_element_type=F32)
    value_grad = jnp.einsum(
        "hqk,qhd->khd", weights.astype(BF), heads_grad, preferred_element_type=F32
    )
    return query_grad, key_grad, value_grad


def make_shards(ne, nh):
    def to_experts(blocks):
        return lax.all_to_all(blocks, "expert", split_axis=0, concat_axis=0, tiled=True)

    def reduce_quarters(rows):
        blocks = rows.reshape(nh, -1, rows.shape[-1])
        bit = 1
        while bit < nh:
            keep = [r for r in range(blocks.shape[0]) if r % 2 == 0]
            send = [r for r in range(blocks.shape[0]) if r % 2 == 1]
            got = swap(jnp.concatenate([blocks[r] for r in send], 0), "hidden", bit)
            blocks = (
                jnp.stack([blocks[r] for r in keep]).astype(F32)
                + got.reshape(len(keep), -1, rows.shape[-1]).astype(F32)
            ).astype(BF)
            bit *= 2
        return blocks[0]

    def gather_quarters(rows):
        bit = nh // 2
        while bit >= 1:
            rows = jnp.concatenate([rows, swap(rows, "hidden", bit)], 0)
            bit //= 2
        return rows

    def quarter_order():
        order = [0]
        bit = nh // 2
        while bit >= 1:
            order = order + [r ^ bit for r in order]
            bit //= 2
        return order

    def sum_hidden(rows):
        h = lax.axis_index("hidden")
        count = rows.shape[0] // 2
        flag = h % 2
        kept = lax.dynamic_slice_in_dim(rows, flag * count, count, 0)
        sent = lax.dynamic_slice_in_dim(rows, (1 - flag) * count, count, 0)
        kept = (kept.astype(F32) + swap(sent, "hidden", 1).astype(F32)).astype(BF)
        bit = 2
        while bit < nh:
            kept = (kept.astype(F32) + swap(kept, "hidden", bit).astype(F32)).astype(BF)
            bit *= 2
        return ordered(flag, kept, swap(kept, "hidden", 1))

    def shards(
        tokens,
        doc_ids,
        pad_mask,
        norm1_gain,
        norm1_bias,
        qkv_weight,
        out_weight,
        norm2_gain,
        norm2_bias,
        router,
        routes,
        up_weight,
        down_weight,
        cotangent,
    ):
        micro_count, row_count, width = tokens.shape
        expert_count = router.shape[1]
        top_count = routes.shape[2]
        pack_cap = 2 * row_count * top_count // expert_count
        quarter = row_count // nh
        cap = round_up((pack_cap + (nh - 1) * (expert_count - 1)) // nh + 2, TILE)
        local_heads = qkv_weight.shape[2] // HEAD_DIM
        e_idx = lax.axis_index("expert")
        h_idx = lax.axis_index("hidden")
        micros = range(micro_count)

        slice_order = quarter_order()
        ups, downs = [up_weight[0]], [down_weight[0]]
        bit = nh // 2
        while bit >= 1:
            got_up = [swap(x, "hidden", bit) for x in ups]
            got_down = [swap(x, "hidden", bit) for x in downs]
            ups, downs = ups + got_up, downs + got_down
            bit //= 2
        ups = [ups[slice_order.index(r)] for r in range(nh)]
        downs = [downs[slice_order.index(r)] for r in range(nh)]

        perms, places, tables = [], [], []
        for m in micros:
            low = jnp.min(routes[m], -1)
            high = jnp.max(routes[m], -1)
            key = (low * expert_count + high) * row_count + jnp.arange(row_count, dtype=jnp.int32)
            rank = jnp.sum((key[:, None] < key[None, :]).astype(jnp.int32), 0)
            targets = jnp.concatenate(
                [jnp.arange(quarter, dtype=jnp.int32) * nh + (h_idx ^ r) for r in range(nh)]
            )
            perm = (targets[:, None] == rank[None, :]).astype(BF)
            perms.append(perm)
            mine = jnp.dot(perm[:quarter], routes[m].astype(BF), preferred_element_type=F32)
            first, second = mine[:, 0], mine[:, 1]
            names = jnp.arange(expert_count, dtype=F32)[:, None]
            member = (first[None, :] == names) | (second[None, :] == names)
            before = (
                jnp.arange(quarter)[:, None] < jnp.arange(quarter)[None, :]
            ).astype(BF)
            place = jnp.dot(member.astype(BF), before, preferred_element_type=F32)
            slot = jnp.arange(cap, dtype=F32)[None, :, None]
            table = (slot == place[:, None, :]) & member[:, None, :]
            tables.append(table.astype(BF))
            others = (first + second)[None, :] - names
            places.append((member, others))

        def dispatch(m, rows):
            return jnp.einsum("ejt,td->ejd", tables[m], rows, preferred_element_type=F32).astype(BF)

        upstream_mine, upstream_slots = [], []
        for m in micros:
            up_rows = jnp.dot(perms[m][:quarter], cotangent[m], preferred_element_type=F32)
            upstream_mine.append(up_rows)
            other = jnp.sum(tables[m].astype(F32) * places[m][1][:, None, :], -1)
            other = jnp.pad(other[:, None, :], ((0, 0), (0, 0), (0, width - cap)))
            sent = jnp.einsum(
                "ejt,td->ejd", tables[m], up_rows.astype(BF), preferred_element_type=F32
            )
            last = (jnp.arange(cap) == cap - 1)[None, :, None]
            upstream_slots.append(to_experts(jnp.where(last, other, sent).astype(BF)))

        state = []
        for m in micros:
            inputs = tokens[m].astype(F32)
            allowed = visible(doc_ids[m, 0], pad_mask[m])
            normed1, scale1 = normalize(inputs)
            attn_in = (normed1 * norm1_gain + norm1_bias).astype(BF)
            projected = jnp.einsum(
                "rd,cdf->crf", attn_in, qkv_weight, preferred_element_type=F32
            ).astype(BF)
            heads = projected.reshape(3, row_count, local_heads, HEAD_DIM)
            heads_out, log_total = attend_forward(heads[0], heads[1], heads[2], allowed)
            heads_low = heads_out.reshape(row_count, -1).astype(BF)
            heads_sorted = jnp.dot(perms[m], heads_low, preferred_element_type=F32).astype(BF)
            term = jnp.dot(heads_sorted, out_weight, preferred_element_type=F32).astype(BF)
            attention = reduce_quarters(term).astype(F32)
            inputs_mine = jnp.dot(perms[m][:quarter], tokens[m], preferred_element_type=F32)
            residual = inputs_mine + attention
            normed2, scale2 = normalize(residual)
            moe_in = (normed2 * norm2_gain + norm2_bias).astype(BF)
            logits = jnp.dot(moe_in, router, preferred_element_type=F32).T
            member = places[m][0]
            masked = jnp.where(member, logits, MASKED)
            raised = jnp.where(member, jnp.exp(masked - jnp.max(masked, 0, keepdims=True)), 0.0)
            gates = raised / jnp.sum(raised, 0, keepdims=True)
            received = to_experts(dispatch(m, moe_in))
            state.append(
                dict(
                    inputs=inputs,
                    allowed=allowed,
                    normed1=normed1,
                    scale1=scale1,
                    attn_in=attn_in,
                    heads=heads,
                    log_total=log_total,
                    heads_sorted=heads_sorted,
                    attention=attention,
                    normed2=normed2,
                    scale2=scale2,
                    moe_in=moe_in,
                    gates=gates,
                    received=received,
                )
            )

        own_expert = jnp.full((1,), e_idx, jnp.int32)
        held = None
        for m in micros:
            s = state[m]
            out, copies, *held = run_expert(
                own_expert,
                s["received"],
                upstream_slots[m],
                router,
                ups,
                downs,
                held,
                m,
                micro_count,
            )
            s["copies_back"] = to_experts(copies)
            s["out_back"] = to_experts(out)

        rows_all, grads_all, act_all, pre_all = held
        parts = []
        for left, right in ((rows_all, pre_all), (grads_all, act_all)):
            hidden = right.shape[1] // nh
            slabs = [
                jnp.einsum(
                    "rd,rf->df",
                    left,
                    right[:, r * hidden : (r + 1) * hidden],
                    preferred_element_type=F32,
                ).astype(BF)
                for r in range(nh)
            ]
            bit = 1
            while bit < nh:
                got = [swap(slab, "hidden", bit) for slab in slabs[1::2]]
                slabs = [
                    (mine.astype(F32) + other.astype(F32)).astype(BF)
                    for mine, other in zip(slabs[0::2], got)
                ]
                bit *= 2
            rows = to_experts(slabs[0].reshape(ne, width // ne, -1))
            parts.append(rows[ne // 2 :].astype(F32))

        grad_router = 0.0
        gain2_total, bias2_total = 0.0, 0.0
        for m in micros:
            s = state[m]
            back = s["copies_back"]
            table = tables[m]
            copies_sum = jnp.einsum("ejt,ejd->td", table, back, preferred_element_type=F32)
            slot_grad = back[:, cap - 1, :cap].astype(F32) + back[:, cap - 2, :cap].astype(F32)
            gate_grad = jnp.sum(table.astype(F32) * slot_grad[:, :, None], 1)
            gates = s["gates"]
            logit_grad = gates * (gate_grad - jnp.sum(gates * gate_grad, 0, keepdims=True))
            normed2_grad = copies_sum + jnp.einsum(
                "et,de->td", logit_grad, router.astype(F32), precision=PRECISE
            )
            grad_router = grad_router + jnp.einsum(
                "et,td->ed", logit_grad, s["moe_in"].astype(F32), precision=PRECISE
            )
            gain2_total = gain2_total + jnp.sum(normed2_grad * s["normed2"], 0)
            bias2_total = bias2_total + jnp.sum(normed2_grad, 0)
            resid_grad = upstream_mine[m] + normalize_pull(
                s["normed2"], s["scale2"], norm2_gain, normed2_grad
            )
            s["resid_all"] = gather_quarters(resid_grad.astype(BF))
            weighted = (table.astype(F32) * gates[:, None, :]).astype(BF)
            mixture = jnp.einsum("ejt,ejd->td", weighted, s["out_back"], preferred_element_type=F32)
            s["delta_all"] = gather_quarters((s["attention"] + mixture).astype(BF))

        small = jnp.concatenate([gain2_total[None], bias2_total[None], grad_router], 0)
        small_rows = round_up(small.shape[0], 16)
        small = jnp.pad(small, ((0, small_rows - small.shape[0]), (0, 0))).astype(BF)

        order = quarter_order()
        grad_qkv, grad_proj = 0.0, 0.0
        gain1_total, bias1_total = 0.0, 0.0
        outputs, input_grads = [], []
        for m in micros:
            s = state[m]
            perm = perms[m].reshape(nh, quarter, row_count)
            perm_all = jnp.concatenate([perm[r] for r in order], 0)
            heads_sorted = s["heads_sorted"].reshape(nh, quarter, -1)
            heads_sorted = jnp.concatenate([heads_sorted[r] for r in order], 0)
            resid_all = s["resid_all"]
            grad_proj = grad_proj + jnp.einsum(
                "rf,rd->fd", heads_sorted, resid_all, preferred_element_type=F32
            )
            heads_grad = jnp.einsum(
                "rd,fd->rf", resid_all, out_weight, preferred_element_type=F32
            ).astype(BF)
            heads_grad = jnp.einsum(
                "rt,rf->tf", perm_all, heads_grad, preferred_element_type=F32
            ).astype(BF)
            heads = s["heads"]
            grads = attend_backward(
                heads[0],
                heads[1],
                heads[2],
                s["allowed"],
                s["log_total"],
                heads_grad.reshape(row_count, local_heads, HEAD_DIM),
            )
            qkv_grad = jnp.stack(grads).reshape(3, row_count, -1).astype(BF)
            grad_qkv = grad_qkv + jnp.einsum(
                "rd,crf->cdf", s["attn_in"], qkv_grad, preferred_element_type=F32
            )
            term = jnp.einsum(
                "crf,cdf->rd", qkv_grad, qkv_weight, preferred_element_type=F32
            ).astype(BF)
            if m == micro_count - 1:
                total = sum_hidden(jnp.concatenate([term, small], 0))
                small_sum = total[row_count:]
                normed1_grad = total[:row_count].astype(F32)
            else:
                normed1_grad = sum_hidden(term).astype(F32)
            gain1_total = gain1_total + jnp.sum(normed1_grad * s["normed1"], 0)
            bias1_total = bias1_total + jnp.sum(normed1_grad, 0)
            resid_grad = jnp.einsum("rt,rd->td", perm_all, resid_all, preferred_element_type=F32)
            input_grads.append(
                resid_grad + normalize_pull(s["normed1"], s["scale1"], norm1_gain, normed1_grad)
            )
            delta = jnp.einsum("rt,rd->td", perm_all, s["delta_all"], preferred_element_type=F32)
            outputs.append(s["inputs"] + delta)

        flat = jnp.concatenate([grad_qkv.reshape(-1), grad_proj.reshape(-1)]).astype(BF)
        share = flat.reshape(ne, -1, width)
        bit = 1
        while bit < ne:
            flag = (e_idx // bit) % 2
            pairs = share.reshape(share.shape[0] // 2, 2, -1, width)
            kept = lax.dynamic_index_in_dim(pairs, flag, 1, False)
            sent = lax.dynamic_index_in_dim(pairs, 1 - flag, 1, False)
            share = (kept.astype(F32) + swap(sent, "expert", bit).astype(F32)).astype(BF)
            bit *= 2
        share = share[0]
        share_rows = share.shape[0]
        extra = jnp.concatenate([gain1_total[None], bias1_total[None]], 0).astype(BF)
        extra = jnp.concatenate([extra, small_sum], 0)
        extra = jnp.pad(extra, ((0, round_up(extra.shape[0], 16) - extra.shape[0]), (0, 0)))
        gathered = jnp.concatenate([share, extra], 0)[None]
        bit = ne // 2
        while bit >= 1:
            gathered = jnp.concatenate([gathered, swap(gathered, "expert", bit)], 0)
            bit //= 2
        bits = []
        bit = ne // 2
        found = [0]
        while bit >= 1:
            found = found + [r ^ bit for r in found]
            bit //= 2
        sums = jnp.sum(gathered[:, share_rows:].astype(F32), 0)
        where = jnp.zeros((ne,), jnp.int32)
        slots = jnp.array([found.index(r) for r in range(ne)], jnp.int32)
        where = slots[jnp.arange(ne, dtype=jnp.int32) ^ e_idx]
        flat = gathered[:, :share_rows][where].astype(F32).reshape(-1)
        split = grad_qkv.size
        return (
            jnp.stack(outputs),
            jnp.stack(input_grads),
            sums[0],
            sums[1],
            flat[:split].reshape(grad_qkv.shape),
            flat[split:].reshape(grad_proj.shape),
            sums[2],
            sums[3],
            sums[4 : 4 + expert_count].T,
            parts[0],
            parts[1],
        )

    return shards


def solution(mesh):
    placed = (
        P(None, "expert", None),
        P(None, "expert", None),
        P(None, "expert"),
        P(),
        P(),
        P(None, None, "hidden"),
        P("hidden", None),
        P(),
        P(),
        P(),
        P(None, "expert", None),
        P("expert", None, "hidden"),
        P("expert", None, "hidden"),
        P(None, "expert", None),
    )
    return jax.shard_map(
        make_shards(mesh.shape["expert"], mesh.shape["hidden"]),
        mesh=mesh,
        in_specs=placed,
        out_specs=(
            P(None, "expert", None),
            P(None, "expert", None),
            P(),
            P(),
            P(None, None, "hidden"),
            P("hidden", None),
            P(),
            P(),
            P(),
            P(None, "expert", "hidden"),
            P(None, "expert", "hidden"),
        ),
        check_vma=False,
    )
```

```python
import jax
import jax.numpy as jnp
from jax import lax
from jax.experimental import pallas as pl
from jax.experimental.pallas import tpu as pltpu
from jax.sharding import PartitionSpec as P

HEAD_DIM = 64
EPSILON = 1e-05
PRECISE = lax.Precision.HIGHEST
MASKED = -1e30
TILE = 16
BF = jnp.bfloat16
F32 = jnp.float32


def round_up(value, step):
    return -(-value // step) * step


def swap(values, axis, bit):
    size = lax.axis_size(axis)
    return lax.ppermute(values, axis, [(i, i ^ bit) for i in range(size)])


def ordered(flag, mine, other):
    return jnp.where(
        flag == 0, jnp.concatenate([mine, other], 0), jnp.concatenate([other, mine], 0)
    )


def normalize(values):
    centre = values - jnp.mean(values, -1, keepdims=True)
    spread = jnp.mean(centre * centre, -1, keepdims=True)
    scale = lax.rsqrt(spread + EPSILON)
    return centre * scale, scale


def normalize_pull(normed, scale, gain, grad):
    wide = grad * gain
    return scale * (
        wide
        - jnp.mean(wide, -1, keepdims=True)
        - normed * jnp.mean(wide * normed, -1, keepdims=True)
    )


def gelu_pair(v):
    c0 = 0.7978845608028654
    inner = c0 * (v + 0.044715 * v * v * v)
    t = jnp.tanh(inner)
    act = 0.5 * v * (1.0 + t)
    slope = 0.5 * (1.0 + t) + 0.5 * v * (1.0 - t * t) * (c0 * (1.0 + 3 * 0.044715 * v * v))
    return act, slope


def after(values, *others):
    return lax.optimization_barrier((values, others))[0]


def diagonal(count):
    return lax.broadcasted_iota(jnp.int32, (count, count), 0) == lax.broadcasted_iota(
        jnp.int32, (count, count), 1
    )


def expert_body(slices, packs, cap, width, aliased):
    rows_n = packs * cap

    def body(own_ref, rows_ref, cot_ref, router_ref, *refs):
        ups, downs = refs[:slices], refs[slices : 2 * slices]
        refs = refs[2 * slices + (4 if aliased else 0) :]
        (out_ref, copies_ref, rows_all, grads_all, act_all, pre_all) = refs[:6]
        up_v, down_v, grad_rows, acc_out, acc_copies, sems = refs[6:]
        i, s = pl.program_id(0), pl.program_id(1)

        def fetch(r):
            return (
                pltpu.make_async_copy(ups[r], up_v.at[r], sems.at[0, r]),
                pltpu.make_async_copy(downs[r], down_v.at[r], sems.at[1, r]),
            )

        @pl.when((i == 0) & (s == 0))
        def _():
            for r in range(slices):
                for copy in fetch(r):
                    copy.start()

        for r in range(slices):

            @pl.when((i == 0) & (s == r))
            def _():
                for copy in fetch(r):
                    copy.wait()

        @pl.when(s == 0)
        def _():
            rows = rows_ref[...].reshape(rows_n, width)
            rows_all[...] = rows
            logits = jnp.dot(rows, router_ref[...], preferred_element_type=F32)
            ordinals = lax.broadcasted_iota(jnp.int32, logits.shape, 1).astype(F32)
            eye = diagonal(cap)
            other = []
            for p in range(packs):
                line = cot_ref[p, cap - TILE :, :][TILE - 1 :, :cap].astype(F32)
                other.append(jnp.sum(jnp.where(eye, line, 0.0), 1, keepdims=True))
            other = jnp.concatenate(other, 0)
            own = own_ref[0].astype(F32)
            picks = jnp.where(ordinals == own, 1.0, 0.0) - jnp.where(ordinals == other, 1.0, 0.0)
            gate = jax.nn.sigmoid(jnp.sum(logits * picks, -1, keepdims=True))
            cot = cot_ref[...].reshape(rows_n, width).astype(F32)
            low = (gate * cot).astype(BF)
            grad_rows[...] = low
            grads_all[...] = low

        up, down = up_v[s], down_v[s]
        pre = jnp.dot(rows_ref[...].reshape(rows_n, width), up, preferred_element_type=F32)
        act_grad = jnp.dot(grad_rows[...], down, preferred_element_type=F32)
        act, slope = gelu_pair(pre)
        act = act.astype(BF)
        act_all[...] = act
        pre_grad = (act_grad * slope).astype(BF)
        pre_all[...] = pre_grad
        along = (((1,), (1,)), ((), ()))
        out = lax.dot_general(act, down, along, preferred_element_type=F32)
        copies = lax.dot_general(pre_grad, up, along, preferred_element_type=F32)

        @pl.when(s == 0)
        def _():
            acc_out[...] = out
            acc_copies[...] = copies

        @pl.when(s > 0)
        def _():
            acc_out[...] += out
            acc_copies[...] += copies

        @pl.when(s == slices - 1)
        def _():
            low = acc_out[...].astype(BF)
            out_ref[...] = low.reshape(packs, cap, width)
            copies_ref[...] = acc_copies[...].astype(BF).reshape(packs, cap, width)
            cot = cot_ref[...].reshape(rows_n, width).astype(F32)
            gate_grad = jnp.sum(cot * low.astype(F32), -1, keepdims=True)
            eye = diagonal(cap)
            index = lax.broadcasted_iota(jnp.int32, (TILE, width), 0)
            for p in range(packs):
                column = gate_grad[p * cap : (p + 1) * cap]
                line = jnp.sum(jnp.where(eye, column, 0.0), 0, keepdims=True)
                line = jnp.concatenate([line, jnp.zeros((1, width - cap), F32)], 1)
                coarse = line.astype(BF).astype(F32)
                tail = copies_ref[p, cap - TILE :, :].astype(F32)
                tail = jnp.where(index == TILE - 1, coarse, tail)
                tail = jnp.where(index == TILE - 2, line - coarse, tail)
                copies_ref[p, cap - TILE :, :] = tail.astype(BF)

    return body


def run_expert(own, rows, cot, router, ups, downs, held, m, micro_count):
    blocks, cap, width = rows.shape
    slices = len(ups)
    hidden = ups[0].shape[1]
    packs = max(p for p in range(1, blocks + 1) if blocks % p == 0 and p * cap <= 448)
    steps = blocks // packs
    total = micro_count * blocks * cap
    aliased = held is not None
    rows_n = packs * cap
    block = pl.BlockSpec((packs, cap, width), lambda i, s: (i, 0, 0))
    any_spec = pl.BlockSpec(memory_space=pl.ANY)
    whole_rows = pl.BlockSpec((rows_n, width), lambda i, s: (m * steps + i, 0))
    whole_hidden = pl.BlockSpec((rows_n, hidden), lambda i, s: (m * steps + i, s))
    inputs = [own, rows, cot, router, *ups, *downs]
    in_specs = [
        pl.BlockSpec(memory_space=pltpu.SMEM),
        block,
        block,
        pl.BlockSpec(router.shape, lambda i, s: (0, 0)),
    ] + [any_spec] * (2 * slices)
    aliases = {}
    if aliased:
        aliases = {len(inputs) + k: 2 + k for k in range(4)}
        inputs += list(held)
        in_specs += [any_spec] * 4
    return pl.pallas_call(
        expert_body(slices, packs, cap, width, aliased),
        grid=(steps, slices),
        in_specs=in_specs,
        out_specs=[block, block, whole_rows, whole_rows, whole_hidden, whole_hidden],
        out_shape=[
            jax.ShapeDtypeStruct((blocks, cap, width), BF),
            jax.ShapeDtypeStruct((blocks, cap, width), BF),
            jax.ShapeDtypeStruct((total, width), BF),
            jax.ShapeDtypeStruct((total, width), BF),
            jax.ShapeDtypeStruct((total, slices * hidden), BF),
            jax.ShapeDtypeStruct((total, slices * hidden), BF),
        ],
        scratch_shapes=[
            pltpu.VMEM((slices,) + ups[0].shape, BF),
            pltpu.VMEM((slices,) + downs[0].shape, BF),
            pltpu.VMEM((rows_n, width), BF),
            pltpu.VMEM((rows_n, width), F32),
            pltpu.VMEM((rows_n, width), F32),
            pltpu.SemaphoreType.DMA((2, slices)),
        ],
        input_output_aliases=aliases,
        compiler_params=pltpu.CompilerParams(vmem_limit_bytes=48 * 1024 * 1024),
        name="expert",
    )(*inputs)


def visible(doc_row, pad_row):
    total_rows = doc_row.shape[0]
    query_pos = jnp.arange(total_rows)[:, None]
    key_pos = jnp.arange(total_rows)[None, :]
    same_doc = doc_row[:, None] == doc_row[None, :]
    is_real = (pad_row[None, :] == 1) | (query_pos == key_pos)
    return (key_pos <= query_pos) & same_doc & is_real


def masked_scores(queries, key_rows, allowed):
    scores = jnp.einsum("qhd,khd->hqk", queries, key_rows, preferred_element_type=F32)
    return jnp.where(allowed[None], scores * HEAD_DIM**-0.5, MASKED)


def attend_forward(queries, key_rows, value_rows, allowed):
    scores = masked_scores(queries, key_rows, allowed)
    row_peak = jnp.max(scores, -1, keepdims=True)
    exponent = jnp.exp(scores - row_peak)
    row_total = jnp.sum(exponent, -1, keepdims=True)
    weights = (exponent / row_total).astype(BF)
    output = jnp.einsum("hqk,khd->qhd", weights, value_rows, preferred_element_type=F32)
    return output, row_peak + jnp.log(row_total)


def attend_backward(queries, key_rows, value_rows, allowed, log_total, heads_grad):
    scale = HEAD_DIM**-0.5
    scores = masked_scores(queries, key_rows, allowed)
    weights = jnp.exp(scores - log_total)
    weight_grad = jnp.einsum("qhd,khd->hqk", heads_grad, value_rows, preferred_element_type=F32)
    row_delta = jnp.sum(weights * weight_grad, -1, keepdims=True)
    score_grad = (weights * (weight_grad - row_delta)).astype(BF)
    query_grad = scale * jnp.einsum("hqk,khd->qhd", score_grad, key_rows, preferred_element_type=F32)
    key_grad = scale * jnp.einsum("hqk,qhd->khd", score_grad, queries, preferred_element_type=F32)
    value_grad = jnp.einsum(
        "hqk,qhd->khd", weights.astype(BF), heads_grad, preferred_element_type=F32
    )
    return query_grad, key_grad, value_grad


def make_shards(ne, nh):
    def to_experts(blocks):
        return lax.all_to_all(blocks, "expert", split_axis=0, concat_axis=0, tiled=True)

    def reduce_quarters(rows):
        blocks = rows.reshape(nh, -1, rows.shape[-1])
        bit = 1
        while bit < nh:
            keep = [r for r in range(blocks.shape[0]) if r % 2 == 0]
            send = [r for r in range(blocks.shape[0]) if r % 2 == 1]
            got = swap(jnp.concatenate([blocks[r] for r in send], 0), "hidden", bit)
            blocks = (
                jnp.stack([blocks[r] for r in keep]).astype(F32)
                + got.reshape(len(keep), -1, rows.shape[-1]).astype(F32)
            ).astype(BF)
            bit *= 2
        return blocks[0]

    def gather_quarters(rows):
        bit = nh // 2
        while bit >= 1:
            rows = jnp.concatenate([rows, swap(rows, "hidden", bit)], 0)
            bit //= 2
        return rows

    def quarter_order():
        order = [0]
        bit = nh // 2
        while bit >= 1:
            order = order + [r ^ bit for r in order]
            bit //= 2
        return order

    def sum_hidden(rows):
        h = lax.axis_index("hidden")
        count = rows.shape[0] // 2
        flag = h % 2
        kept = lax.dynamic_slice_in_dim(rows, flag * count, count, 0)
        sent = lax.dynamic_slice_in_dim(rows, (1 - flag) * count, count, 0)
        kept = (kept.astype(F32) + swap(sent, "hidden", 1).astype(F32)).astype(BF)
        bit = 2
        while bit < nh:
            kept = (kept.astype(F32) + swap(kept, "hidden", bit).astype(F32)).astype(BF)
            bit *= 2
        return ordered(flag, kept, swap(kept, "hidden", 1))

    def shards(
        tokens,
        doc_ids,
        pad_mask,
        norm1_gain,
        norm1_bias,
        qkv_weight,
        out_weight,
        norm2_gain,
        norm2_bias,
        router,
        routes,
        up_weight,
        down_weight,
        cotangent,
    ):
        micro_count, row_count, width = tokens.shape
        expert_count = router.shape[1]
        top_count = routes.shape[2]
        pack_cap = 2 * row_count * top_count // expert_count
        quarter = row_count // nh
        cap = round_up((pack_cap + (nh - 1) * (expert_count - 1)) // nh + 2, TILE)
        local_heads = qkv_weight.shape[2] // HEAD_DIM
        e_idx = lax.axis_index("expert")
        h_idx = lax.axis_index("hidden")
        micros = range(micro_count)

        slice_order = quarter_order()
        far = nh // 2
        up_far = swap(up_weight[0], "hidden", far)

        def spread(mine, got):
            parts = [mine, got]
            bit = far // 2
            while bit >= 1:
                parts = parts + [swap(x, "hidden", bit) for x in parts]
                bit //= 2
            return [parts[slice_order.index(r)] for r in range(nh)]

        def route(m):
            low = jnp.min(routes[m], -1)
            high = jnp.max(routes[m], -1)
            key = (low * expert_count + high) * row_count + jnp.arange(row_count, dtype=jnp.int32)
            rank = jnp.sum((key[:, None] < key[None, :]).astype(jnp.int32), 0)
            targets = jnp.concatenate(
                [jnp.arange(quarter, dtype=jnp.int32) * nh + (h_idx ^ r) for r in range(nh)]
            )
            perm = (targets[:, None] == rank[None, :]).astype(BF)
            mine = jnp.dot(perm[:quarter], routes[m].astype(BF), preferred_element_type=F32)
            first, second = mine[:, 0], mine[:, 1]
            names = jnp.arange(expert_count, dtype=F32)[:, None]
            member = (first[None, :] == names) | (second[None, :] == names)
            before = (jnp.arange(quarter)[:, None] < jnp.arange(quarter)[None, :]).astype(BF)
            place = jnp.dot(member.astype(BF), before, preferred_element_type=F32)
            slot = jnp.arange(cap, dtype=F32)[None, :, None]
            table = ((slot == place[:, None, :]) & member[:, None, :]).astype(BF)
            others = (first + second)[None, :] - names
            return perm, table, member, others

        def dispatch(table, rows):
            return jnp.einsum("ejt,td->ejd", table, rows, preferred_element_type=F32).astype(BF)

        def dispatch_upstream(m, perm, table, others):
            up_rows = jnp.dot(perm[:quarter], cotangent[m], preferred_element_type=F32)
            other = jnp.sum(table.astype(F32) * others[:, None, :], -1)
            other = jnp.pad(other[:, None, :], ((0, 0), (0, 0), (0, width - cap)))
            sent = jnp.einsum("ejt,td->ejd", table, up_rows.astype(BF), preferred_element_type=F32)
            last = (jnp.arange(cap) == cap - 1)[None, :, None]
            return up_rows, jnp.where(last, other, sent).astype(BF)

        perms, tables, upstream_mine, upstream_slots = [], [], [], []
        state = []
        for m in micros:
            if m == 0:
                perm, table, member, others = route(m)
                up_rows, up_sent = dispatch_upstream(m, perm, table, others)
                upstream_slots.append(to_experts(up_sent))
                following = None
            else:
                perm, table, member, others, up_rows, up_sent = following
            perms.append(perm)
            tables.append(table)
            upstream_mine.append(up_rows)
            mine_tokens = after(tokens[m], up_sent)
            inputs = mine_tokens.astype(F32)
            allowed = visible(doc_ids[m, 0], pad_mask[m])
            normed1, scale1 = normalize(inputs)
            attn_in = (normed1 * norm1_gain + norm1_bias).astype(BF)
            projected = jnp.einsum(
                "rd,cdf->crf", attn_in, qkv_weight, preferred_element_type=F32
            ).astype(BF)
            heads = projected.reshape(3, row_count, local_heads, HEAD_DIM)
            heads_out, log_total = attend_forward(heads[0], heads[1], heads[2], allowed)
            heads_low = heads_out.reshape(row_count, -1).astype(BF)
            heads_sorted = jnp.dot(perms[m], heads_low, preferred_element_type=F32).astype(BF)
            term = jnp.dot(heads_sorted, out_weight, preferred_element_type=F32).astype(BF)
            if m == 0:
                term, up_far = after((term, up_far), up_far)
                down_mine = after(down_weight[0], term)
                down_far = swap(down_mine, "hidden", far)
                ups = spread(up_weight[0], up_far)
            elif m == micro_count - 1:
                term, down_far = after((term, down_far), down_far)
                downs = spread(down_weight[0], down_far)
            attention = reduce_quarters(term).astype(F32)
            inputs_mine = jnp.dot(perm[:quarter], mine_tokens, preferred_element_type=F32)
            residual = inputs_mine + attention
            normed2, scale2 = normalize(residual)
            moe_in = (normed2 * norm2_gain + norm2_bias).astype(BF)
            logits = jnp.dot(moe_in, router, preferred_element_type=F32).T
            masked = jnp.where(member, logits, MASKED)
            raised = jnp.where(member, jnp.exp(masked - jnp.max(masked, 0, keepdims=True)), 0.0)
            gates = raised / jnp.sum(raised, 0, keepdims=True)
            if m + 1 < micro_count:
                following = route(m + 1)
                moe_in, following = after((moe_in, following), following)
            sent = dispatch(table, moe_in)
            received = to_experts(sent)
            if m + 1 < micro_count:
                perm, table, member, others = after(following, sent)
                up_rows, up_sent = dispatch_upstream(m + 1, perm, table, others)
                upstream_slots.append(to_experts(up_sent))
                following = (perm, table, member, others, up_rows, up_sent)
            last_sent = sent
            state.append(
                dict(
                    inputs=inputs,
                    allowed=allowed,
                    normed1=normed1,
                    scale1=scale1,
                    attn_in=attn_in,
                    heads=heads,
                    log_total=log_total,
                    heads_sorted=heads_sorted,
                    attention=attention,
                    normed2=normed2,
                    scale2=scale2,
                    moe_in=moe_in,
                    gates=gates,
                    received=received,
                )
            )

        own_expert = jnp.full((1,), e_idx, jnp.int32)
        held = None
        for m in micros:
            s = state[m]
            rows = after(s["received"], last_sent) if m == 0 else s["received"]
            out, copies, *held = run_expert(
                own_expert,
                rows,
                upstream_slots[m],
                router,
                ups,
                downs,
                held,
                m,
                micro_count,
            )
            s["copies_back"] = to_experts(copies)
            s["out"] = out
        for m in micros:
            state[m]["out_back"] = to_experts(after(state[m]["out"], copies))

        rows_all, grads_all, act_all, pre_all = held
        parts = []
        made = []
        for left, right in ((rows_all, pre_all), (grads_all, act_all)):
            hidden = right.shape[1] // nh
            slabs = [
                jnp.einsum(
                    "rd,rf->df",
                    left,
                    right[:, r * hidden : (r + 1) * hidden],
                    preferred_element_type=F32,
                ).astype(BF)
                for r in range(nh)
            ]
            made += slabs
            bit = 1
            while bit < nh:
                got = [swap(slab, "hidden", bit) for slab in slabs[1::2]]
                slabs = [
                    (mine.astype(F32) + other.astype(F32)).astype(BF)
                    for mine, other in zip(slabs[0::2], got)
                ]
                bit *= 2
            rows = to_experts(slabs[0].reshape(ne, width // ne, -1))
            parts.append(rows[ne // 2 :].astype(F32))

        grad_router = 0.0
        gain2_total, bias2_total = 0.0, 0.0
        for m in micros:
            s = state[m]
            back = after(s["copies_back"], made) if m == 0 else s["copies_back"]
            table = tables[m]
            copies_sum = jnp.einsum("ejt,ejd->td", table, back, preferred_element_type=F32)
            slot_grad = back[:, cap - 1, :cap].astype(F32) + back[:, cap - 2, :cap].astype(F32)
            gate_grad = jnp.sum(table.astype(F32) * slot_grad[:, :, None], 1)
            gates = s["gates"]
            logit_grad = gates * (gate_grad - jnp.sum(gates * gate_grad, 0, keepdims=True))
            normed2_grad = copies_sum + jnp.einsum(
                "et,de->td", logit_grad, router.astype(F32), precision=PRECISE
            )
            grad_router = grad_router + jnp.einsum(
                "et,td->ed", logit_grad, s["moe_in"].astype(F32), precision=PRECISE
            )
            gain2_total = gain2_total + jnp.sum(normed2_grad * s["normed2"], 0)
            bias2_total = bias2_total + jnp.sum(normed2_grad, 0)
            resid_grad = upstream_mine[m] + normalize_pull(
                s["normed2"], s["scale2"], norm2_gain, normed2_grad
            )
            s["resid_all"] = gather_quarters(resid_grad.astype(BF))
            weighted = (table.astype(F32) * gates[:, None, :]).astype(BF)
            mixture = jnp.einsum("ejt,ejd->td", weighted, s["out_back"], preferred_element_type=F32)
            s["delta_all"] = gather_quarters((s["attention"] + mixture).astype(BF))

        small = jnp.concatenate([gain2_total[None], bias2_total[None], grad_router], 0)
        small_rows = round_up(small.shape[0], 16)
        small = jnp.pad(small, ((0, small_rows - small.shape[0]), (0, 0))).astype(BF)

        order = quarter_order()
        grad_qkv, grad_proj = 0.0, 0.0
        gain1_total, bias1_total = 0.0, 0.0
        outputs, input_grads = [], []
        for m in micros:
            s = state[m]
            perm = perms[m].reshape(nh, quarter, row_count)
            perm_all = jnp.concatenate([perm[r] for r in order], 0)
            heads_sorted = s["heads_sorted"].reshape(nh, quarter, -1)
            heads_sorted = jnp.concatenate([heads_sorted[r] for r in order], 0)
            resid_all = s["resid_all"]
            grad_proj = grad_proj + jnp.einsum(
                "rf,rd->fd", heads_sorted, resid_all, preferred_element_type=F32
            )
            heads_grad = jnp.einsum(
                "rd,fd->rf", resid_all, out_weight, preferred_element_type=F32
            ).astype(BF)
            heads_grad = jnp.einsum(
                "rt,rf->tf", perm_all, heads_grad, preferred_element_type=F32
            ).astype(BF)
            heads = s["heads"]
            grads = attend_backward(
                heads[0],
                heads[1],
                heads[2],
                s["allowed"],
                s["log_total"],
                heads_grad.reshape(row_count, local_heads, HEAD_DIM),
            )
            qkv_grad = jnp.stack(grads).reshape(3, row_count, -1).astype(BF)
            grad_qkv = grad_qkv + jnp.einsum(
                "rd,crf->cdf", s["attn_in"], qkv_grad, preferred_element_type=F32
            )
            term = jnp.einsum(
                "crf,cdf->rd", qkv_grad, qkv_weight, preferred_element_type=F32
            ).astype(BF)
            if m == micro_count - 1:
                total = sum_hidden(jnp.concatenate([term, small], 0))
                small_sum = total[row_count:]
                normed1_grad = total[:row_count].astype(F32)
            else:
                normed1_grad = sum_hidden(term).astype(F32)
            gain1_total = gain1_total + jnp.sum(normed1_grad * s["normed1"], 0)
            bias1_total = bias1_total + jnp.sum(normed1_grad, 0)
            resid_grad = jnp.einsum("rt,rd->td", perm_all, resid_all, preferred_element_type=F32)
            input_grads.append(
                resid_grad + normalize_pull(s["normed1"], s["scale1"], norm1_gain, normed1_grad)
            )
            delta = jnp.einsum("rt,rd->td", perm_all, s["delta_all"], preferred_element_type=F32)
            outputs.append(s["inputs"] + delta)

        flat = jnp.concatenate([grad_qkv.reshape(-1), grad_proj.reshape(-1)]).astype(BF)
        share = flat.reshape(ne, -1, width)
        bit = 1
        while bit < ne:
            flag = (e_idx // bit) % 2
            pairs = share.reshape(share.shape[0] // 2, 2, -1, width)
            kept = lax.dynamic_index_in_dim(pairs, flag, 1, False)
            sent = lax.dynamic_index_in_dim(pairs, 1 - flag, 1, False)
            share = (kept.astype(F32) + swap(sent, "expert", bit).astype(F32)).astype(BF)
            bit *= 2
        share = share[0]
        share_rows = share.shape[0]
        extra = jnp.concatenate([gain1_total[None], bias1_total[None]], 0).astype(BF)
        extra = jnp.concatenate([extra, small_sum], 0)
        extra = jnp.pad(extra, ((0, round_up(extra.shape[0], 16) - extra.shape[0]), (0, 0)))
        gathered = jnp.concatenate([share, extra], 0)[None]
        bit = ne // 2
        while bit >= 1:
            gathered = jnp.concatenate([gathered, swap(gathered, "expert", bit)], 0)
            bit //= 2
        bits = []
        bit = ne // 2
        found = [0]
        while bit >= 1:
            found = found + [r ^ bit for r in found]
            bit //= 2
        sums = jnp.sum(gathered[:, share_rows:].astype(F32), 0)
        where = jnp.zeros((ne,), jnp.int32)
        slots = jnp.array([found.index(r) for r in range(ne)], jnp.int32)
        where = slots[jnp.arange(ne, dtype=jnp.int32) ^ e_idx]
        flat = gathered[:, :share_rows][where].astype(F32).reshape(-1)
        split = grad_qkv.size
        return (
            jnp.stack(outputs),
            jnp.stack(input_grads),
            sums[0],
            sums[1],
            flat[:split].reshape(grad_qkv.shape),
            flat[split:].reshape(grad_proj.shape),
            sums[2],
            sums[3],
            sums[4 : 4 + expert_count].T,
            parts[0],
            parts[1],
        )

    return shards


def solution(mesh):
    placed = (
        P(None, "expert", None),
        P(None, "expert", None),
        P(None, "expert"),
        P(),
        P(),
        P(None, None, "hidden"),
        P("hidden", None),
        P(),
        P(),
        P(),
        P(None, "expert", None),
        P("expert", None, "hidden"),
        P("expert", None, "hidden"),
        P(None, "expert", None),
    )
    return jax.shard_map(
        make_shards(mesh.shape["expert"], mesh.shape["hidden"]),
        mesh=mesh,
        in_specs=placed,
        out_specs=(
            P(None, "expert", None),
            P(None, "expert", None),
            P(),
            P(),
            P(None, None, "hidden"),
            P("hidden", None),
            P(),
            P(),
            P(),
            P(None, "expert", "hidden"),
            P(None, "expert", "hidden"),
        ),
        check_vma=False,
    )
```

```python
import jax
import jax.numpy as jnp
from jax import lax
from jax.experimental import pallas as pl
from jax.experimental.pallas import tpu as pltpu
from jax.sharding import PartitionSpec as P

HEAD_DIM = 64
EPSILON = 1e-05
PRECISE = lax.Precision.HIGHEST
MASKED = -1e30
TILE = 16
BF = jnp.bfloat16
F32 = jnp.float32


def round_up(value, step):
    return -(-value // step) * step


def swap(values, axis, bit):
    size = lax.axis_size(axis)
    return lax.ppermute(values, axis, [(i, i ^ bit) for i in range(size)])


def ordered(flag, mine, other):
    return jnp.where(
        flag == 0, jnp.concatenate([mine, other], 0), jnp.concatenate([other, mine], 0)
    )


def normalize(values):
    centre = values - jnp.mean(values, -1, keepdims=True)
    spread = jnp.mean(centre * centre, -1, keepdims=True)
    scale = lax.rsqrt(spread + EPSILON)
    return centre * scale, scale


def normalize_pull(normed, scale, gain, grad):
    wide = grad * gain
    return scale * (
        wide
        - jnp.mean(wide, -1, keepdims=True)
        - normed * jnp.mean(wide * normed, -1, keepdims=True)
    )


def gelu_pair(v):
    c0 = 0.7978845608028654
    inner = c0 * (v + 0.044715 * v * v * v)
    t = jnp.tanh(inner)
    act = 0.5 * v * (1.0 + t)
    slope = 0.5 * (1.0 + t) + 0.5 * v * (1.0 - t * t) * (c0 * (1.0 + 3 * 0.044715 * v * v))
    return act, slope


def after(values, *others):
    return lax.optimization_barrier((values, others))[0]


def diagonal(count):
    return lax.broadcasted_iota(jnp.int32, (count, count), 0) == lax.broadcasted_iota(
        jnp.int32, (count, count), 1
    )


def expert_body(slices, packs, cap, width, aliased):
    rows_n = packs * cap

    def body(own_ref, rows_ref, cot_ref, router_ref, *refs):
        ups, downs = refs[:slices], refs[slices : 2 * slices]
        refs = refs[2 * slices + (1 if aliased else 0) :]
        (out_ref, copies_ref, rows_all, grads_all, act_all, pre_all) = refs[:6]
        up_v, down_v, grad_rows, acc_out, acc_copies, sems = refs[6:]
        i, s = pl.program_id(0), pl.program_id(1)

        def fetch(r):
            return (
                pltpu.make_async_copy(ups[r], up_v.at[r], sems.at[0, r]),
                pltpu.make_async_copy(downs[r], down_v.at[r], sems.at[1, r]),
            )

        @pl.when((i == 0) & (s == 0))
        def _():
            for r in range(slices):
                for copy in fetch(r):
                    copy.start()

        for r in range(slices):

            @pl.when((i == 0) & (s == r))
            def _():
                for copy in fetch(r):
                    copy.wait()

        @pl.when(s == 0)
        def _():
            rows = rows_ref[...].reshape(rows_n, width)
            rows_all[...] = rows
            logits = jnp.dot(rows, router_ref[...], preferred_element_type=F32)
            ordinals = lax.broadcasted_iota(jnp.int32, logits.shape, 1).astype(F32)
            eye = diagonal(cap)
            other = []
            for p in range(packs):
                line = cot_ref[p, cap - TILE :, :][TILE - 1 :, :cap].astype(F32)
                other.append(jnp.sum(jnp.where(eye, line, 0.0), 1, keepdims=True))
            other = jnp.concatenate(other, 0)
            own = own_ref[0].astype(F32)
            picks = jnp.where(ordinals == own, 1.0, 0.0) - jnp.where(ordinals == other, 1.0, 0.0)
            gate = jax.nn.sigmoid(jnp.sum(logits * picks, -1, keepdims=True))
            cot = cot_ref[...].reshape(rows_n, width).astype(F32)
            low = (gate * cot).astype(BF)
            grad_rows[...] = low
            grads_all[...] = low

        up, down = up_v[s], down_v[s]
        pre = jnp.dot(rows_ref[...].reshape(rows_n, width), up, preferred_element_type=F32)
        act_grad = jnp.dot(grad_rows[...], down, preferred_element_type=F32)
        act, slope = gelu_pair(pre)
        act = act.astype(BF)
        act_all[...] = act
        pre_grad = (act_grad * slope).astype(BF)
        pre_all[...] = pre_grad
        along = (((1,), (1,)), ((), ()))
        out = lax.dot_general(act, down, along, preferred_element_type=F32)
        copies = lax.dot_general(pre_grad, up, along, preferred_element_type=F32)

        @pl.when(s == 0)
        def _():
            acc_out[...] = out
            acc_copies[...] = copies

        @pl.when(s > 0)
        def _():
            acc_out[...] += out
            acc_copies[...] += copies

        @pl.when(s == slices - 1)
        def _():
            low = acc_out[...].astype(BF)
            out_ref[...] = low.reshape(packs, cap, width)
            copies_ref[...] = acc_copies[...].astype(BF).reshape(packs, cap, width)
            cot = cot_ref[...].reshape(rows_n, width).astype(F32)
            gate_grad = jnp.sum(cot * low.astype(F32), -1, keepdims=True)
            eye = diagonal(cap)
            index = lax.broadcasted_iota(jnp.int32, (TILE, width), 0)
            for p in range(packs):
                column = gate_grad[p * cap : (p + 1) * cap]
                line = jnp.sum(jnp.where(eye, column, 0.0), 0, keepdims=True)
                line = jnp.concatenate([line, jnp.zeros((1, width - cap), F32)], 1)
                coarse = line.astype(BF).astype(F32)
                tail = copies_ref[p, cap - TILE :, :].astype(F32)
                tail = jnp.where(index == TILE - 1, coarse, tail)
                tail = jnp.where(index == TILE - 2, line - coarse, tail)
                copies_ref[p, cap - TILE :, :] = tail.astype(BF)

    return body


def run_expert(own, rows, row_part, cots, cot_part, router, ups, downs, held, m, micro_count):
    blocks, width = rows.shape[0], rows.shape[2]
    cap = cots.shape[1] // (cot_part + 1)
    slices = len(ups)
    hidden = ups[0].shape[1]
    packs = max(p for p in range(1, blocks + 1) if blocks % p == 0 and p * cap <= 448)
    steps = blocks // packs
    total = blocks * cap
    aliased = held is not None
    rows_n = packs * cap

    def block(part):
        return pl.BlockSpec((packs, cap, width), lambda i, s: (i, part, 0))

    any_spec = pl.BlockSpec(memory_space=pl.ANY)
    whole_rows = pl.BlockSpec((rows_n, width), lambda i, s: (i, 0))
    whole_hidden = pl.BlockSpec((rows_n, hidden), lambda i, s: (i, s))
    inputs = [own, rows, cots, router, *ups, *downs]
    in_specs = [
        pl.BlockSpec(memory_space=pltpu.SMEM),
        block(row_part),
        block(cot_part),
        pl.BlockSpec(router.shape, lambda i, s: (0, 0)),
    ] + [any_spec] * (2 * slices)
    aliases = {}
    if aliased:
        aliases = {len(inputs): 0}
        inputs.append(held)
        in_specs.append(any_spec)
    return pl.pallas_call(
        expert_body(slices, packs, cap, width, aliased),
        grid=(steps, slices),
        in_specs=in_specs,
        out_specs=[block(m), block(0), whole_rows, whole_rows, whole_hidden, whole_hidden],
        out_shape=[
            jax.ShapeDtypeStruct((blocks, micro_count * cap, width), BF),
            jax.ShapeDtypeStruct((blocks, cap, width), BF),
            jax.ShapeDtypeStruct((total, width), BF),
            jax.ShapeDtypeStruct((total, width), BF),
            jax.ShapeDtypeStruct((total, slices * hidden), BF),
            jax.ShapeDtypeStruct((total, slices * hidden), BF),
        ],
        scratch_shapes=[
            pltpu.VMEM((slices,) + ups[0].shape, BF),
            pltpu.VMEM((slices,) + downs[0].shape, BF),
            pltpu.VMEM((rows_n, width), BF),
            pltpu.VMEM((rows_n, width), F32),
            pltpu.VMEM((rows_n, width), F32),
            pltpu.SemaphoreType.DMA((2, slices)),
        ],
        input_output_aliases=aliases,
        compiler_params=pltpu.CompilerParams(vmem_limit_bytes=48 * 1024 * 1024),
        name="expert",
    )(*inputs)


def visible(doc_row, pad_row):
    total_rows = doc_row.shape[0]
    query_pos = jnp.arange(total_rows)[:, None]
    key_pos = jnp.arange(total_rows)[None, :]
    same_doc = doc_row[:, None] == doc_row[None, :]
    is_real = (pad_row[None, :] == 1) | (query_pos == key_pos)
    return (key_pos <= query_pos) & same_doc & is_real


def masked_scores(queries, key_rows, allowed):
    scores = jnp.einsum("qhd,khd->hqk", queries, key_rows, preferred_element_type=F32)
    return jnp.where(allowed[None], scores * HEAD_DIM**-0.5, MASKED)


def attend_forward(queries, key_rows, value_rows, allowed):
    scores = masked_scores(queries, key_rows, allowed)
    row_peak = jnp.max(scores, -1, keepdims=True)
    exponent = jnp.exp(scores - row_peak)
    row_total = jnp.sum(exponent, -1, keepdims=True)
    weights = (exponent / row_total).astype(BF)
    output = jnp.einsum("hqk,khd->qhd", weights, value_rows, preferred_element_type=F32)
    return output, row_peak + jnp.log(row_total)


def attend_backward(queries, key_rows, value_rows, allowed, log_total, heads_grad):
    scale = HEAD_DIM**-0.5
    scores = masked_scores(queries, key_rows, allowed)
    weights = jnp.exp(scores - log_total)
    weight_grad = jnp.einsum("qhd,khd->hqk", heads_grad, value_rows, preferred_element_type=F32)
    row_delta = jnp.sum(weights * weight_grad, -1, keepdims=True)
    score_grad = (weights * (weight_grad - row_delta)).astype(BF)
    query_grad = scale * jnp.einsum("hqk,khd->qhd", score_grad, key_rows, preferred_element_type=F32)
    key_grad = scale * jnp.einsum("hqk,qhd->khd", score_grad, queries, preferred_element_type=F32)
    value_grad = jnp.einsum(
        "hqk,qhd->khd", weights.astype(BF), heads_grad, preferred_element_type=F32
    )
    return query_grad, key_grad, value_grad


def make_shards(ne, nh):
    def to_experts(blocks):
        return lax.all_to_all(blocks, "expert", split_axis=0, concat_axis=0, tiled=True)

    def reduce_quarters(rows):
        blocks = rows.reshape(nh, -1, rows.shape[-1])
        bit = 1
        while bit < nh:
            keep = [r for r in range(blocks.shape[0]) if r % 2 == 0]
            send = [r for r in range(blocks.shape[0]) if r % 2 == 1]
            got = swap(jnp.concatenate([blocks[r] for r in send], 0), "hidden", bit)
            blocks = (
                jnp.stack([blocks[r] for r in keep]).astype(F32)
                + got.reshape(len(keep), -1, rows.shape[-1]).astype(F32)
            ).astype(BF)
            bit *= 2
        return blocks[0]

    def gather_quarters(rows):
        bit = nh // 2
        while bit >= 1:
            rows = jnp.concatenate([rows, swap(rows, "hidden", bit)], 0)
            bit //= 2
        return rows

    def quarter_order():
        order = [0]
        bit = nh // 2
        while bit >= 1:
            order = order + [r ^ bit for r in order]
            bit //= 2
        return order

    def sum_hidden(rows):
        h = lax.axis_index("hidden")
        count = rows.shape[0] // 2
        flag = h % 2
        kept = lax.dynamic_slice_in_dim(rows, flag * count, count, 0)
        sent = lax.dynamic_slice_in_dim(rows, (1 - flag) * count, count, 0)
        kept = (kept.astype(F32) + swap(sent, "hidden", 1).astype(F32)).astype(BF)
        bit = 2
        while bit < nh:
            kept = (kept.astype(F32) + swap(kept, "hidden", bit).astype(F32)).astype(BF)
            bit *= 2
        return ordered(flag, kept, swap(kept, "hidden", 1))

    def shards(
        tokens,
        doc_ids,
        pad_mask,
        norm1_gain,
        norm1_bias,
        qkv_weight,
        out_weight,
        norm2_gain,
        norm2_bias,
        router,
        routes,
        up_weight,
        down_weight,
        cotangent,
    ):
        micro_count, row_count, width = tokens.shape
        expert_count = router.shape[1]
        top_count = routes.shape[2]
        pack_cap = 2 * row_count * top_count // expert_count
        quarter = row_count // nh
        cap = round_up((pack_cap + (nh - 1) * (expert_count - 1)) // nh + 2, TILE)
        local_heads = qkv_weight.shape[2] // HEAD_DIM
        e_idx = lax.axis_index("expert")
        h_idx = lax.axis_index("hidden")
        micros = range(micro_count)

        slice_order = quarter_order()
        far = nh // 2
        up_far = swap(up_weight[0], "hidden", far)

        def spread(mine, got):
            parts = [mine, got]
            bit = far // 2
            while bit >= 1:
                parts = parts + [swap(x, "hidden", bit) for x in parts]
                bit //= 2
            return [parts[slice_order.index(r)] for r in range(nh)]

        def route(m):
            low = jnp.min(routes[m], -1)
            high = jnp.max(routes[m], -1)
            key = (low * expert_count + high) * row_count + jnp.arange(row_count, dtype=jnp.int32)
            rank = jnp.sum((key[:, None] < key[None, :]).astype(jnp.int32), 0)
            targets = jnp.concatenate(
                [jnp.arange(quarter, dtype=jnp.int32) * nh + (h_idx ^ r) for r in range(nh)]
            )
            perm = (targets[:, None] == rank[None, :]).astype(BF)
            mine = jnp.dot(perm[:quarter], routes[m].astype(BF), preferred_element_type=F32)
            first, second = mine[:, 0], mine[:, 1]
            names = jnp.arange(expert_count, dtype=F32)[:, None]
            member = (first[None, :] == names) | (second[None, :] == names)
            before = (jnp.arange(quarter)[:, None] < jnp.arange(quarter)[None, :]).astype(BF)
            place = jnp.dot(member.astype(BF), before, preferred_element_type=F32)
            slot = jnp.arange(cap, dtype=F32)[None, :, None]
            table = ((slot == place[:, None, :]) & member[:, None, :]).astype(BF)
            others = (first + second)[None, :] - names
            return perm, table, member, others

        def dispatch(table, rows):
            return jnp.einsum("ejt,td->ejd", table, rows, preferred_element_type=F32).astype(BF)

        def dispatch_upstream(m, perm, table, others):
            up_rows = jnp.dot(perm[:quarter], cotangent[m], preferred_element_type=F32)
            other = jnp.sum(table.astype(F32) * others[:, None, :], -1)
            other = jnp.pad(other[:, None, :], ((0, 0), (0, 0), (0, width - cap)))
            sent = jnp.einsum("ejt,td->ejd", table, up_rows.astype(BF), preferred_element_type=F32)
            last = (jnp.arange(cap) == cap - 1)[None, :, None]
            return up_rows, jnp.where(last, other, sent).astype(BF)

        perms, tables, upstream_mine = [], [], []
        state = []
        for m in micros:
            if m == 0:
                perm, table, member, others = route(m)
                up_rows, up_sent = dispatch_upstream(m, perm, table, others)
                upstream_slots = to_experts(up_sent)
                earlier = up_sent
            else:
                perm, table, member, others = following
                up_rows, up_sent = dispatch_upstream(m, perm, table, others)
                earlier = last_sent
            perms.append(perm)
            tables.append(table)
            upstream_mine.append(up_rows)
            mine_tokens = after(tokens[m], earlier)
            inputs = mine_tokens.astype(F32)
            allowed = visible(doc_ids[m, 0], pad_mask[m])
            normed1, scale1 = normalize(inputs)
            attn_in = (normed1 * norm1_gain + norm1_bias).astype(BF)
            projected = jnp.einsum(
                "rd,cdf->crf", attn_in, qkv_weight, preferred_element_type=F32
            ).astype(BF)
            heads = projected.reshape(3, row_count, local_heads, HEAD_DIM)
            heads_out, log_total = attend_forward(heads[0], heads[1], heads[2], allowed)
            heads_low = heads_out.reshape(row_count, -1).astype(BF)
            heads_sorted = jnp.dot(perms[m], heads_low, preferred_element_type=F32).astype(BF)
            term = jnp.dot(heads_sorted, out_weight, preferred_element_type=F32).astype(BF)
            if m == 0:
                term, up_far = after((term, up_far), up_far)
                down_mine = after(down_weight[0], term)
                down_far = swap(down_mine, "hidden", far)
                ups = spread(up_weight[0], up_far)
            elif m == micro_count - 1:
                term, down_far = after((term, down_far), down_far)
                downs = spread(down_weight[0], down_far)
            attention = reduce_quarters(term).astype(F32)
            inputs_mine = jnp.dot(perm[:quarter], mine_tokens, preferred_element_type=F32)
            residual = inputs_mine + attention
            normed2, scale2 = normalize(residual)
            moe_in = (normed2 * norm2_gain + norm2_bias).astype(BF)
            logits = jnp.dot(moe_in, router, preferred_element_type=F32).T
            masked = jnp.where(member, logits, MASKED)
            raised = jnp.where(member, jnp.exp(masked - jnp.max(masked, 0, keepdims=True)), 0.0)
            gates = raised / jnp.sum(raised, 0, keepdims=True)
            if m + 1 < micro_count:
                following = route(m + 1)
                moe_in, following = after((moe_in, following), following)
            last_sent = dispatch(table, moe_in)
            if m == 0:
                received = (to_experts(last_sent), 0, upstream_slots, 0)
            else:
                both = to_experts(jnp.concatenate([last_sent, up_sent], 1))
                received = (both, 0, both, 1)
            state.append(
                dict(
                    inputs=inputs,
                    allowed=allowed,
                    normed1=normed1,
                    scale1=scale1,
                    attn_in=attn_in,
                    heads=heads,
                    log_total=log_total,
                    heads_sorted=heads_sorted,
                    attention=attention,
                    normed2=normed2,
                    scale2=scale2,
                    moe_in=moe_in,
                    gates=gates,
                    received=received,
                )
            )

        own_expert = jnp.full((1,), e_idx, jnp.int32)
        held, slabs = None, None
        for m in micros:
            s = state[m]
            rows, row_part, cots, cot_part = s["received"]
            if m == 0:
                rows = after(rows, last_sent)
            else:
                rows = after(rows, slabs)
                cots = rows
            held, copies, rows_all, grads_all, act_all, pre_all = run_expert(
                own_expert,
                rows,
                row_part,
                cots,
                cot_part,
                router,
                ups,
                downs,
                held,
                m,
                micro_count,
            )
            s["copies_back"] = to_experts(copies)
            made = []
            for left, right in ((rows_all, pre_all), (grads_all, act_all)):
                hidden = right.shape[1] // nh
                for r in range(nh):
                    slab = jnp.einsum(
                        "rd,rf->df",
                        left,
                        right[:, r * hidden : (r + 1) * hidden],
                        preferred_element_type=F32,
                    )
                    if slabs is not None:
                        slab = slab + slabs[len(made)].astype(F32)
                    made.append(slab.astype(BF))
            slabs = made

        owned = []
        for part in (slabs[:nh], slabs[nh:]):
            bit = 1
            while bit < nh:
                got = [swap(slab, "hidden", bit) for slab in part[1::2]]
                part = [
                    (mine.astype(F32) + other.astype(F32)).astype(BF)
                    for mine, other in zip(part[0::2], got)
                ]
                bit *= 2
            owned.append(part[0].reshape(ne, width // ne, -1))
        owned = jnp.concatenate(owned, 1)

        order = quarter_order()
        grad_router = 0.0
        gain2_total, bias2_total = 0.0, 0.0
        previous = slabs
        for m in micros:
            s = state[m]
            back = s["copies_back"] = after(s["copies_back"], previous)
            table = tables[m]
            copies_sum = jnp.einsum("ejt,ejd->td", table, back, preferred_element_type=F32)
            slot_grad = back[:, cap - 1, :cap].astype(F32) + back[:, cap - 2, :cap].astype(F32)
            gate_grad = jnp.sum(table.astype(F32) * slot_grad[:, :, None], 1)
            gates = s["gates"]
            logit_grad = gates * (gate_grad - jnp.sum(gates * gate_grad, 0, keepdims=True))
            normed2_grad = copies_sum + jnp.einsum(
                "et,de->td", logit_grad, router.astype(F32), precision=PRECISE
            )
            grad_router = grad_router + jnp.einsum(
                "et,td->ed", logit_grad, s["moe_in"].astype(F32), precision=PRECISE
            )
            gain2_total = gain2_total + jnp.sum(normed2_grad * s["normed2"], 0)
            bias2_total = bias2_total + jnp.sum(normed2_grad, 0)
            resid_grad = upstream_mine[m] + normalize_pull(
                s["normed2"], s["scale2"], norm2_gain, normed2_grad
            )
            s["resid_all"] = gather_quarters(resid_grad.astype(BF))
            perm = perms[m].reshape(nh, quarter, row_count)
            s["perm_all"] = jnp.concatenate([perm[r] for r in order], 0)
            heads_grad = jnp.einsum(
                "rd,fd->rf", s["resid_all"], out_weight, preferred_element_type=F32
            ).astype(BF)
            s["heads_grad"] = jnp.einsum(
                "rt,rf->tf", s["perm_all"], heads_grad, preferred_element_type=F32
            ).astype(BF)
            previous = s["heads_grad"]

        small = jnp.concatenate([gain2_total[None], bias2_total[None], grad_router], 0)
        small_rows = round_up(small.shape[0], 16)
        small = jnp.pad(small, ((0, small_rows - small.shape[0]), (0, 0))).astype(BF)

        grad_qkv, grad_proj = 0.0, 0.0
        gain1_total, bias1_total = 0.0, 0.0
        input_grads = []
        out_back = to_experts(after(held, state[-1]["copies_back"]))
        for m in micros:
            s = state[m]
            perm_all, resid_all, heads_grad = s["perm_all"], s["resid_all"], s["heads_grad"]
            heads_sorted = s["heads_sorted"].reshape(nh, quarter, -1)
            heads_sorted = jnp.concatenate([heads_sorted[r] for r in order], 0)
            grad_proj = grad_proj + jnp.einsum(
                "rf,rd->fd", heads_sorted, resid_all, preferred_element_type=F32
            )
            heads = s["heads"]
            grads = attend_backward(
                heads[0],
                heads[1],
                heads[2],
                s["allowed"],
                s["log_total"],
                heads_grad.reshape(row_count, local_heads, HEAD_DIM),
            )
            qkv_grad = jnp.stack(grads).reshape(3, row_count, -1).astype(BF)
            grad_qkv = grad_qkv + jnp.einsum(
                "rd,crf->cdf", s["attn_in"], qkv_grad, preferred_element_type=F32
            )
            term = jnp.einsum(
                "crf,cdf->rd", qkv_grad, qkv_weight, preferred_element_type=F32
            ).astype(BF)
            if m == micro_count - 1:
                total = sum_hidden(jnp.concatenate([term, small], 0))
                small_sum = total[row_count:]
                normed1_grad = total[:row_count].astype(F32)
            else:
                normed1_grad = sum_hidden(term).astype(F32)
            gain1_total = gain1_total + jnp.sum(normed1_grad * s["normed1"], 0)
            bias1_total = bias1_total + jnp.sum(normed1_grad, 0)
            resid_grad = jnp.einsum("rt,rd->td", perm_all, resid_all, preferred_element_type=F32)
            input_grads.append(
                resid_grad + normalize_pull(s["normed1"], s["scale1"], norm1_gain, normed1_grad)
            )
            if m == micro_count - 1:
                out_back, _ = after((out_back, term), term)

        parts = to_experts(after(owned, out_back))[ne // 2 :].astype(F32)

        flat = jnp.concatenate([grad_qkv.reshape(-1), grad_proj.reshape(-1)]).astype(BF)
        share = flat.reshape(ne, -1, width)
        bit = 1
        while bit < ne:
            flag = (e_idx // bit) % 2
            pairs = share.reshape(share.shape[0] // 2, 2, -1, width)
            kept = lax.dynamic_index_in_dim(pairs, flag, 1, False)
            sent = lax.dynamic_index_in_dim(pairs, 1 - flag, 1, False)
            share = (kept.astype(F32) + swap(sent, "expert", bit).astype(F32)).astype(BF)
            bit *= 2
        share = share[0]
        share_rows = share.shape[0]
        extra = jnp.concatenate([gain1_total[None], bias1_total[None]], 0).astype(BF)
        extra = jnp.concatenate([extra, small_sum], 0)
        extra = jnp.pad(extra, ((0, round_up(extra.shape[0], 16) - extra.shape[0]), (0, 0)))
        gathered = jnp.concatenate([share, extra], 0)[None]
        bit = ne // 2
        while bit >= 1:
            gathered = jnp.concatenate([gathered, swap(gathered, "expert", bit)], 0)
            bit //= 2
        bits = []
        bit = ne // 2
        found = [0]
        while bit >= 1:
            found = found + [r ^ bit for r in found]
            bit //= 2
        outputs = []
        for m in micros:
            s = state[m]
            weighted = (tables[m].astype(F32) * s["gates"][:, None, :]).astype(BF)
            mixture = jnp.einsum(
                "ejt,ejd->td",
                weighted,
                out_back[:, m * cap : (m + 1) * cap],
                preferred_element_type=F32,
            )
            delta_all = gather_quarters((s["attention"] + mixture).astype(BF))
            delta = jnp.einsum("rt,rd->td", s["perm_all"], delta_all, preferred_element_type=F32)
            outputs.append(s["inputs"] + delta)
        sums = jnp.sum(gathered[:, share_rows:].astype(F32), 0)
        where = jnp.zeros((ne,), jnp.int32)
        slots = jnp.array([found.index(r) for r in range(ne)], jnp.int32)
        where = slots[jnp.arange(ne, dtype=jnp.int32) ^ e_idx]
        flat = gathered[:, :share_rows][where].astype(F32).reshape(-1)
        split = grad_qkv.size
        return (
            jnp.stack(outputs),
            jnp.stack(input_grads),
            sums[0],
            sums[1],
            flat[:split].reshape(grad_qkv.shape),
            flat[split:].reshape(grad_proj.shape),
            sums[2],
            sums[3],
            sums[4 : 4 + expert_count].T,
            parts[:, : width // ne],
            parts[:, width // ne :],
        )

    return shards


def solution(mesh):
    placed = (
        P(None, "expert", None),
        P(None, "expert", None),
        P(None, "expert"),
        P(),
        P(),
        P(None, None, "hidden"),
        P("hidden", None),
        P(),
        P(),
        P(),
        P(None, "expert", None),
        P("expert", None, "hidden"),
        P("expert", None, "hidden"),
        P(None, "expert", None),
    )
    return jax.shard_map(
        make_shards(mesh.shape["expert"], mesh.shape["hidden"]),
        mesh=mesh,
        in_specs=placed,
        out_specs=(
            P(None, "expert", None),
            P(None, "expert", None),
            P(),
            P(),
            P(None, None, "hidden"),
            P("hidden", None),
            P(),
            P(),
            P(),
            P(None, "expert", "hidden"),
            P(None, "expert", "hidden"),
        ),
        check_vma=False,
    )
```

```python
import jax
import jax.numpy as jnp
from jax import lax
from jax.experimental import pallas as pl
from jax.experimental.pallas import tpu as pltpu
from jax.sharding import PartitionSpec as P

HEAD_DIM = 64
EPSILON = 1e-05
PRECISE = lax.Precision.HIGHEST
MASKED = -1e30
TILE = 16
LONGEST = 384
BLOCK = 256
BF = jnp.bfloat16
F32 = jnp.float32


def round_up(value, step):
    return -(-value // step) * step


def swap(values, axis, bit):
    size = lax.axis_size(axis)
    return lax.ppermute(values, axis, [(i, i ^ bit) for i in range(size)])


def ordered(flag, mine, other):
    return jnp.where(
        flag == 0, jnp.concatenate([mine, other], 0), jnp.concatenate([other, mine], 0)
    )


def normalize(values):
    centre = values - jnp.mean(values, -1, keepdims=True)
    spread = jnp.mean(centre * centre, -1, keepdims=True)
    scale = lax.rsqrt(spread + EPSILON)
    return centre * scale, scale


def normalize_pull(normed, scale, gain, grad):
    wide = grad * gain
    return scale * (
        wide
        - jnp.mean(wide, -1, keepdims=True)
        - normed * jnp.mean(wide * normed, -1, keepdims=True)
    )


def gelu_pair(v):
    c0 = 0.7978845608028654
    inner = c0 * (v + 0.044715 * v * v * v)
    t = jnp.tanh(inner)
    act = 0.5 * v * (1.0 + t)
    slope = 0.5 * (1.0 + t) + 0.5 * v * (1.0 - t * t) * (c0 * (1.0 + 3 * 0.044715 * v * v))
    return act, slope


def after(values, *others):
    return lax.optimization_barrier((values, others))[0]


def diagonal(count):
    return lax.broadcasted_iota(jnp.int32, (count, count), 0) == lax.broadcasted_iota(
        jnp.int32, (count, count), 1
    )


def expert_body(slices, packs, cap, width, aliased):
    rows_n = packs * cap

    def body(own_ref, rows_ref, cot_ref, router_ref, *refs):
        ups, downs = refs[:slices], refs[slices : 2 * slices]
        refs = refs[2 * slices + (1 if aliased else 0) :]
        (out_ref, copies_ref, rows_all, grads_all, act_all, pre_all) = refs[:6]
        up_v, down_v, grad_rows, acc_out, acc_copies, sems = refs[6:]
        i, s = pl.program_id(0), pl.program_id(1)

        def fetch(r):
            return (
                pltpu.make_async_copy(ups[r], up_v.at[r], sems.at[0, r]),
                pltpu.make_async_copy(downs[r], down_v.at[r], sems.at[1, r]),
            )

        @pl.when((i == 0) & (s == 0))
        def _():
            for r in range(slices):
                for copy in fetch(r):
                    copy.start()

        for r in range(slices):

            @pl.when((i == 0) & (s == r))
            def _():
                for copy in fetch(r):
                    copy.wait()

        @pl.when(s == 0)
        def _():
            rows = rows_ref[...].reshape(rows_n, width)
            rows_all[...] = rows
            logits = jnp.dot(rows, router_ref[...], preferred_element_type=F32)
            ordinals = lax.broadcasted_iota(jnp.int32, logits.shape, 1).astype(F32)
            eye = diagonal(cap)
            other = []
            for p in range(packs):
                line = cot_ref[p, cap - TILE :, :][TILE - 1 :, :cap].astype(F32)
                other.append(jnp.sum(jnp.where(eye, line, 0.0), 1, keepdims=True))
            other = jnp.concatenate(other, 0)
            own = own_ref[0].astype(F32)
            picks = jnp.where(ordinals == own, 1.0, 0.0) - jnp.where(ordinals == other, 1.0, 0.0)
            gate = jax.nn.sigmoid(jnp.sum(logits * picks, -1, keepdims=True))
            cot = cot_ref[...].reshape(rows_n, width).astype(F32)
            low = (gate * cot).astype(BF)
            grad_rows[...] = low
            grads_all[...] = low

        up, down = up_v[s], down_v[s]
        pre = jnp.dot(rows_ref[...].reshape(rows_n, width), up, preferred_element_type=F32)
        act_grad = jnp.dot(grad_rows[...], down, preferred_element_type=F32)
        act, slope = gelu_pair(pre)
        act = act.astype(BF)
        act_all[...] = act
        pre_grad = (act_grad * slope).astype(BF)
        pre_all[...] = pre_grad
        along = (((1,), (1,)), ((), ()))
        out = lax.dot_general(act, down, along, preferred_element_type=F32)
        copies = lax.dot_general(pre_grad, up, along, preferred_element_type=F32)

        @pl.when(s == 0)
        def _():
            acc_out[...] = out
            acc_copies[...] = copies

        @pl.when(s > 0)
        def _():
            acc_out[...] += out
            acc_copies[...] += copies

        @pl.when(s == slices - 1)
        def _():
            low = acc_out[...].astype(BF)
            out_ref[...] = low.reshape(packs, cap, width)
            copies_ref[...] = acc_copies[...].astype(BF).reshape(packs, cap, width)
            cot = cot_ref[...].reshape(rows_n, width).astype(F32)
            gate_grad = jnp.sum(cot * low.astype(F32), -1, keepdims=True)
            eye = diagonal(cap)
            index = lax.broadcasted_iota(jnp.int32, (TILE, width), 0)
            for p in range(packs):
                column = gate_grad[p * cap : (p + 1) * cap]
                line = jnp.sum(jnp.where(eye, column, 0.0), 0, keepdims=True)
                line = jnp.concatenate([line, jnp.zeros((1, width - cap), F32)], 1)
                coarse = line.astype(BF).astype(F32)
                tail = copies_ref[p, cap - TILE :, :].astype(F32)
                tail = jnp.where(index == TILE - 1, coarse, tail)
                tail = jnp.where(index == TILE - 2, line - coarse, tail)
                copies_ref[p, cap - TILE :, :] = tail.astype(BF)

    return body


def run_expert(own, rows, row_part, cots, cot_part, router, ups, downs, held, m, micro_count):
    blocks, width = rows.shape[0], rows.shape[2]
    cap = cots.shape[1] // (cot_part + 1)
    slices = len(ups)
    hidden = ups[0].shape[1]
    packs = max(p for p in range(1, blocks + 1) if blocks % p == 0 and p * cap <= 448)
    steps = blocks // packs
    total = blocks * cap
    aliased = held is not None
    rows_n = packs * cap

    def block(part):
        return pl.BlockSpec((packs, cap, width), lambda i, s: (i, part, 0))

    any_spec = pl.BlockSpec(memory_space=pl.ANY)
    whole_rows = pl.BlockSpec((rows_n, width), lambda i, s: (i, 0))
    whole_hidden = pl.BlockSpec((rows_n, hidden), lambda i, s: (i, s))
    inputs = [own, rows, cots, router, *ups, *downs]
    in_specs = [
        pl.BlockSpec(memory_space=pltpu.SMEM),
        block(row_part),
        block(cot_part),
        pl.BlockSpec(router.shape, lambda i, s: (0, 0)),
    ] + [any_spec] * (2 * slices)
    aliases = {}
    if aliased:
        aliases = {len(inputs): 0}
        inputs.append(held)
        in_specs.append(any_spec)
    return pl.pallas_call(
        expert_body(slices, packs, cap, width, aliased),
        grid=(steps, slices),
        in_specs=in_specs,
        out_specs=[block(m), block(0), whole_rows, whole_rows, whole_hidden, whole_hidden],
        out_shape=[
            jax.ShapeDtypeStruct((blocks, micro_count * cap, width), BF),
            jax.ShapeDtypeStruct((blocks, cap, width), BF),
            jax.ShapeDtypeStruct((total, width), BF),
            jax.ShapeDtypeStruct((total, width), BF),
            jax.ShapeDtypeStruct((total, slices * hidden), BF),
            jax.ShapeDtypeStruct((total, slices * hidden), BF),
        ],
        scratch_shapes=[
            pltpu.VMEM((slices,) + ups[0].shape, BF),
            pltpu.VMEM((slices,) + downs[0].shape, BF),
            pltpu.VMEM((rows_n, width), BF),
            pltpu.VMEM((rows_n, width), F32),
            pltpu.VMEM((rows_n, width), F32),
            pltpu.SemaphoreType.DMA((2, slices)),
        ],
        input_output_aliases=aliases,
        compiler_params=pltpu.CompilerParams(vmem_limit_bytes=48 * 1024 * 1024),
        cost_estimate=CHEAP,
        name="expert",
    )(*inputs)


CHEAP = pl.CostEstimate(flops=1, bytes_accessed=1, transcendentals=0)
ALONG = (((1,), (1,)), ((), ()))
DOWN = (((0,), (0,)), ((), ()))


def mm(left, right, dims=None):
    if dims is None:
        return jnp.dot(left, right, preferred_element_type=F32)
    return lax.dot_general(left, right, dims, preferred_element_type=F32)


def windows(total_rows):
    for q0 in range(0, total_rows, BLOCK):
        q1 = min(q0 + BLOCK, total_rows)
        yield q0, q1, max(0, (q0 - LONGEST + 1) // 128 * 128)


def visible(info, info_t, q0, q1, k0):
    shape = (q1 - k0, q1 - q0)
    key_pos = lax.broadcasted_iota(jnp.int32, shape, 0) + k0
    query_pos = lax.broadcasted_iota(jnp.int32, shape, 1) + q0
    same_doc = info_t[k0:q1, 0:1] == info[0:1, q0:q1]
    is_real = (info_t[k0:q1, 1:2] == 1.0) | (query_pos == key_pos)
    return (key_pos <= query_pos) & same_doc & is_real


def attend_forward_body(
    tokens_ref, info_ref, gain_ref, bias_ref, qkv_w_ref, out_w_ref,
    term_ref, attn_in_ref, qkv_ref, heads_ref, log_ref,
):
    total_rows = tokens_ref.shape[0]
    local = qkv_w_ref.shape[2]
    info = info_ref[...]
    info_t = info.T
    normed, _ = normalize(tokens_ref[...].astype(F32))
    attn_in = (normed * gain_ref[...] + bias_ref[...]).astype(BF)
    attn_in_ref[...] = attn_in
    for c in range(3):
        qkv_ref[c] = mm(attn_in, qkv_w_ref[c]).astype(BF)
    for q0, q1, k0 in windows(total_rows):
        allowed = visible(info, info_t, q0, q1, k0)
        for h in range(local // HEAD_DIM):
            part = slice(h * HEAD_DIM, (h + 1) * HEAD_DIM)
            scores = mm(qkv_ref[1, k0:q1, part], qkv_ref[0, q0:q1, part], ALONG)
            scores = jnp.where(allowed, scores * HEAD_DIM**-0.5, MASKED)
            peak = jnp.max(scores, 0, keepdims=True)
            exponent = jnp.exp(scores - peak)
            total = jnp.sum(exponent, 0, keepdims=True)
            weights = (exponent * (1.0 / total)).astype(BF)
            output = mm(qkv_ref[2, k0:q1, part], weights, DOWN)
            heads_ref[q0:q1, part] = output.T.astype(BF)
            log_ref[h : h + 1, q0:q1] = peak + jnp.log(total)
    perm = jnp.where(info_t[:, 3:4] == info[2:3, :], 1.0, 0.0).astype(BF)
    arranged = mm(perm, heads_ref[...]).astype(BF)
    term_ref[...] = mm(arranged, out_w_ref[...]).astype(BF)


def attend_forward(tokens, info, gain, bias, qkv_weight, out_weight):
    total_rows, width = tokens.shape
    local = out_weight.shape[0]
    shape = jax.ShapeDtypeStruct
    return pl.pallas_call(
        attend_forward_body,
        out_shape=[
            shape((total_rows, width), BF),
            shape((total_rows, width), BF),
            shape((3, total_rows, local), BF),
            shape((total_rows, local), BF),
            shape((8, total_rows), F32),
        ],
        compiler_params=pltpu.CompilerParams(vmem_limit_bytes=40 * 1024 * 1024),
        cost_estimate=CHEAP,
        name="attend_forward",
    )(tokens, info, gain[None], bias[None], qkv_weight, out_weight)


def attend_backward_body(adds):
    def body(resid_ref, info_ref, attn_in_ref, qkv_ref, heads_ref, log_ref, qkv_w_ref, out_w_ref, *refs):
        if adds:
            earlier_ref, refs = refs[0], refs[1:]
        term_ref, resid_out, sums_ref, grads, key_sum, value_sum = refs
        total_rows = resid_ref.shape[0]
        local = out_w_ref.shape[0]
        scale = HEAD_DIM**-0.5
        info = info_ref[...]
        info_t = info.T
        unperm = jnp.where(info_t[:, 2:3] == info[4:5, :], 1.0, 0.0).astype(BF)
        resid = mm(unperm, resid_ref[...]).astype(BF)
        resid_out[...] = resid
        heads_grad = mm(resid, out_w_ref[...], ALONG).astype(BF)
        key_sum[...] = jnp.zeros(key_sum.shape, F32)
        value_sum[...] = jnp.zeros(value_sum.shape, F32)
        for q0, q1, k0 in windows(total_rows):
            allowed = visible(info, info_t, q0, q1, k0)
            for h in range(local // HEAD_DIM):
                part = slice(h * HEAD_DIM, (h + 1) * HEAD_DIM)
                query, key = qkv_ref[0, q0:q1, part], qkv_ref[1, k0:q1, part]
                value, out_grad = qkv_ref[2, k0:q1, part], heads_grad[q0:q1, part]
                scores = mm(key, query, ALONG) * scale
                scores = jnp.where(allowed, scores, MASKED)
                weights = jnp.exp(scores - log_ref[h : h + 1, q0:q1])
                weight_grad = mm(value, out_grad, ALONG)
                delta = jnp.sum(weights * weight_grad, 0, keepdims=True)
                score_grad = (weights * (weight_grad - delta)).astype(BF)
                grads[0, q0:q1, part] = (scale * mm(key, score_grad, DOWN)).T.astype(BF)
                key_sum[h, k0:q1] += mm(score_grad, query)
                value_sum[h, k0:q1] += mm(weights.astype(BF), out_grad)
        for h in range(local // HEAD_DIM):
            part = slice(h * HEAD_DIM, (h + 1) * HEAD_DIM)
            grads[1, :, part] = (scale * key_sum[h]).astype(BF)
            grads[2, :, part] = value_sum[h].astype(BF)
        term = mm(grads[0], qkv_w_ref[0], ALONG)
        for c in (1, 2):
            term = term + mm(grads[c], qkv_w_ref[c], ALONG)
        term_ref[...] = term.astype(BF)
        attn_in = attn_in_ref[...]
        for c in range(4):
            rows = slice(c * local, (c + 1) * local)
            if c < 3:
                found = mm(grads[c], attn_in, DOWN)
            else:
                found = mm(heads_ref[...], resid, DOWN)
            if adds:
                found = found + earlier_ref[rows, :]
            sums_ref[rows, :] = found.astype(sums_ref.dtype)

    return body


def attend_backward(resid, info, saved, qkv_weight, out_weight, earlier, last):
    attn_in, qkv, heads, log_total = saved
    total_rows, width = resid.shape
    local = out_weight.shape[0]
    shape = jax.ShapeDtypeStruct
    inputs = [resid, info, attn_in, qkv, heads, log_total, qkv_weight, out_weight]
    if earlier is not None:
        inputs.append(earlier)
    return pl.pallas_call(
        attend_backward_body(earlier is not None),
        out_shape=[
            shape((total_rows, width), BF),
            shape((total_rows, width), BF),
            shape((4 * local, width), BF if last else F32),
        ],
        scratch_shapes=[
            pltpu.VMEM((3, total_rows, local), BF),
            pltpu.VMEM((local // HEAD_DIM, total_rows, HEAD_DIM), F32),
            pltpu.VMEM((local // HEAD_DIM, total_rows, HEAD_DIM), F32),
        ],
        compiler_params=pltpu.CompilerParams(vmem_limit_bytes=48 * 1024 * 1024),
        cost_estimate=CHEAP,
        name="attend_backward",
    )(*inputs)


def make_shards(ne, nh):
    def to_experts(blocks):
        return lax.all_to_all(blocks, "expert", split_axis=0, concat_axis=0, tiled=True)

    def reduce_quarters(rows):
        blocks = rows.reshape(nh, -1, rows.shape[-1])
        bit = 1
        while bit < nh:
            keep = [r for r in range(blocks.shape[0]) if r % 2 == 0]
            send = [r for r in range(blocks.shape[0]) if r % 2 == 1]
            got = swap(jnp.concatenate([blocks[r] for r in send], 0), "hidden", bit)
            blocks = (
                jnp.stack([blocks[r] for r in keep]).astype(F32)
                + got.reshape(len(keep), -1, rows.shape[-1]).astype(F32)
            ).astype(BF)
            bit *= 2
        return blocks[0]

    def gather_quarters(rows):
        bit = nh // 2
        while bit >= 1:
            rows = jnp.concatenate([rows, swap(rows, "hidden", bit)], 0)
            bit //= 2
        return rows

    def quarter_order():
        order = [0]
        bit = nh // 2
        while bit >= 1:
            order = order + [r ^ bit for r in order]
            bit //= 2
        return order

    def sum_hidden(rows):
        h = lax.axis_index("hidden")
        count = rows.shape[0] // 2
        flag = h % 2
        kept = lax.dynamic_slice_in_dim(rows, flag * count, count, 0)
        sent = lax.dynamic_slice_in_dim(rows, (1 - flag) * count, count, 0)
        kept = (kept.astype(F32) + swap(sent, "hidden", 1).astype(F32)).astype(BF)
        bit = 2
        while bit < nh:
            kept = (kept.astype(F32) + swap(kept, "hidden", bit).astype(F32)).astype(BF)
            bit *= 2
        return ordered(flag, kept, swap(kept, "hidden", 1))

    def shards(
        tokens,
        doc_ids,
        pad_mask,
        norm1_gain,
        norm1_bias,
        qkv_weight,
        out_weight,
        norm2_gain,
        norm2_bias,
        router,
        routes,
        up_weight,
        down_weight,
        cotangent,
    ):
        micro_count, row_count, width = tokens.shape
        expert_count = router.shape[1]
        top_count = routes.shape[2]
        pack_cap = 2 * row_count * top_count // expert_count
        quarter = row_count // nh
        cap = round_up((pack_cap + (nh - 1) * (expert_count - 1)) // nh + 2, TILE)
        order = quarter_order()
        e_idx = lax.axis_index("expert")
        h_idx = lax.axis_index("hidden")
        micros = range(micro_count)

        slice_order = quarter_order()
        far = nh // 2
        up_far = swap(up_weight[0], "hidden", far)

        def spread(mine, got):
            parts = [mine, got]
            bit = far // 2
            while bit >= 1:
                parts = parts + [swap(x, "hidden", bit) for x in parts]
                bit //= 2
            return [parts[slice_order.index(r)] for r in range(nh)]

        def route(m):
            low = jnp.min(routes[m], -1)
            high = jnp.max(routes[m], -1)
            key = (low * expert_count + high) * row_count + jnp.arange(row_count, dtype=jnp.int32)
            rank = jnp.sum((key[:, None] < key[None, :]).astype(jnp.int32), 0)
            targets = jnp.concatenate(
                [jnp.arange(quarter, dtype=jnp.int32) * nh + (h_idx ^ r) for r in range(nh)]
            )
            perm = (targets[:, None] == rank[None, :]).astype(BF)
            mine = jnp.dot(perm[:quarter], routes[m].astype(BF), preferred_element_type=F32)
            first, second = mine[:, 0], mine[:, 1]
            names = jnp.arange(expert_count, dtype=F32)[:, None]
            member = (first[None, :] == names) | (second[None, :] == names)
            before = (jnp.arange(quarter)[:, None] < jnp.arange(quarter)[None, :]).astype(BF)
            place = jnp.dot(member.astype(BF), before, preferred_element_type=F32)
            slot = jnp.arange(cap, dtype=F32)[None, :, None]
            table = ((slot == place[:, None, :]) & member[:, None, :]).astype(BF)
            others = (first + second)[None, :] - names
            deal = jnp.concatenate(
                [jnp.arange(quarter, dtype=jnp.int32) * nh + (h_idx ^ r) for r in order]
            )
            blank = jnp.zeros((row_count,), jnp.int32)
            info = [doc_ids[m, 0], pad_mask[m], rank, targets, deal, blank, blank, blank]
            return perm, table, member, others, jnp.stack(info).astype(F32)

        def dispatch(table, rows):
            return jnp.einsum("ejt,td->ejd", table, rows, preferred_element_type=F32).astype(BF)

        def dispatch_upstream(m, perm, table, others):
            up_rows = jnp.dot(perm[:quarter], cotangent[m], preferred_element_type=F32)
            other = jnp.sum(table.astype(F32) * others[:, None, :], -1)
            other = jnp.pad(other[:, None, :], ((0, 0), (0, 0), (0, width - cap)))
            sent = jnp.einsum("ejt,td->ejd", table, up_rows.astype(BF), preferred_element_type=F32)
            last = (jnp.arange(cap) == cap - 1)[None, :, None]
            return up_rows, jnp.where(last, other, sent).astype(BF)

        perms, tables, upstream_mine = [], [], []
        state = []
        for m in micros:
            if m == 0:
                perm, table, member, others, info = route(m)
                up_rows, up_sent = dispatch_upstream(m, perm, table, others)
                upstream_slots = to_experts(up_sent)
                earlier = up_sent
            else:
                perm, table, member, others, info = following
                up_rows, up_sent = dispatch_upstream(m, perm, table, others)
                earlier = last_sent
            perms.append(perm)
            tables.append(table)
            upstream_mine.append(up_rows)
            mine_tokens = after(tokens[m], earlier)
            term, *saved = attend_forward(
                mine_tokens, info, norm1_gain, norm1_bias, qkv_weight, out_weight
            )
            if m == 0:
                term, up_far = after((term, up_far), up_far)
                down_mine = after(down_weight[0], term)
                down_far = swap(down_mine, "hidden", far)
                ups = spread(up_weight[0], up_far)
            elif m == micro_count - 1:
                term, down_far = after((term, down_far), down_far)
                downs = spread(down_weight[0], down_far)
            attention = reduce_quarters(term).astype(F32)
            inputs_mine = jnp.dot(perm[:quarter], mine_tokens, preferred_element_type=F32)
            residual = inputs_mine + attention
            normed2, scale2 = normalize(residual)
            moe_in = (normed2 * norm2_gain + norm2_bias).astype(BF)
            logits = jnp.dot(moe_in, router, preferred_element_type=F32).T
            masked = jnp.where(member, logits, MASKED)
            raised = jnp.where(member, jnp.exp(masked - jnp.max(masked, 0, keepdims=True)), 0.0)
            gates = raised / jnp.sum(raised, 0, keepdims=True)
            if m + 1 < micro_count:
                following = route(m + 1)
                moe_in, following = after((moe_in, following), following)
            last_sent = dispatch(table, moe_in)
            if m == 0:
                received = (to_experts(last_sent), 0, upstream_slots, 0)
            else:
                both = to_experts(jnp.concatenate([last_sent, up_sent], 1))
                received = (both, 0, both, 1)
            state.append(
                dict(
                    saved=saved,
                    info=info,
                    attention=attention,
                    normed2=normed2,
                    scale2=scale2,
                    moe_in=moe_in,
                    gates=gates,
                    received=received,
                )
            )

        own_expert = jnp.full((1,), e_idx, jnp.int32)
        held, slabs = None, None
        for m in micros:
            s = state[m]
            rows, row_part, cots, cot_part = s["received"]
            if m == 0:
                rows = after(rows, last_sent)
            else:
                rows = after(rows, slabs)
                cots = rows
            held, copies, rows_all, grads_all, act_all, pre_all = run_expert(
                own_expert,
                rows,
                row_part,
                cots,
                cot_part,
                router,
                ups,
                downs,
                held,
                m,
                micro_count,
            )
            s["copies_back"] = to_experts(copies)
            made = []
            for left, right in ((rows_all, pre_all), (grads_all, act_all)):
                hidden = right.shape[1] // nh
                for r in range(nh):
                    slab = jnp.einsum(
                        "rd,rf->df",
                        left,
                        right[:, r * hidden : (r + 1) * hidden],
                        preferred_element_type=F32,
                    )
                    if slabs is not None:
                        slab = slab + slabs[len(made)].astype(F32)
                    made.append(slab.astype(BF))
            slabs = made

        owned = []
        for part in (slabs[:nh], slabs[nh:]):
            bit = 1
            while bit < nh:
                got = [swap(slab, "hidden", bit) for slab in part[1::2]]
                part = [
                    (mine.astype(F32) + other.astype(F32)).astype(BF)
                    for mine, other in zip(part[0::2], got)
                ]
                bit *= 2
            owned.append(part[0].reshape(ne, width // ne, -1))
        owned = jnp.concatenate(owned, 1)

        order = quarter_order()
        grad_router = 0.0
        gain2_total, bias2_total = 0.0, 0.0
        previous = slabs
        for m in micros:
            s = state[m]
            back = s["copies_back"] = after(s["copies_back"], previous)
            table = tables[m]
            copies_sum = jnp.einsum("ejt,ejd->td", table, back, preferred_element_type=F32)
            slot_grad = back[:, cap - 1, :cap].astype(F32) + back[:, cap - 2, :cap].astype(F32)
            gate_grad = jnp.sum(table.astype(F32) * slot_grad[:, :, None], 1)
            gates = s["gates"]
            logit_grad = gates * (gate_grad - jnp.sum(gates * gate_grad, 0, keepdims=True))
            normed2_grad = copies_sum + jnp.einsum(
                "et,de->td", logit_grad, router.astype(F32), precision=PRECISE
            )
            grad_router = grad_router + jnp.einsum(
                "et,td->ed", logit_grad, s["moe_in"].astype(F32), precision=PRECISE
            )
            gain2_total = gain2_total + jnp.sum(normed2_grad * s["normed2"], 0)
            bias2_total = bias2_total + jnp.sum(normed2_grad, 0)
            resid_grad = upstream_mine[m] + normalize_pull(
                s["normed2"], s["scale2"], norm2_gain, normed2_grad
            )
            s["resid_all"] = gather_quarters(resid_grad.astype(BF))
            previous = s["resid_all"]

        small = jnp.concatenate([gain2_total[None], bias2_total[None], grad_router], 0)
        small_rows = round_up(small.shape[0], 16)
        small = jnp.pad(small, ((0, small_rows - small.shape[0]), (0, 0))).astype(BF)

        pack_sums = None
        gain1_total, bias1_total = 0.0, 0.0
        input_grads = []
        out_back = to_experts(after(held, state[-1]["copies_back"]))
        for m in micros:
            s = state[m]
            term, resid, pack_sums = attend_backward(
                s["resid_all"],
                s["info"],
                s["saved"],
                qkv_weight,
                out_weight,
                pack_sums,
                m == micro_count - 1,
            )
            if m == micro_count - 1:
                total = sum_hidden(jnp.concatenate([term, small], 0))
                small_sum = total[row_count:]
                normed1_grad = total[:row_count].astype(F32)
            else:
                normed1_grad = sum_hidden(term).astype(F32)
            normed1, scale1 = normalize(tokens[m].astype(F32))
            gain1_total = gain1_total + jnp.sum(normed1_grad * normed1, 0)
            bias1_total = bias1_total + jnp.sum(normed1_grad, 0)
            input_grads.append(
                resid.astype(F32) + normalize_pull(normed1, scale1, norm1_gain, normed1_grad)
            )
            if m == micro_count - 1:
                out_back, _ = after((out_back, term), term)

        parts = to_experts(after(owned, out_back))[ne // 2 :].astype(F32)

        share = pack_sums.reshape(ne, -1, width)
        bit = 1
        while bit < ne:
            flag = (e_idx // bit) % 2
            pairs = share.reshape(share.shape[0] // 2, 2, -1, width)
            kept = lax.dynamic_index_in_dim(pairs, flag, 1, False)
            sent = lax.dynamic_index_in_dim(pairs, 1 - flag, 1, False)
            share = (kept.astype(F32) + swap(sent, "expert", bit).astype(F32)).astype(BF)
            bit *= 2
        share = share[0]
        share_rows = share.shape[0]
        extra = jnp.concatenate([gain1_total[None], bias1_total[None]], 0).astype(BF)
        extra = jnp.concatenate([extra, small_sum], 0)
        extra = jnp.pad(extra, ((0, round_up(extra.shape[0], 16) - extra.shape[0]), (0, 0)))
        gathered = jnp.concatenate([share, extra], 0)[None]
        bit = ne // 2
        while bit >= 1:
            gathered = jnp.concatenate([gathered, swap(gathered, "expert", bit)], 0)
            bit //= 2
        bits = []
        bit = ne // 2
        found = [0]
        while bit >= 1:
            found = found + [r ^ bit for r in found]
            bit //= 2
        outputs = []
        for m in micros:
            s = state[m]
            weighted = (tables[m].astype(F32) * s["gates"][:, None, :]).astype(BF)
            mixture = jnp.einsum(
                "ejt,ejd->td",
                weighted,
                out_back[:, m * cap : (m + 1) * cap],
                preferred_element_type=F32,
            )
            delta_all = gather_quarters((s["attention"] + mixture).astype(BF))
            perm = perms[m].reshape(nh, quarter, row_count)
            perm = jnp.concatenate([perm[r] for r in order], 0)
            delta = jnp.einsum("rt,rd->td", perm, delta_all, preferred_element_type=F32)
            outputs.append(tokens[m].astype(F32) + delta)
        sums = jnp.sum(gathered[:, share_rows:].astype(F32), 0)
        where = jnp.zeros((ne,), jnp.int32)
        slots = jnp.array([found.index(r) for r in range(ne)], jnp.int32)
        where = slots[jnp.arange(ne, dtype=jnp.int32) ^ e_idx]
        flat = gathered[:, :share_rows][where].astype(F32).reshape(4, -1, width)
        return (
            jnp.stack(outputs),
            jnp.stack(input_grads),
            sums[0],
            sums[1],
            flat[:3].transpose(0, 2, 1),
            flat[3],
            sums[2],
            sums[3],
            sums[4 : 4 + expert_count].T,
            parts[:, : width // ne],
            parts[:, width // ne :],
        )

    return shards


def solution(mesh):
    placed = (
        P(None, "expert", None),
        P(None, "expert", None),
        P(None, "expert"),
        P(),
        P(),
        P(None, None, "hidden"),
        P("hidden", None),
        P(),
        P(),
        P(),
        P(None, "expert", None),
        P("expert", None, "hidden"),
        P("expert", None, "hidden"),
        P(None, "expert", None),
    )
    return jax.shard_map(
        make_shards(mesh.shape["expert"], mesh.shape["hidden"]),
        mesh=mesh,
        in_specs=placed,
        out_specs=(
            P(None, "expert", None),
            P(None, "expert", None),
            P(),
            P(),
            P(None, None, "hidden"),
            P("hidden", None),
            P(),
            P(),
            P(),
            P(None, "expert", "hidden"),
            P(None, "expert", "hidden"),
        ),
        check_vma=False,
    )
```

```python
import jax
import jax.numpy as jnp
from jax import lax
from jax.experimental import pallas as pl
from jax.experimental.pallas import tpu as pltpu
from jax.sharding import PartitionSpec as P

HEAD_DIM = 64
EPSILON = 1e-05
PRECISE = lax.Precision.HIGHEST
MASKED = -1e30
TILE = 16
LONGEST = 384
BLOCK = 256
BF = jnp.bfloat16
F32 = jnp.float32


def round_up(value, step):
    return -(-value // step) * step


def swap(values, axis, bit):
    size = lax.axis_size(axis)
    return lax.ppermute(values, axis, [(i, i ^ bit) for i in range(size)])


def normalize(values):
    centre = values - jnp.mean(values, -1, keepdims=True)
    spread = jnp.mean(centre * centre, -1, keepdims=True)
    scale = lax.rsqrt(spread + EPSILON)
    return centre * scale, scale


def normalize_pull(normed, scale, gain, grad):
    wide = grad * gain
    return scale * (
        wide
        - jnp.mean(wide, -1, keepdims=True)
        - normed * jnp.mean(wide * normed, -1, keepdims=True)
    )


def gelu_pair(v):
    c0 = 0.7978845608028654
    inner = c0 * (v + 0.044715 * v * v * v)
    t = jnp.tanh(inner)
    act = 0.5 * v * (1.0 + t)
    slope = 0.5 * (1.0 + t) + 0.5 * v * (1.0 - t * t) * (c0 * (1.0 + 3 * 0.044715 * v * v))
    return act, slope


def after(values, *others):
    return lax.optimization_barrier((values, others))[0]


def diagonal(count):
    return lax.broadcasted_iota(jnp.int32, (count, count), 0) == lax.broadcasted_iota(
        jnp.int32, (count, count), 1
    )


def expert_body(slices, packs, cap, width, aliased):
    rows_n = packs * cap

    def body(own_ref, rows_ref, cot_ref, router_ref, *refs):
        ups, downs = refs[:2]
        refs = refs[2 + (1 if aliased else 0) :]
        (out_ref, copies_ref, rows_all, grads_all, act_all, pre_all) = refs[:6]
        up_v, down_v, grad_rows, acc_out, acc_copies, sems = refs[6:]
        i, s = pl.program_id(0), pl.program_id(1)

        def fetch(r):
            return (
                pltpu.make_async_copy(ups.at[own_ref[1] ^ r], up_v.at[r], sems.at[0, r]),
                pltpu.make_async_copy(downs.at[own_ref[1] ^ r], down_v.at[r], sems.at[1, r]),
            )

        @pl.when((i == 0) & (s == 0))
        def _():
            for r in range(slices):
                for copy in fetch(r):
                    copy.start()

        for r in range(slices):

            @pl.when((i == 0) & (s == r))
            def _():
                for copy in fetch(r):
                    copy.wait()

        @pl.when(s == 0)
        def _():
            rows = rows_ref[...].reshape(rows_n, width)
            rows_all[...] = rows
            logits = mm(rows, router_ref[...], ALONG)
            ordinals = lax.broadcasted_iota(jnp.int32, logits.shape, 1).astype(F32)
            eye = diagonal(cap)
            other = []
            for p in range(packs):
                line = cot_ref[p, cap - TILE :, :][TILE - 1 :, :cap].astype(F32)
                other.append(jnp.sum(jnp.where(eye, line, 0.0), 1, keepdims=True))
            other = jnp.concatenate(other, 0)
            own = own_ref[0].astype(F32)
            picks = jnp.where(ordinals == own, 1.0, 0.0) - jnp.where(ordinals == other, 1.0, 0.0)
            gate = jax.nn.sigmoid(jnp.sum(logits * picks, -1, keepdims=True))
            cot = cot_ref[...].reshape(rows_n, width).astype(F32)
            low = (gate * cot).astype(BF)
            grad_rows[...] = low
            grads_all[...] = low

        up, down = up_v[s], down_v[s]
        pre = jnp.dot(rows_ref[...].reshape(rows_n, width), up, preferred_element_type=F32)
        act_grad = jnp.dot(grad_rows[...], down, preferred_element_type=F32)
        act, slope = gelu_pair(pre)
        act = act.astype(BF)
        act_all[...] = act
        pre_grad = (act_grad * slope).astype(BF)
        pre_all[...] = pre_grad
        along = (((1,), (1,)), ((), ()))
        out = lax.dot_general(act, down, along, preferred_element_type=F32)
        copies = lax.dot_general(pre_grad, up, along, preferred_element_type=F32)

        @pl.when(s == 0)
        def _():
            acc_out[...] = out
            acc_copies[...] = copies

        @pl.when(s > 0)
        def _():
            acc_out[...] += out
            acc_copies[...] += copies

        @pl.when(s == slices - 1)
        def _():
            low = acc_out[...].astype(BF)
            out_ref[...] = low.reshape(packs, cap, width)
            copies_ref[...] = acc_copies[...].astype(BF).reshape(packs, cap, width)
            cot = cot_ref[...].reshape(rows_n, width).astype(F32)
            gate_grad = jnp.sum(cot * low.astype(F32), -1, keepdims=True)
            eye = diagonal(cap)
            index = lax.broadcasted_iota(jnp.int32, (TILE, width), 0)
            for p in range(packs):
                column = gate_grad[p * cap : (p + 1) * cap]
                line = jnp.sum(jnp.where(eye, column, 0.0), 0, keepdims=True)
                line = jnp.concatenate([line, jnp.zeros((1, width - cap), F32)], 1)
                coarse = line.astype(BF).astype(F32)
                tail = copies_ref[p, cap - TILE :, :].astype(F32)
                tail = jnp.where(index == TILE - 1, coarse, tail)
                tail = jnp.where(index == TILE - 2, line - coarse, tail)
                copies_ref[p, cap - TILE :, :] = tail.astype(BF)

    return body


def run_expert(own, rows, row_part, cots, cot_part, router, ups, downs, held, m, micro_count):
    blocks, width = rows.shape[0], rows.shape[2]
    cap = cots.shape[1] // (cot_part + 1)
    slices, _, hidden = ups.shape
    packs = max(p for p in range(1, blocks + 1) if blocks % p == 0 and p * cap <= 448)
    steps = blocks // packs
    total = blocks * cap
    aliased = held is not None
    rows_n = packs * cap

    def block(part):
        return pl.BlockSpec((packs, cap, width), lambda i, s: (i, part, 0))

    any_spec = pl.BlockSpec(memory_space=pl.ANY)
    whole_rows = pl.BlockSpec((rows_n, width), lambda i, s: (i, 0))
    whole_hidden = pl.BlockSpec((rows_n, hidden), lambda i, s: (i, s))
    inputs = [own, rows, cots, router, ups, downs]
    in_specs = [
        pl.BlockSpec(memory_space=pltpu.SMEM),
        block(row_part),
        block(cot_part),
        pl.BlockSpec(router.shape, lambda i, s: (0, 0)),
    ] + [any_spec] * 2
    aliases = {}
    if aliased:
        aliases = {len(inputs): 0}
        inputs.append(held)
        in_specs.append(any_spec)
    return pl.pallas_call(
        expert_body(slices, packs, cap, width, aliased),
        grid=(steps, slices),
        in_specs=in_specs,
        out_specs=[block(m), block(0), whole_rows, whole_rows, whole_hidden, whole_hidden],
        out_shape=[
            jax.ShapeDtypeStruct((blocks, micro_count * cap, width), BF),
            jax.ShapeDtypeStruct((blocks, cap, width), BF),
            jax.ShapeDtypeStruct((total, width), BF),
            jax.ShapeDtypeStruct((total, width), BF),
            jax.ShapeDtypeStruct((total, slices * hidden), BF),
            jax.ShapeDtypeStruct((total, slices * hidden), BF),
        ],
        scratch_shapes=[
            pltpu.VMEM(ups.shape, BF),
            pltpu.VMEM(downs.shape, BF),
            pltpu.VMEM((rows_n, width), BF),
            pltpu.VMEM((rows_n, width), F32),
            pltpu.VMEM((rows_n, width), F32),
            pltpu.SemaphoreType.DMA((2, slices)),
        ],
        input_output_aliases=aliases,
        compiler_params=pltpu.CompilerParams(vmem_limit_bytes=48 * 1024 * 1024),
        cost_estimate=CHEAP,
        name="expert",
    )(*inputs)


CHEAP = pl.CostEstimate(flops=1, bytes_accessed=1, transcendentals=0)
ALONG = (((1,), (1,)), ((), ()))
DOWN = (((0,), (0,)), ((), ()))


def mm(left, right, dims=None):
    if dims is None:
        return jnp.dot(left, right, preferred_element_type=F32)
    return lax.dot_general(left, right, dims, preferred_element_type=F32)


def windows(total_rows):
    for q0 in range(0, total_rows, BLOCK):
        q1 = min(q0 + BLOCK, total_rows)
        yield q0, q1, max(0, (q0 - LONGEST + 1) // 128 * 128)


def visible(info, info_t, q0, q1, k0):
    shape = (q1 - k0, q1 - q0)
    key_pos = lax.broadcasted_iota(jnp.int32, shape, 0) + k0
    query_pos = lax.broadcasted_iota(jnp.int32, shape, 1) + q0
    same_doc = info_t[k0:q1, 0:1] == info[0:1, q0:q1]
    is_real = (info_t[k0:q1, 1:2] == 1.0) | (query_pos == key_pos)
    return (key_pos <= query_pos) & same_doc & is_real


def attend_forward_body(
    tokens_ref, info_ref, gain_ref, bias_ref, qkv_w_ref, out_w_ref,
    keep_ref, send_ref, attn_in_ref, qkv_ref, heads_ref, log_ref,
):
    total_rows = tokens_ref.shape[1]
    local = qkv_w_ref.shape[1]
    info = info_ref[...]
    info_t = info.T
    normed, _ = normalize(tokens_ref[0].astype(F32))
    attn_in = (normed * gain_ref[...] + bias_ref[...]).astype(BF)
    attn_in_ref[...] = attn_in
    for c in range(3):
        qkv_ref[c] = mm(attn_in, qkv_w_ref[c], ALONG).astype(BF)
    for q0, q1, k0 in windows(total_rows):
        allowed = visible(info, info_t, q0, q1, k0)
        for h in range(local // HEAD_DIM):
            part = slice(h * HEAD_DIM, (h + 1) * HEAD_DIM)
            scores = mm(qkv_ref[1, k0:q1, part], qkv_ref[0, q0:q1, part], ALONG)
            scores = jnp.where(allowed, scores * HEAD_DIM**-0.5, MASKED)
            peak = jnp.max(scores, 0, keepdims=True)
            exponent = jnp.exp(scores - peak)
            total = jnp.sum(exponent, 0, keepdims=True)
            weights = (exponent * (1.0 / total)).astype(BF)
            output = mm(qkv_ref[2, k0:q1, part], weights, DOWN)
            heads_ref[q0:q1, part] = output.T.astype(BF)
            log_ref[h : h + 1, q0:q1] = peak + jnp.log(total)
    perm = jnp.where(info_t[:, 3:4] == info[2:3, :], 1.0, 0.0).astype(BF)
    arranged = mm(perm, heads_ref[...]).astype(BF)
    term = mm(arranged, out_w_ref[...]).astype(BF)
    keep_ref[...] = term[: total_rows // 2]
    send_ref[...] = term[total_rows // 2 :]


def attend_forward(m, tokens, info, gain, bias, qkv_weight, out_weight):
    total_rows, width = tokens.shape[1:]
    local = out_weight.shape[0]
    shape = jax.ShapeDtypeStruct
    inputs = [tokens, info, gain[None], bias[None], qkv_weight, out_weight]
    out_shape = [
        shape((total_rows // 2, width), BF),
        shape((total_rows // 2, width), BF),
        shape((total_rows, width), BF),
        shape((3, total_rows, local), BF),
        shape((total_rows, local), BF),
        shape((8, total_rows), F32),
    ]
    return kernel(
        attend_forward_body,
        out_shape,
        "attend_forward",
        grid=(1,),
        in_specs=[picked(x, m) if k == 0 else whole(x.shape) for k, x in enumerate(inputs)],
        out_specs=[whole(x.shape) for x in out_shape],
    )(*inputs)


def attend_backward_body(adds, count):
    def body(*refs):
        blocks, refs = refs[:count], refs[count:]
        info_ref, attn_in_ref, qkv_ref, heads_ref, log_ref, qkv_w_ref, out_w_ref = refs[:7]
        refs = refs[7:]
        if adds:
            earlier_ref, refs = refs[0], refs[1:]
        term_ref, resid_out, sums_ref, grads, key_sum, value_sum = refs
        total_rows = attn_in_ref.shape[0]
        local = out_w_ref.shape[0]
        scale = HEAD_DIM**-0.5
        info = info_ref[...]
        info_t = info.T
        unperm = jnp.where(info_t[:, 2:3] == info[3:4, :], 1.0, 0.0).astype(BF)
        resid = jnp.concatenate([block[...] for block in blocks], 0)
        resid = mm(unperm, resid).astype(BF)
        resid_out[...] = resid
        heads_grad = mm(resid, out_w_ref[...], ALONG).astype(BF)
        key_sum[...] = jnp.zeros(key_sum.shape, F32)
        value_sum[...] = jnp.zeros(value_sum.shape, F32)
        for q0, q1, k0 in windows(total_rows):
            allowed = visible(info, info_t, q0, q1, k0)
            for h in range(local // HEAD_DIM):
                part = slice(h * HEAD_DIM, (h + 1) * HEAD_DIM)
                query, key = qkv_ref[0, q0:q1, part], qkv_ref[1, k0:q1, part]
                value, out_grad = qkv_ref[2, k0:q1, part], heads_grad[q0:q1, part]
                scores = mm(key, query, ALONG) * scale
                scores = jnp.where(allowed, scores, MASKED)
                weights = jnp.exp(scores - log_ref[h : h + 1, q0:q1])
                weight_grad = mm(value, out_grad, ALONG)
                delta = jnp.sum(weights * weight_grad, 0, keepdims=True)
                score_grad = (weights * (weight_grad - delta)).astype(BF)
                grads[0, q0:q1, part] = (scale * mm(key, score_grad, DOWN)).T.astype(BF)
                key_sum[h, k0:q1] += mm(score_grad, query)
                value_sum[h, k0:q1] += mm(weights.astype(BF), out_grad)
        for h in range(local // HEAD_DIM):
            part = slice(h * HEAD_DIM, (h + 1) * HEAD_DIM)
            grads[1, :, part] = (scale * key_sum[h]).astype(BF)
            grads[2, :, part] = value_sum[h].astype(BF)
        term = mm(grads[0], qkv_w_ref[0])
        for c in (1, 2):
            term = term + mm(grads[c], qkv_w_ref[c])
        term_ref[...] = term.astype(BF)
        attn_in = attn_in_ref[...]
        for c in range(4):
            rows = slice(c * local, (c + 1) * local)
            if c < 3:
                found = mm(grads[c], attn_in, DOWN)
            else:
                found = mm(heads_ref[...], resid, DOWN)
            if adds:
                found = found + earlier_ref[rows, :]
            sums_ref[rows, :] = found.astype(sums_ref.dtype)

    return body


def attend_backward(blocks, info, saved, qkv_weight, out_weight, earlier, last):
    attn_in, qkv, heads, log_total = saved
    total_rows, width = attn_in.shape
    local = out_weight.shape[0]
    shape = jax.ShapeDtypeStruct
    inputs = [*blocks, info, attn_in, qkv, heads, log_total, qkv_weight, out_weight]
    if earlier is not None:
        inputs.append(earlier)
    return pl.pallas_call(
        attend_backward_body(earlier is not None, len(blocks)),
        out_shape=[
            shape((total_rows, width), BF),
            shape((total_rows, width), BF),
            shape((4 * local, width), BF if last else F32),
        ],
        scratch_shapes=[
            pltpu.VMEM((3, total_rows, local), BF),
            pltpu.VMEM((local // HEAD_DIM, total_rows, HEAD_DIM), F32),
            pltpu.VMEM((local // HEAD_DIM, total_rows, HEAD_DIM), F32),
        ],
        compiler_params=pltpu.CompilerParams(vmem_limit_bytes=48 * 1024 * 1024),
        cost_estimate=CHEAP,
        name="attend_backward",
    )(*inputs)


def chosen(info, info_t, count):
    return jnp.where(info_t[:count, 3:4] == info[2:3, :], 1.0, 0.0).astype(BF)


def kernel(body, out_shape, name, mebibytes=40, **options):
    return pl.pallas_call(
        body,
        out_shape=out_shape,
        compiler_params=pltpu.CompilerParams(vmem_limit_bytes=mebibytes * 1024 * 1024),
        cost_estimate=CHEAP,
        name=name,
        **options,
    )


def route_body(m, order):
    def body(hid_ref, doc_ref, pad_ref, routes_ref, cot_ref, *outs):
        route_pack(m, order, hid_ref, doc_ref, pad_ref, routes_ref, cot_ref, *outs)

    return body


def route_pack(m, order, hid_ref, doc_ref, pad_ref, routes_ref, cot_ref, info_out, member_ref, table_ref, rows_ref, sent_ref):
    experts, cap, quarter = table_ref.shape
    total_rows, width = cot_ref.shape[1:]
    dealt = lax.broadcasted_iota(jnp.int32, (1, quarter), 1) * len(order)
    deal = jnp.concatenate([dealt + (hid_ref[0] ^ r) for r in order], 1).astype(F32)
    info = jnp.zeros(info_out.shape, F32)
    line = lax.broadcasted_iota(jnp.int32, info.shape, 0)
    routes = routes_ref[m].astype(F32)
    known = (doc_ref[m].astype(F32), pad_ref[m : m + 1, :].astype(F32), None, deal, routes[:1], routes[1:])
    for k, row in enumerate(known):
        if row is not None:
            info = jnp.where(line == k, row, info)
    low = jnp.minimum(info[4:5], info[5:6])
    high = jnp.maximum(info[4:5], info[5:6])
    place = lax.broadcasted_iota(jnp.int32, (1, total_rows), 1).astype(F32)
    key = (low * experts + high) * total_rows + place
    key_t = jnp.where(line == 6, key, info).T
    rank = jnp.sum(jnp.where(key_t[:, 6:7] < key, 1.0, 0.0), 0, keepdims=True)
    info = jnp.where(line == 2, rank, info)
    info_out[...] = info
    perm = chosen(info, info.T, quarter)
    mine = mm(info.astype(BF), perm, ALONG)
    first, second = mine[4:5], mine[5:6]
    names = lax.broadcasted_iota(jnp.int32, (experts, quarter), 0).astype(F32)
    member = jnp.where((first == names) | (second == names), 1.0, 0.0)
    member_ref[...] = member
    shape = (quarter, quarter)
    before = lax.broadcasted_iota(jnp.int32, shape, 0) < lax.broadcasted_iota(jnp.int32, shape, 1)
    place = mm(member.astype(BF), jnp.where(before, 1.0, 0.0).astype(BF))
    rows = mm(perm, cot_ref[0]).astype(BF)
    rows_ref[...] = rows
    slot = lax.broadcasted_iota(jnp.int32, (cap, quarter), 0).astype(F32)
    last = lax.broadcasted_iota(jnp.int32, (cap, width), 0) == cap - 1
    for e in range(experts):
        match = (slot == place[e : e + 1]) & (member[e : e + 1] > 0.5)
        table = jnp.where(match, 1.0, 0.0).astype(BF)
        table_ref[e] = table
        others = jnp.broadcast_to(first + second - e, (8, quarter)).astype(BF)
        other = mm(others, table, ALONG)[:1]
        other = jnp.concatenate([other, jnp.zeros((1, width - cap), F32)], 1)
        sent_ref[e] = jnp.where(last, other, mm(table, rows)).astype(BF)


def whole(shape):
    return pl.BlockSpec(shape, lambda i: (0,) * len(shape))


def picked(values, m):
    return pl.BlockSpec((1,) + values.shape[1:], lambda i: (m, 0, 0))


def route_tokens(m, hid, doc_ids, pad_mask, routes, cotangent, experts, cap, order):
    total_rows, width = cotangent.shape[1:]
    quarter = total_rows // len(order)
    out_shape = [
        jax.ShapeDtypeStruct((8, total_rows), F32),
        jax.ShapeDtypeStruct((experts, quarter), F32),
        jax.ShapeDtypeStruct((experts, cap, quarter), BF),
        jax.ShapeDtypeStruct((quarter, width), BF),
        jax.ShapeDtypeStruct((experts, cap, width), BF),
    ]
    return kernel(
        route_body(m, order),
        out_shape,
        "route",
        grid=(1,),
        in_specs=[
            pl.BlockSpec(memory_space=pltpu.SMEM),
            whole(doc_ids.shape),
            whole(pad_mask.shape),
            whole(routes.shape),
            picked(cotangent, m),
        ],
        out_specs=[whole(x.shape) for x in out_shape],
    )(hid, doc_ids, pad_mask, routes, cotangent)


def middle_body(joined):
    def body(mine_ref, got_ref, tokens_ref, info_ref, member_ref, table_ref, gain_ref, bias_ref, router_ref, *refs):
        if joined:
            cots_ref, refs = refs[0], refs[1:]
        sent_ref, moe_ref, attention_ref, residual_ref, gates_ref = refs
        experts, cap, quarter = table_ref.shape
        info = info_ref[...]
        perm = chosen(info, info.T, quarter)
        attention = mine_ref[...].astype(F32) + got_ref[...].astype(F32)
        attention_ref[...] = attention.astype(BF)
        residual = mm(perm, tokens_ref[0]) + attention
        residual_ref[...] = residual
        normed, _ = normalize(residual)
        moe_in = (normed * gain_ref[...] + bias_ref[...]).astype(BF)
        moe_ref[...] = moe_in
        logits = mm(router_ref[...], moe_in, ALONG)
        member = member_ref[...] > 0.5
        masked = jnp.where(member, logits, MASKED)
        raised = jnp.where(member, jnp.exp(masked - jnp.max(masked, 0, keepdims=True)), 0.0)
        gates_ref[...] = raised / jnp.sum(raised, 0, keepdims=True)
        for e in range(experts):
            sent_ref[e, :cap] = mm(table_ref[e], moe_in).astype(BF)
            if joined:
                sent_ref[e, cap:] = cots_ref[e]

    return body


def middle(m, mine, got, tokens, info, member, table, gain, bias, router_t, cots):
    experts, cap, quarter = table.shape
    width = tokens.shape[2]
    shape = jax.ShapeDtypeStruct
    inputs = [mine, got, tokens, info, member, table, gain[None], bias[None], router_t]
    if cots is not None:
        inputs.append(cots)
    out_shape = [
        shape((experts, cap if cots is None else 2 * cap, width), BF),
        shape((quarter, width), BF),
        shape((quarter, width), BF),
        shape((quarter, width), F32),
        shape((experts, quarter), F32),
    ]
    return kernel(
        middle_body(cots is not None),
        out_shape,
        "middle",
        grid=(1,),
        in_specs=[picked(x, m) if k == 2 else whole(x.shape) for k, x in enumerate(inputs)],
        out_specs=[whole(x.shape) for x in out_shape],
    )(*inputs)


def token_back_body(adds):
    def body(back_ref, table_ref, gates_ref, router_ref, moe_ref, residual_ref, rows_ref, gain_ref, *refs):
        if adds:
            earlier_ref, refs = refs[0], refs[1:]
        grad_ref, small_ref = refs
        experts, cap, quarter = table_ref.shape
        width = moe_ref.shape[1]
        table = table_ref[...].reshape(experts * cap, quarter)
        copies = mm(table, back_ref[...].reshape(experts * cap, width), DOWN)
        lines = []
        for e in range(experts):
            both = mm(back_ref[e, cap - TILE :, :][:, :cap], table_ref[e])
            lines.append(both[TILE - 2 : TILE - 1] + both[TILE - 1 :])
        gate_grad = jnp.concatenate(lines, 0)
        gates = gates_ref[...]
        logit_grad = gates * (gate_grad - jnp.sum(gates * gate_grad, 0, keepdims=True))
        coarse = logit_grad.astype(BF)
        fine = (logit_grad - coarse.astype(F32)).astype(BF)
        router = router_ref[...]
        normed2_grad = copies + mm(coarse, router, DOWN) + mm(fine, router, DOWN)
        normed, scale = normalize(residual_ref[...])
        grad_router = mm(coarse, moe_ref[...]) + mm(fine, moe_ref[...])
        small = [
            jnp.sum(normed2_grad * normed, 0, keepdims=True),
            jnp.sum(normed2_grad, 0, keepdims=True),
            grad_router,
        ]
        spare = small_ref.shape[0] - 2 - experts
        small = jnp.concatenate(small + [jnp.zeros((spare, width), F32)], 0)
        if adds:
            small = small + earlier_ref[...]
        small_ref[...] = small.astype(small_ref.dtype)
        pull = normalize_pull(normed, scale, gain_ref[...], normed2_grad)
        grad_ref[...] = (rows_ref[...].astype(F32) + pull).astype(BF)

    return body


def token_back(back, table, gates, router_t, moe_in, residual, rows, gain, earlier, last):
    quarter, width = moe_in.shape
    small_rows = round_up(2 + table.shape[0], 2 * TILE)
    shape = jax.ShapeDtypeStruct
    inputs = [back, table, gates, router_t, moe_in, residual, rows, gain[None]]
    if earlier is not None:
        inputs.append(earlier)
    out_shape = [shape((quarter, width), BF), shape((small_rows, width), BF if last else F32)]
    return kernel(token_back_body(earlier is not None), out_shape, "token_back")(*inputs)


def weight_body(count, hidden):
    def body(*refs):
        lefts, rights = refs[:count], refs[count : 2 * count]
        outs, turned = refs[2 * count : 2 * count + 2], refs[-1]

        @pl.when(pl.program_id(0) == 0)
        def _():
            for m in range(count):
                turned[m] = lefts[m][...].T

        for k in range(2):
            part = slice(k * hidden, (k + 1) * hidden)
            found = mm(turned[0], rights[0][:, part])
            for m in range(1, count):
                found = found + mm(turned[m], rights[m][:, part])
            outs[k][0] = found.astype(BF)

    return body


def weight_grad(lefts, rights, slices):
    total, width = lefts[0].shape
    hidden = rights[0].shape[1] // slices
    count = len(lefts)
    pair = pl.BlockSpec((1, width, hidden), lambda p: (p, 0, 0))
    return kernel(
        weight_body(count, hidden),
        [jax.ShapeDtypeStruct((slices // 2, width, hidden), BF)] * 2,
        "weight_grad",
        56,
        grid=(slices // 2,),
        in_specs=[pl.BlockSpec((total, width), lambda p: (0, 0))] * count
        + [pl.BlockSpec((total, 2 * hidden), lambda p: (0, p))] * count,
        out_specs=[pair, pair],
        scratch_shapes=[pltpu.VMEM((count, width, total), BF)],
    )(*lefts, *rights)


def mix_body(back_ref, table_ref, gates_ref, attention_ref, delta_ref):
    experts, cap, quarter = table_ref.shape
    width = back_ref.shape[2]
    weighted = []
    for e in range(experts):
        weighted.append((table_ref[e].astype(F32) * gates_ref[e : e + 1, :]).astype(BF))
    weighted = jnp.concatenate(weighted, 0)
    mixture = mm(weighted, back_ref[...].reshape(experts * cap, width), DOWN)
    delta_ref[...] = (attention_ref[...].astype(F32) + mixture).astype(BF)


def mix(back, part, table, gates, attention):
    experts, cap, quarter = table.shape
    width = attention.shape[1]
    return kernel(
        mix_body,
        jax.ShapeDtypeStruct((quarter, width), BF),
        "mix",
        grid=(1,),
        in_specs=[
            pl.BlockSpec((experts, cap, width), lambda i: (0, part, 0)),
            pl.BlockSpec((experts, cap, quarter), lambda i: (0, 0, 0)),
            pl.BlockSpec((experts, quarter), lambda i: (0, 0)),
            pl.BlockSpec((quarter, width), lambda i: (0, 0)),
        ],
        out_specs=pl.BlockSpec((quarter, width), lambda i: (0, 0)),
    )(back, table, gates, attention)


def output_body(count):
    def body(*refs):
        blocks, (tokens_ref, info_ref) = refs[:count], refs[count : count + 2]
        out_ref = refs[-1]
        info = info_ref[...]
        info_t = info.T
        unperm = jnp.where(info_t[:, 2:3] == info[3:4, :], 1.0, 0.0).astype(BF)
        delta = jnp.concatenate([block[...] for block in blocks], 0)
        out_ref[0] = tokens_ref[0].astype(F32) + mm(unperm, delta)

    return body


def place_rows(inputs, body, name, held, m, micro_count, more_out=(), smem=0):
    total_rows, width = held[1]
    first = pl.BlockSpec((1, total_rows, width), lambda i: (m, 0, 0))

    in_specs = [picked(x, m) if x.ndim == 3 else whole(x.shape) for x in inputs]
    in_specs[:smem] = [pl.BlockSpec(memory_space=pltpu.SMEM)] * smem
    aliases = {}
    inputs = list(inputs)
    if held[0] is not None:
        aliases = {len(inputs): 0}
        inputs.append(held[0])
        in_specs.append(pl.BlockSpec(memory_space=pl.ANY))
    return kernel(
        body,
        [jax.ShapeDtypeStruct((micro_count, total_rows, width), F32)] + list(more_out),
        name,
        grid=(1,),
        in_specs=in_specs,
        out_specs=[first] + [whole(x.shape) for x in more_out],
        input_output_aliases=aliases,
    )(*inputs)


def input_grad_body(total_rows, half):
    def body(flag_ref, mine_ref, other_ref, tokens_ref, resid_ref, gain_ref, *refs):
        grad_ref, sums_ref = refs[-2:]
        mine, other = mine_ref[...].astype(F32), other_ref[...].astype(F32)
        zero = flag_ref[0] == 0
        low = jnp.where(zero, mine, other)
        high = jnp.where(zero, other, mine)
        grad = jnp.concatenate([low, high], 0)[:total_rows]
        normed, scale = normalize(tokens_ref[0].astype(F32))
        sums = [jnp.sum(grad * normed, 0, keepdims=True), jnp.sum(grad, 0, keepdims=True)]
        sums_ref[...] = jnp.concatenate(sums + [jnp.zeros((6, grad.shape[1]), F32)], 0)
        grad_ref[0] = resid_ref[...].astype(F32) + normalize_pull(normed, scale, gain_ref[...], grad)

    return body


def make_shards(ne, nh):
    def to_experts(blocks):
        return lax.all_to_all(blocks, "expert", split_axis=0, concat_axis=0, tiled=True)

    def reduce_quarters(keep, send):
        bit = 1
        while bit < nh // 2:
            got = swap(send, "hidden", bit)
            half = keep.shape[0] // 2
            send = (keep[half:].astype(F32) + got[half:].astype(F32)).astype(BF)
            keep = (keep[:half].astype(F32) + got[:half].astype(F32)).astype(BF)
            bit *= 2
        return keep, swap(send, "hidden", bit)

    def gather_quarters(rows):
        blocks = [rows]
        bit = nh // 2
        while bit >= 1:
            blocks = blocks + [swap(block, "hidden", bit) for block in blocks]
            bit //= 2
        return blocks

    def quarter_order():
        order = [0]
        bit = nh // 2
        while bit >= 1:
            order = order + [r ^ bit for r in order]
            bit //= 2
        return order

    def sum_hidden(rows):
        h = lax.axis_index("hidden")
        count = rows.shape[0] // 2
        flag = h % 2
        kept = lax.dynamic_slice_in_dim(rows, flag * count, count, 0)
        sent = lax.dynamic_slice_in_dim(rows, (1 - flag) * count, count, 0)
        kept = (kept.astype(F32) + swap(sent, "hidden", 1).astype(F32)).astype(BF)
        bit = 2
        while bit < nh:
            kept = (kept.astype(F32) + swap(kept, "hidden", bit).astype(F32)).astype(BF)
            bit *= 2
        return kept, swap(kept, "hidden", 1)

    def shards(
        tokens,
        doc_ids,
        pad_mask,
        norm1_gain,
        norm1_bias,
        qkv_weight,
        out_weight,
        norm2_gain,
        norm2_bias,
        router,
        routes,
        up_weight,
        down_weight,
        cotangent,
    ):
        micro_count, row_count, width = tokens.shape
        expert_count = router.shape[1]
        top_count = routes.shape[2]
        pack_cap = 2 * row_count * top_count // expert_count
        quarter = row_count // nh
        cap = round_up((pack_cap + (nh - 1) * (expert_count - 1)) // nh + 2, TILE)
        order = quarter_order()
        e_idx = lax.axis_index("expert")
        h_idx = lax.axis_index("hidden")
        micros = range(micro_count)

        ups = lax.all_gather(up_weight[0], "hidden")
        downs = lax.all_gather(down_weight[0], "hidden")

        router_t = router.T
        hid = jnp.full((1,), h_idx, jnp.int32)
        routes_t = routes.transpose(0, 2, 1)
        qkv_t = qkv_weight.transpose(0, 2, 1)

        def route(m):
            return route_tokens(
                m, hid, doc_ids, pad_mask, routes_t, cotangent, expert_count, cap, order
            )

        state = []
        for m in micros:
            if m == 0:
                info, member, table, up_rows, up_sent = route(m)
                upstream_slots = to_experts(up_sent)
                earlier = up_sent
            else:
                info, member, table, up_rows, up_sent = following
                earlier = last_sent
            mine_tokens = after(tokens, earlier)
            keep, send, *saved = attend_forward(
                m, mine_tokens, info, norm1_gain, norm1_bias, qkv_t, out_weight
            )
            mine, got = reduce_quarters(keep, send)
            if m + 1 < micro_count:
                following = route(m + 1)
                got, following = after((got, following), following)
            last_sent, moe_in, attention, residual, gates = middle(
                m,
                mine,
                got,
                mine_tokens,
                info,
                member,
                table,
                norm2_gain,
                norm2_bias,
                router_t,
                None if m == 0 else up_sent,
            )
            if m == micro_count - 1:
                last_sent, ups, downs = after((last_sent, ups, downs), (ups, downs))
            if m == 0:
                received = (to_experts(last_sent), 0, upstream_slots, 0)
            else:
                both = to_experts(last_sent)
                received = (both, 0, both, 1)
            state.append(
                dict(
                    saved=saved,
                    info=info,
                    attention=attention,
                    residual=residual,
                    moe_in=moe_in,
                    gates=gates,
                    table=table,
                    up_rows=up_rows,
                    received=received,
                )
            )

        own_expert = jnp.stack([e_idx, h_idx]).astype(jnp.int32)
        held, works = None, []
        for m in micros:
            s = state[m]
            rows, row_part, cots, cot_part = s["received"]
            if m == 0:
                rows = after(rows, last_sent)
            held, copies, *work = run_expert(
                own_expert,
                rows,
                row_part,
                cots,
                cot_part,
                router_t,
                ups,
                downs,
                held,
                m,
                micro_count,
            )
            s["copies_back"] = to_experts(copies)
            works.append(work)
        small = None
        copies_back = [s["copies_back"] for s in state]
        copies_back[:-1], works = after((copies_back[:-1], works), copies)
        for m in micros:
            s = state[m]
            last = m == micro_count - 1
            if m == 1:
                works = after(works, grad_low)
                first = weight_grad([work[0] for work in works], [work[3] for work in works], nh)
                works, state[0]["resid_all"] = after(
                    (works, state[0]["resid_all"]), (first, state[0]["resid_all"])
                )
                slabs = (
                    first,
                    weight_grad([work[1] for work in works], [work[2] for work in works], nh),
                )
                copies_back[1:] = after(copies_back[1:], slabs)
                halves = []
                for keep, send in slabs:
                    got = swap(send, "hidden", 1)
                    halves.append(
                        [
                            (keep[p].astype(F32) + got[p].astype(F32)).astype(BF)
                            for p in range(nh // 2)
                        ]
                    )
            grad_low, small = token_back(
                copies_back[m],
                s["table"],
                s["gates"],
                router_t,
                s["moe_in"],
                s["residual"],
                s["up_rows"],
                norm2_gain,
                small,
                last,
            )
            s["resid_all"] = gather_quarters(grad_low)

        firsts = halves
        gathers = [s["resid_all"] for s in state]

        def finish(part):
            bit = 2
            while bit < nh:
                got = [swap(slab, "hidden", bit) for slab in part[1::2]]
                part = [
                    (mine.astype(F32) + other.astype(F32)).astype(BF)
                    for mine, other in zip(part[0::2], got)
                ]
                bit *= 2
            return part[0].reshape(ne, width // ne, -1)

        owned_up = finish(after(halves[0], gathers))

        flag = jnp.full((1,), h_idx % 2, jnp.int32)
        pack_sums = None
        input_grads, norm1_sums = None, 0.0
        out_back = to_experts(after(held, copies_back[-1]))
        terms, resids = [], []
        state[0]["resid_all"] = after(state[0]["resid_all"], (firsts, grad_low))
        for m in micros:
            s = state[m]
            term, resid, pack_sums = attend_backward(
                s["resid_all"],
                s["info"],
                s["saved"],
                qkv_t,
                out_weight,
                pack_sums,
                m == micro_count - 1,
            )
            terms.append(term)
            resids.append(resid)
        terms[:-1] = after(terms[:-1], terms[-1])
        pack_sums, owned_up = after((pack_sums, owned_up), owned_up)
        for m in micros:
            s = state[m]
            term, resid = terms[m], resids[m]
            if m == micro_count - 1:
                term_all = jnp.concatenate([term, small], 0)
            else:
                term_all = term
            mine, other = sum_hidden(term_all)
            input_grads, sums = place_rows(
                [flag, mine, other, tokens, resid, norm1_gain[None]],
                input_grad_body(row_count, mine.shape[0]),
                "input_grad",
                (input_grads, tokens.shape[1:]),
                m,
                micro_count,
                [jax.ShapeDtypeStruct((8, width), F32)],
                1,
            )
            norm1_sums = norm1_sums + sums

        owned = jnp.concatenate([owned_up, finish(after(halves[1], (mine, other)))], 1)

        share = pack_sums.reshape(ne, -1, width)
        bit = 1
        while bit < ne:
            side = (e_idx // bit) % 2
            if bit == 2:
                share, out_back = after((share, out_back), out_back)
            pairs = share.reshape(share.shape[0] // 2, 2, -1, width)
            kept = lax.dynamic_index_in_dim(pairs, side, 1, False)
            sent = lax.dynamic_index_in_dim(pairs, 1 - side, 1, False)
            share = (kept.astype(F32) + swap(sent, "expert", bit).astype(F32)).astype(BF)
            bit *= 2
        share = share[0]

        half = small.shape[0]
        kept = term_all.shape[0] // 2
        small = jnp.where(flag == 0, other[kept - half :], mine[kept - half :]).astype(F32)
        small = jnp.concatenate([norm1_sums[:2], small[: 2 + expert_count]], 0)
        small = jnp.pad(small, ((0, round_up(small.shape[0], 8) - small.shape[0]), (0, 0)))
        bit = 1
        while bit < ne:
            small = small + swap(small, "expert", bit)
            bit *= 2
        outputs = None
        for m in micros:
            s = state[m]
            delta = mix(out_back, m, s["table"], s["gates"], s["attention"])
            blocks = gather_quarters(delta)
            (outputs,) = place_rows(
                [*blocks, tokens, s["info"]],
                output_body(len(blocks)),
                "output",
                (outputs, tokens.shape[1:]),
                m,
                micro_count,
            )
        gathered = share[None]
        bit = ne // 2
        while bit >= 1:
            if bit == 1:
                parts = to_experts(after(owned, (out_back, gathered, small)))[ne // 2 :].astype(F32)
                gathered, outputs = after((gathered, outputs), outputs)
            gathered = jnp.concatenate([gathered, swap(gathered, "expert", bit)], 0)
            bit //= 2
        bits = []
        bit = ne // 2
        found = [0]
        while bit >= 1:
            found = found + [r ^ bit for r in found]
            bit //= 2
        where = jnp.zeros((ne,), jnp.int32)
        slots = jnp.array([found.index(r) for r in range(ne)], jnp.int32)
        where = slots[jnp.arange(ne, dtype=jnp.int32) ^ e_idx]
        flat = gathered[where].astype(F32).reshape(4, -1, width)
        return (
            outputs,
            input_grads,
            small[0],
            small[1],
            flat[:3].transpose(0, 2, 1),
            flat[3],
            small[2],
            small[3],
            small[4 : 4 + expert_count].T,
            parts[:, : width // ne],
            parts[:, width // ne :],
        )

    return shards


def solution(mesh):
    placed = (
        P(None, "expert", None),
        P(None, "expert", None),
        P(None, "expert"),
        P(),
        P(),
        P(None, None, "hidden"),
        P("hidden", None),
        P(),
        P(),
        P(),
        P(None, "expert", None),
        P("expert", None, "hidden"),
        P("expert", None, "hidden"),
        P(None, "expert", None),
    )
    return jax.shard_map(
        make_shards(mesh.shape["expert"], mesh.shape["hidden"]),
        mesh=mesh,
        in_specs=placed,
        out_specs=(
            P(None, "expert", None),
            P(None, "expert", None),
            P(),
            P(),
            P(None, None, "hidden"),
            P("hidden", None),
            P(),
            P(),
            P(),
            P(None, "expert", "hidden"),
            P(None, "expert", "hidden"),
        ),
        check_vma=False,
    )
```

```python
import jax
import jax.numpy as jnp
from jax import lax
from jax.experimental import pallas as pl
from jax.experimental.pallas import tpu as pltpu
from jax.sharding import PartitionSpec as P

HEAD_DIM = 64
EPSILON = 1e-05
PRECISE = lax.Precision.HIGHEST
MASKED = -1e30
TILE = 16
LONGEST = 384
BLOCK = 256
BF = jnp.bfloat16
F32 = jnp.float32


def round_up(value, step):
    return -(-value // step) * step


def swap(values, axis, bit):
    size = lax.axis_size(axis)
    return lax.ppermute(values, axis, [(i, i ^ bit) for i in range(size)])


def normalize(values):
    centre = values - jnp.mean(values, -1, keepdims=True)
    spread = jnp.mean(centre * centre, -1, keepdims=True)
    scale = lax.rsqrt(spread + EPSILON)
    return centre * scale, scale


def normalize_pull(normed, scale, gain, grad):
    wide = grad * gain
    return scale * (
        wide
        - jnp.mean(wide, -1, keepdims=True)
        - normed * jnp.mean(wide * normed, -1, keepdims=True)
    )


def gelu_pair(v):
    c0 = 0.7978845608028654
    inner = c0 * (v + 0.044715 * v * v * v)
    t = jnp.tanh(inner)
    act = 0.5 * v * (1.0 + t)
    slope = 0.5 * (1.0 + t) + 0.5 * v * (1.0 - t * t) * (c0 * (1.0 + 3 * 0.044715 * v * v))
    return act, slope


def after(values, *others):
    return lax.optimization_barrier((values, others))[0]


def diagonal(count):
    return lax.broadcasted_iota(jnp.int32, (count, count), 0) == lax.broadcasted_iota(
        jnp.int32, (count, count), 1
    )


def expert_body(slices, packs, cap, width, aliased):
    rows_n = packs * cap

    def body(own_ref, rows_ref, cot_ref, router_ref, *refs):
        ups, downs = refs[:2]
        refs = refs[2 + (1 if aliased else 0) :]
        (out_ref, copies_ref, rows_all, grads_all, act_all, pre_all) = refs[:6]
        up_v, down_v, grad_rows, acc_out, acc_copies, sems = refs[6:]
        i, s = pl.program_id(0), pl.program_id(1)

        def fetch(r):
            return (
                pltpu.make_async_copy(ups.at[own_ref[1] ^ r], up_v.at[r], sems.at[0, r]),
                pltpu.make_async_copy(downs.at[own_ref[1] ^ r], down_v.at[r], sems.at[1, r]),
            )

        @pl.when((i == 0) & (s == 0))
        def _():
            for r in range(slices):
                for copy in fetch(r):
                    copy.start()

        for r in range(slices):

            @pl.when((i == 0) & (s == r))
            def _():
                for copy in fetch(r):
                    copy.wait()

        @pl.when(s == 0)
        def _():
            rows = rows_ref[...].reshape(rows_n, width)
            rows_all[...] = rows
            logits = mm(rows, router_ref[...], ALONG)
            ordinals = lax.broadcasted_iota(jnp.int32, logits.shape, 1).astype(F32)
            eye = diagonal(cap)
            other = []
            for p in range(packs):
                line = cot_ref[p, cap - TILE :, :][TILE - 1 :, :cap].astype(F32)
                other.append(jnp.sum(jnp.where(eye, line, 0.0), 1, keepdims=True))
            other = jnp.concatenate(other, 0)
            own = own_ref[0].astype(F32)
            picks = jnp.where(ordinals == own, 1.0, 0.0) - jnp.where(ordinals == other, 1.0, 0.0)
            gate = jax.nn.sigmoid(jnp.sum(logits * picks, -1, keepdims=True))
            cot = cot_ref[...].reshape(rows_n, width).astype(F32)
            low = (gate * cot).astype(BF)
            grad_rows[...] = low
            grads_all[...] = low

        up, down = up_v[s], down_v[s]
        pre = jnp.dot(rows_ref[...].reshape(rows_n, width), up, preferred_element_type=F32)
        act_grad = jnp.dot(grad_rows[...], down, preferred_element_type=F32)
        act, slope = gelu_pair(pre)
        act = act.astype(BF)
        act_all[...] = act
        pre_grad = (act_grad * slope).astype(BF)
        pre_all[...] = pre_grad
        along = (((1,), (1,)), ((), ()))
        out = lax.dot_general(act, down, along, preferred_element_type=F32)
        copies = lax.dot_general(pre_grad, up, along, preferred_element_type=F32)

        @pl.when(s == 0)
        def _():
            acc_out[...] = out
            acc_copies[...] = copies

        @pl.when(s > 0)
        def _():
            acc_out[...] += out
            acc_copies[...] += copies

        @pl.when(s == slices - 1)
        def _():
            low = acc_out[...].astype(BF)
            out_ref[...] = low.reshape(packs, cap, width)
            copies_ref[...] = acc_copies[...].astype(BF).reshape(packs, cap, width)
            cot = cot_ref[...].reshape(rows_n, width).astype(F32)
            gate_grad = jnp.sum(cot * low.astype(F32), -1, keepdims=True)
            eye = diagonal(cap)
            index = lax.broadcasted_iota(jnp.int32, (TILE, width), 0)
            for p in range(packs):
                column = gate_grad[p * cap : (p + 1) * cap]
                line = jnp.sum(jnp.where(eye, column, 0.0), 0, keepdims=True)
                line = jnp.concatenate([line, jnp.zeros((1, width - cap), F32)], 1)
                coarse = line.astype(BF).astype(F32)
                tail = copies_ref[p, cap - TILE :, :].astype(F32)
                tail = jnp.where(index == TILE - 1, coarse, tail)
                tail = jnp.where(index == TILE - 2, line - coarse, tail)
                copies_ref[p, cap - TILE :, :] = tail.astype(BF)

    return body


def run_expert(own, rows, row_part, cots, cot_part, router, ups, downs, held, m, micro_count):
    blocks, width = rows.shape[0], rows.shape[2]
    cap = cots.shape[1] // (cot_part + 1)
    slices, _, hidden = ups.shape
    packs = max(p for p in range(1, blocks + 1) if blocks % p == 0 and p * cap <= 448)
    steps = blocks // packs
    total = blocks * cap
    aliased = held is not None
    rows_n = packs * cap

    def block(part):
        return pl.BlockSpec((packs, cap, width), lambda i, s: (i, part, 0))

    any_spec = pl.BlockSpec(memory_space=pl.ANY)
    whole_rows = pl.BlockSpec((rows_n, width), lambda i, s: (i, 0))
    whole_hidden = pl.BlockSpec((rows_n, hidden), lambda i, s: (i, s))
    inputs = [own, rows, cots, router, ups, downs]
    in_specs = [
        pl.BlockSpec(memory_space=pltpu.SMEM),
        block(row_part),
        block(cot_part),
        pl.BlockSpec(router.shape, lambda i, s: (0, 0)),
    ] + [any_spec] * 2
    aliases = {}
    if aliased:
        aliases = {len(inputs): 0}
        inputs.append(held)
        in_specs.append(any_spec)
    return pl.pallas_call(
        expert_body(slices, packs, cap, width, aliased),
        grid=(steps, slices),
        in_specs=in_specs,
        out_specs=[block(m), block(0), whole_rows, whole_rows, whole_hidden, whole_hidden],
        out_shape=[
            jax.ShapeDtypeStruct((blocks, micro_count * cap, width), BF),
            jax.ShapeDtypeStruct((blocks, cap, width), BF),
            jax.ShapeDtypeStruct((total, width), BF),
            jax.ShapeDtypeStruct((total, width), BF),
            jax.ShapeDtypeStruct((total, slices * hidden), BF),
            jax.ShapeDtypeStruct((total, slices * hidden), BF),
        ],
        scratch_shapes=[
            pltpu.VMEM(ups.shape, BF),
            pltpu.VMEM(downs.shape, BF),
            pltpu.VMEM((rows_n, width), BF),
            pltpu.VMEM((rows_n, width), F32),
            pltpu.VMEM((rows_n, width), F32),
            pltpu.SemaphoreType.DMA((2, slices)),
        ],
        input_output_aliases=aliases,
        compiler_params=pltpu.CompilerParams(vmem_limit_bytes=48 * 1024 * 1024),
        cost_estimate=CHEAP,
        name="expert",
    )(*inputs)


CHEAP = pl.CostEstimate(flops=1, bytes_accessed=1, transcendentals=0)
ALONG = (((1,), (1,)), ((), ()))
DOWN = (((0,), (0,)), ((), ()))


def mm(left, right, dims=None):
    if dims is None:
        return jnp.dot(left, right, preferred_element_type=F32)
    return lax.dot_general(left, right, dims, preferred_element_type=F32)


def windows(total_rows):
    for q0 in range(0, total_rows, BLOCK):
        q1 = min(q0 + BLOCK, total_rows)
        yield q0, q1, max(0, (q0 - LONGEST + 1) // 128 * 128)


def visible(info, info_t, q0, q1, k0):
    shape = (q1 - k0, q1 - q0)
    key_pos = lax.broadcasted_iota(jnp.int32, shape, 0) + k0
    query_pos = lax.broadcasted_iota(jnp.int32, shape, 1) + q0
    same_doc = info_t[k0:q1, 0:1] == info[0:1, q0:q1]
    is_real = (info_t[k0:q1, 1:2] == 1.0) | (query_pos == key_pos)
    return (key_pos <= query_pos) & same_doc & is_real


def attend_forward_body(
    tokens_ref, info_ref, gain_ref, bias_ref, qkv_w_ref, out_w_ref,
    keep_ref, send_ref, attn_in_ref, qkv_ref, heads_ref, log_ref,
):
    total_rows = tokens_ref.shape[1]
    local = qkv_w_ref.shape[1]
    info = info_ref[...]
    info_t = info.T
    normed, _ = normalize(tokens_ref[0].astype(F32))
    attn_in = (normed * gain_ref[...] + bias_ref[...]).astype(BF)
    attn_in_ref[...] = attn_in
    for c in range(3):
        qkv_ref[c] = mm(attn_in, qkv_w_ref[c], ALONG).astype(BF)
    for q0, q1, k0 in windows(total_rows):
        allowed = visible(info, info_t, q0, q1, k0)
        for h in range(local // HEAD_DIM):
            part = slice(h * HEAD_DIM, (h + 1) * HEAD_DIM)
            scores = mm(qkv_ref[1, k0:q1, part], qkv_ref[0, q0:q1, part], ALONG)
            scores = jnp.where(allowed, scores * HEAD_DIM**-0.5, MASKED)
            peak = jnp.max(scores, 0, keepdims=True)
            exponent = jnp.exp(scores - peak)
            total = jnp.sum(exponent, 0, keepdims=True)
            weights = (exponent * (1.0 / total)).astype(BF)
            output = mm(qkv_ref[2, k0:q1, part], weights, DOWN)
            heads_ref[q0:q1, part] = output.T.astype(BF)
            log_ref[h : h + 1, q0:q1] = peak + jnp.log(total)
    perm = jnp.where(info_t[:, 3:4] == info[2:3, :], 1.0, 0.0).astype(BF)
    arranged = mm(perm, heads_ref[...]).astype(BF)
    term = mm(arranged, out_w_ref[...]).astype(BF)
    keep_ref[...] = term[: total_rows // 2]
    send_ref[...] = term[total_rows // 2 :]


def attend_forward(m, tokens, info, gain, bias, qkv_weight, out_weight):
    total_rows, width = tokens.shape[1:]
    local = out_weight.shape[0]
    shape = jax.ShapeDtypeStruct
    inputs = [tokens, info, gain[None], bias[None], qkv_weight, out_weight]
    out_shape = [
        shape((total_rows // 2, width), BF),
        shape((total_rows // 2, width), BF),
        shape((total_rows, width), BF),
        shape((3, total_rows, local), BF),
        shape((total_rows, local), BF),
        shape((8, total_rows), F32),
    ]
    return kernel(
        attend_forward_body,
        out_shape,
        "attend_forward",
        grid=(1,),
        in_specs=[picked(x, m) if k == 0 else whole(x.shape) for k, x in enumerate(inputs)],
        out_specs=[whole(x.shape) for x in out_shape],
    )(*inputs)


def attend_backward_body(adds, count):
    def body(*refs):
        blocks, refs = refs[:count], refs[count:]
        info_ref, attn_in_ref, qkv_ref, heads_ref, log_ref, qkv_w_ref, out_w_ref = refs[:7]
        refs = refs[7:]
        if adds:
            earlier_ref, refs = refs[0], refs[1:]
        term_ref, resid_out, sums_ref, grads, key_sum, value_sum = refs
        total_rows = attn_in_ref.shape[0]
        local = out_w_ref.shape[0]
        scale = HEAD_DIM**-0.5
        info = info_ref[...]
        info_t = info.T
        unperm = jnp.where(info_t[:, 2:3] == info[3:4, :], 1.0, 0.0).astype(BF)
        resid = jnp.concatenate([block[...] for block in blocks], 0)
        resid = mm(unperm, resid).astype(BF)
        resid_out[...] = resid
        heads_grad = mm(resid, out_w_ref[...], ALONG).astype(BF)
        key_sum[...] = jnp.zeros(key_sum.shape, F32)
        value_sum[...] = jnp.zeros(value_sum.shape, F32)
        for q0, q1, k0 in windows(total_rows):
            allowed = visible(info, info_t, q0, q1, k0)
            for h in range(local // HEAD_DIM):
                part = slice(h * HEAD_DIM, (h + 1) * HEAD_DIM)
                query, key = qkv_ref[0, q0:q1, part], qkv_ref[1, k0:q1, part]
                value, out_grad = qkv_ref[2, k0:q1, part], heads_grad[q0:q1, part]
                scores = mm(key, query, ALONG) * scale
                scores = jnp.where(allowed, scores, MASKED)
                weights = jnp.exp(scores - log_ref[h : h + 1, q0:q1])
                weight_grad = mm(value, out_grad, ALONG)
                delta = jnp.sum(weights * weight_grad, 0, keepdims=True)
                score_grad = (weights * (weight_grad - delta)).astype(BF)
                grads[0, q0:q1, part] = (scale * mm(key, score_grad, DOWN)).T.astype(BF)
                key_sum[h, k0:q1] += mm(score_grad, query)
                value_sum[h, k0:q1] += mm(weights.astype(BF), out_grad)
        for h in range(local // HEAD_DIM):
            part = slice(h * HEAD_DIM, (h + 1) * HEAD_DIM)
            grads[1, :, part] = (scale * key_sum[h]).astype(BF)
            grads[2, :, part] = value_sum[h].astype(BF)
        term = mm(grads[0], qkv_w_ref[0])
        for c in (1, 2):
            term = term + mm(grads[c], qkv_w_ref[c])
        term_ref[...] = term.astype(BF)
        attn_in = attn_in_ref[...]
        for c in range(4):
            rows = slice(c * local, (c + 1) * local)
            if c < 3:
                found = mm(grads[c], attn_in, DOWN)
            else:
                found = mm(heads_ref[...], resid, DOWN)
            if adds:
                found = found + earlier_ref[rows, :]
            sums_ref[rows, :] = found.astype(sums_ref.dtype)

    return body


def attend_backward(blocks, info, saved, qkv_weight, out_weight, earlier, last):
    attn_in, qkv, heads, log_total = saved
    total_rows, width = attn_in.shape
    local = out_weight.shape[0]
    shape = jax.ShapeDtypeStruct
    inputs = [*blocks, info, attn_in, qkv, heads, log_total, qkv_weight, out_weight]
    if earlier is not None:
        inputs.append(earlier)
    return pl.pallas_call(
        attend_backward_body(earlier is not None, len(blocks)),
        out_shape=[
            shape((total_rows, width), BF),
            shape((total_rows, width), BF),
            shape((4 * local, width), BF if last else F32),
        ],
        scratch_shapes=[
            pltpu.VMEM((3, total_rows, local), BF),
            pltpu.VMEM((local // HEAD_DIM, total_rows, HEAD_DIM), F32),
            pltpu.VMEM((local // HEAD_DIM, total_rows, HEAD_DIM), F32),
        ],
        compiler_params=pltpu.CompilerParams(vmem_limit_bytes=48 * 1024 * 1024),
        cost_estimate=CHEAP,
        name="attend_backward",
    )(*inputs)


def chosen(info, info_t, count):
    return jnp.where(info_t[:count, 3:4] == info[2:3, :], 1.0, 0.0).astype(BF)


def kernel(body, out_shape, name, mebibytes=40, **options):
    return pl.pallas_call(
        body,
        out_shape=out_shape,
        compiler_params=pltpu.CompilerParams(vmem_limit_bytes=mebibytes * 1024 * 1024),
        cost_estimate=CHEAP,
        name=name,
        **options,
    )


def route_body(m, order):
    def body(hid_ref, doc_ref, pad_ref, routes_ref, cot_ref, *outs):
        route_pack(m, order, hid_ref, doc_ref, pad_ref, routes_ref, cot_ref, *outs)

    return body


def route_pack(m, order, hid_ref, doc_ref, pad_ref, routes_ref, cot_ref, info_out, member_ref, table_ref, rows_ref, sent_ref):
    experts, cap, quarter = table_ref.shape
    total_rows, width = cot_ref.shape[1:]
    dealt = lax.broadcasted_iota(jnp.int32, (1, quarter), 1) * len(order)
    deal = jnp.concatenate([dealt + (hid_ref[0] ^ r) for r in order], 1).astype(F32)
    info = jnp.zeros(info_out.shape, F32)
    line = lax.broadcasted_iota(jnp.int32, info.shape, 0)
    routes = routes_ref[m].astype(F32)
    known = (doc_ref[m].astype(F32), pad_ref[m : m + 1, :].astype(F32), None, deal, routes[:1], routes[1:])
    for k, row in enumerate(known):
        if row is not None:
            info = jnp.where(line == k, row, info)
    low = jnp.minimum(info[4:5], info[5:6])
    high = jnp.maximum(info[4:5], info[5:6])
    place = lax.broadcasted_iota(jnp.int32, (1, total_rows), 1).astype(F32)
    key = (low * experts + high) * total_rows + place
    key_t = jnp.where(line == 6, key, info).T
    rank = jnp.sum(jnp.where(key_t[:, 6:7] < key, 1.0, 0.0), 0, keepdims=True)
    info = jnp.where(line == 2, rank, info)
    info_out[...] = info
    perm = chosen(info, info.T, quarter)
    mine = mm(info.astype(BF), perm, ALONG)
    first, second = mine[4:5], mine[5:6]
    names = lax.broadcasted_iota(jnp.int32, (experts, quarter), 0).astype(F32)
    member = jnp.where((first == names) | (second == names), 1.0, 0.0)
    member_ref[...] = member
    shape = (quarter, quarter)
    before = lax.broadcasted_iota(jnp.int32, shape, 0) < lax.broadcasted_iota(jnp.int32, shape, 1)
    place = mm(member.astype(BF), jnp.where(before, 1.0, 0.0).astype(BF))
    rows = mm(perm, cot_ref[0]).astype(BF)
    rows_ref[...] = rows
    slot = lax.broadcasted_iota(jnp.int32, (cap, quarter), 0).astype(F32)
    last = lax.broadcasted_iota(jnp.int32, (cap, width), 0) == cap - 1
    for e in range(experts):
        match = (slot == place[e : e + 1]) & (member[e : e + 1] > 0.5)
        table = jnp.where(match, 1.0, 0.0).astype(BF)
        table_ref[e] = table
        others = jnp.broadcast_to(first + second - e, (8, quarter)).astype(BF)
        other = mm(others, table, ALONG)[:1]
        other = jnp.concatenate([other, jnp.zeros((1, width - cap), F32)], 1)
        sent_ref[e] = jnp.where(last, other, mm(table, rows)).astype(BF)


def whole(shape):
    return pl.BlockSpec(shape, lambda i: (0,) * len(shape))


def picked(values, m):
    return pl.BlockSpec((1,) + values.shape[1:], lambda i: (m, 0, 0))


def route_tokens(m, hid, doc_ids, pad_mask, routes, cotangent, experts, cap, order):
    total_rows, width = cotangent.shape[1:]
    quarter = total_rows // len(order)
    out_shape = [
        jax.ShapeDtypeStruct((8, total_rows), F32),
        jax.ShapeDtypeStruct((experts, quarter), F32),
        jax.ShapeDtypeStruct((experts, cap, quarter), BF),
        jax.ShapeDtypeStruct((quarter, width), BF),
        jax.ShapeDtypeStruct((experts, cap, width), BF),
    ]
    return kernel(
        route_body(m, order),
        out_shape,
        "route",
        grid=(1,),
        in_specs=[
            pl.BlockSpec(memory_space=pltpu.SMEM),
            whole(doc_ids.shape),
            whole(pad_mask.shape),
            whole(routes.shape),
            picked(cotangent, m),
        ],
        out_specs=[whole(x.shape) for x in out_shape],
    )(hid, doc_ids, pad_mask, routes, cotangent)


def middle_body(joined):
    def body(mine_ref, got_ref, tokens_ref, info_ref, member_ref, table_ref, gain_ref, bias_ref, router_ref, *refs):
        if joined:
            cots_ref, refs = refs[0], refs[1:]
        sent_ref, moe_ref, attention_ref, residual_ref, gates_ref = refs
        experts, cap, quarter = table_ref.shape
        info = info_ref[...]
        perm = chosen(info, info.T, quarter)
        attention = mine_ref[...].astype(F32) + got_ref[...].astype(F32)
        attention_ref[...] = attention.astype(BF)
        residual = mm(perm, tokens_ref[0]) + attention
        residual_ref[...] = residual
        normed, _ = normalize(residual)
        moe_in = (normed * gain_ref[...] + bias_ref[...]).astype(BF)
        moe_ref[...] = moe_in
        logits = mm(router_ref[...], moe_in, ALONG)
        member = member_ref[...] > 0.5
        masked = jnp.where(member, logits, MASKED)
        raised = jnp.where(member, jnp.exp(masked - jnp.max(masked, 0, keepdims=True)), 0.0)
        gates_ref[...] = raised / jnp.sum(raised, 0, keepdims=True)
        for e in range(experts):
            sent_ref[e, :cap] = mm(table_ref[e], moe_in).astype(BF)
            if joined:
                sent_ref[e, cap:] = cots_ref[e]

    return body


def middle(m, mine, got, tokens, info, member, table, gain, bias, router_t, cots):
    experts, cap, quarter = table.shape
    width = tokens.shape[2]
    shape = jax.ShapeDtypeStruct
    inputs = [mine, got, tokens, info, member, table, gain[None], bias[None], router_t]
    if cots is not None:
        inputs.append(cots)
    out_shape = [
        shape((experts, cap if cots is None else 2 * cap, width), BF),
        shape((quarter, width), BF),
        shape((quarter, width), BF),
        shape((quarter, width), F32),
        shape((experts, quarter), F32),
    ]
    return kernel(
        middle_body(cots is not None),
        out_shape,
        "middle",
        grid=(1,),
        in_specs=[picked(x, m) if k == 2 else whole(x.shape) for k, x in enumerate(inputs)],
        out_specs=[whole(x.shape) for x in out_shape],
    )(*inputs)


def token_back_body(adds):
    def body(back_ref, table_ref, gates_ref, router_ref, moe_ref, residual_ref, rows_ref, gain_ref, *refs):
        if adds:
            earlier_ref, refs = refs[0], refs[1:]
        grad_ref, small_ref = refs
        experts, cap, quarter = table_ref.shape
        width = moe_ref.shape[1]
        table = table_ref[...].reshape(experts * cap, quarter)
        copies = mm(table, back_ref[...].reshape(experts * cap, width), DOWN)
        lines = []
        for e in range(experts):
            both = mm(back_ref[e, cap - TILE :, :][:, :cap], table_ref[e])
            lines.append(both[TILE - 2 : TILE - 1] + both[TILE - 1 :])
        gate_grad = jnp.concatenate(lines, 0)
        gates = gates_ref[...]
        logit_grad = gates * (gate_grad - jnp.sum(gates * gate_grad, 0, keepdims=True))
        coarse = logit_grad.astype(BF)
        fine = (logit_grad - coarse.astype(F32)).astype(BF)
        router = router_ref[...]
        normed2_grad = copies + mm(coarse, router, DOWN) + mm(fine, router, DOWN)
        normed, scale = normalize(residual_ref[...])
        grad_router = mm(coarse, moe_ref[...]) + mm(fine, moe_ref[...])
        small = [
            jnp.sum(normed2_grad * normed, 0, keepdims=True),
            jnp.sum(normed2_grad, 0, keepdims=True),
            grad_router,
        ]
        spare = small_ref.shape[0] - 2 - experts
        small = jnp.concatenate(small + [jnp.zeros((spare, width), F32)], 0)
        if adds:
            small = small + earlier_ref[...]
        small_ref[...] = small.astype(small_ref.dtype)
        pull = normalize_pull(normed, scale, gain_ref[...], normed2_grad)
        grad_ref[...] = (rows_ref[...].astype(F32) + pull).astype(BF)

    return body


def token_back(back, table, gates, router_t, moe_in, residual, rows, gain, earlier, last):
    quarter, width = moe_in.shape
    small_rows = round_up(2 + table.shape[0], 2 * TILE)
    shape = jax.ShapeDtypeStruct
    inputs = [back, table, gates, router_t, moe_in, residual, rows, gain[None]]
    if earlier is not None:
        inputs.append(earlier)
    out_shape = [shape((quarter, width), BF), shape((small_rows, width), BF if last else F32)]
    return kernel(token_back_body(earlier is not None), out_shape, "token_back")(*inputs)


def weight_body(adds, hidden):
    def body(left_ref, right_ref, *refs):
        if adds:
            earlier, refs = refs[:2], refs[2:]
        outs, turned = refs[:2], refs[2]

        @pl.when(pl.program_id(0) == 0)
        def _():
            turned[...] = left_ref[...].T

        for k in range(2):
            found = mm(turned[...], right_ref[:, k * hidden : (k + 1) * hidden])
            if adds:
                found = found + earlier[k][0].astype(F32)
            outs[k][0] = found.astype(BF)

    return body


def weight_grad(left, right, slices, earlier):
    total, width = left.shape
    hidden = right.shape[1] // slices
    pair = pl.BlockSpec((1, width, hidden), lambda p: (p, 0, 0))
    inputs = [left, right]
    in_specs = [
        pl.BlockSpec((total, width), lambda p: (0, 0)),
        pl.BlockSpec((total, 2 * hidden), lambda p: (0, p)),
    ]
    if earlier is not None:
        inputs += list(earlier)
        in_specs += [pair, pair]
    return kernel(
        weight_body(earlier is not None, hidden),
        [jax.ShapeDtypeStruct((slices // 2, width, hidden), BF)] * 2,
        "weight_grad",
        56,
        grid=(slices // 2,),
        in_specs=in_specs,
        out_specs=[pair, pair],
        scratch_shapes=[pltpu.VMEM((width, total), BF)],
    )(*inputs)


def mix_body(back_ref, table_ref, gates_ref, attention_ref, delta_ref):
    experts, cap, quarter = table_ref.shape
    width = back_ref.shape[2]
    weighted = []
    for e in range(experts):
        weighted.append((table_ref[e].astype(F32) * gates_ref[e : e + 1, :]).astype(BF))
    weighted = jnp.concatenate(weighted, 0)
    mixture = mm(weighted, back_ref[...].reshape(experts * cap, width), DOWN)
    delta_ref[...] = (attention_ref[...].astype(F32) + mixture).astype(BF)


def mix(back, part, table, gates, attention):
    experts, cap, quarter = table.shape
    width = attention.shape[1]
    return kernel(
        mix_body,
        jax.ShapeDtypeStruct((quarter, width), BF),
        "mix",
        grid=(1,),
        in_specs=[
            pl.BlockSpec((experts, cap, width), lambda i: (0, part, 0)),
            pl.BlockSpec((experts, cap, quarter), lambda i: (0, 0, 0)),
            pl.BlockSpec((experts, quarter), lambda i: (0, 0)),
            pl.BlockSpec((quarter, width), lambda i: (0, 0)),
        ],
        out_specs=pl.BlockSpec((quarter, width), lambda i: (0, 0)),
    )(back, table, gates, attention)


def output_body(count):
    def body(*refs):
        blocks, (tokens_ref, info_ref) = refs[:count], refs[count : count + 2]
        out_ref = refs[-1]
        info = info_ref[...]
        info_t = info.T
        unperm = jnp.where(info_t[:, 2:3] == info[3:4, :], 1.0, 0.0).astype(BF)
        delta = jnp.concatenate([block[...] for block in blocks], 0)
        out_ref[0] = tokens_ref[0].astype(F32) + mm(unperm, delta)

    return body


def place_rows(inputs, body, name, held, m, micro_count, more_out=(), smem=0):
    total_rows, width = held[1]
    first = pl.BlockSpec((1, total_rows, width), lambda i: (m, 0, 0))

    in_specs = [picked(x, m) if x.ndim == 3 else whole(x.shape) for x in inputs]
    in_specs[:smem] = [pl.BlockSpec(memory_space=pltpu.SMEM)] * smem
    aliases = {}
    inputs = list(inputs)
    if held[0] is not None:
        aliases = {len(inputs): 0}
        inputs.append(held[0])
        in_specs.append(pl.BlockSpec(memory_space=pl.ANY))
    return kernel(
        body,
        [jax.ShapeDtypeStruct((micro_count, total_rows, width), F32)] + list(more_out),
        name,
        grid=(1,),
        in_specs=in_specs,
        out_specs=[first] + [whole(x.shape) for x in more_out],
        input_output_aliases=aliases,
    )(*inputs)


def input_grad_body(total_rows, half):
    def body(flag_ref, mine_ref, other_ref, tokens_ref, resid_ref, gain_ref, *refs):
        grad_ref, sums_ref = refs[-2:]
        mine, other = mine_ref[...].astype(F32), other_ref[...].astype(F32)
        zero = flag_ref[0] == 0
        low = jnp.where(zero, mine, other)
        high = jnp.where(zero, other, mine)
        grad = jnp.concatenate([low, high], 0)[:total_rows]
        normed, scale = normalize(tokens_ref[0].astype(F32))
        sums = [jnp.sum(grad * normed, 0, keepdims=True), jnp.sum(grad, 0, keepdims=True)]
        sums_ref[...] = jnp.concatenate(sums + [jnp.zeros((6, grad.shape[1]), F32)], 0)
        grad_ref[0] = resid_ref[...].astype(F32) + normalize_pull(normed, scale, gain_ref[...], grad)

    return body


def make_shards(ne, nh):
    def to_experts(blocks):
        return lax.all_to_all(blocks, "expert", split_axis=0, concat_axis=0, tiled=True)

    def reduce_quarters(keep, send):
        bit = 1
        while bit < nh // 2:
            got = swap(send, "hidden", bit)
            half = keep.shape[0] // 2
            send = (keep[half:].astype(F32) + got[half:].astype(F32)).astype(BF)
            keep = (keep[:half].astype(F32) + got[:half].astype(F32)).astype(BF)
            bit *= 2
        return keep, swap(send, "hidden", bit)

    def gather_quarters(rows):
        blocks = [rows]
        bit = nh // 2
        while bit >= 1:
            blocks = blocks + [swap(block, "hidden", bit) for block in blocks]
            bit //= 2
        return blocks

    def quarter_order():
        order = [0]
        bit = nh // 2
        while bit >= 1:
            order = order + [r ^ bit for r in order]
            bit //= 2
        return order

    def begin_sum(rows):
        h = lax.axis_index("hidden")
        count = rows.shape[0] // 2
        flag = h % 2
        kept = lax.dynamic_slice_in_dim(rows, flag * count, count, 0)
        sent = lax.dynamic_slice_in_dim(rows, (1 - flag) * count, count, 0)
        kept = (kept.astype(F32) + swap(sent, "hidden", 1).astype(F32)).astype(BF)
        bit = 2
        while bit < nh // 2:
            kept = (kept.astype(F32) + swap(kept, "hidden", bit).astype(F32)).astype(BF)
            bit *= 2
        return kept

    def end_sum(kept, got):
        kept = (kept.astype(F32) + got.astype(F32)).astype(BF)
        return kept, swap(kept, "hidden", 1)

    def shards(
        tokens,
        doc_ids,
        pad_mask,
        norm1_gain,
        norm1_bias,
        qkv_weight,
        out_weight,
        norm2_gain,
        norm2_bias,
        router,
        routes,
        up_weight,
        down_weight,
        cotangent,
    ):
        micro_count, row_count, width = tokens.shape
        expert_count = router.shape[1]
        top_count = routes.shape[2]
        pack_cap = 2 * row_count * top_count // expert_count
        quarter = row_count // nh
        cap = round_up((pack_cap + (nh - 1) * (expert_count - 1)) // nh + 2, TILE)
        order = quarter_order()
        e_idx = lax.axis_index("expert")
        h_idx = lax.axis_index("hidden")
        micros = range(micro_count)

        ups = lax.all_gather(up_weight[0], "hidden")
        downs = lax.all_gather(down_weight[0], "hidden")

        router_t = router.T
        hid = jnp.full((1,), h_idx, jnp.int32)
        routes_t = routes.transpose(0, 2, 1)
        qkv_t = qkv_weight.transpose(0, 2, 1)

        def route(m):
            return route_tokens(
                m, hid, doc_ids, pad_mask, routes_t, cotangent, expert_count, cap, order
            )

        state = []
        for m in micros:
            if m == 0:
                info, member, table, up_rows, up_sent = route(m)
                upstream_slots = to_experts(up_sent)
                earlier = up_sent
            else:
                info, member, table, up_rows, up_sent = following
                earlier = last_sent
            mine_tokens = after(tokens, earlier)
            keep, send, *saved = attend_forward(
                m, mine_tokens, info, norm1_gain, norm1_bias, qkv_t, out_weight
            )
            mine, got = reduce_quarters(keep, send)
            if m + 1 < micro_count:
                following = route(m + 1)
                got, following = after((got, following), following)
            last_sent, moe_in, attention, residual, gates = middle(
                m,
                mine,
                got,
                mine_tokens,
                info,
                member,
                table,
                norm2_gain,
                norm2_bias,
                router_t,
                None if m == 0 else up_sent,
            )
            if m == micro_count - 1:
                last_sent, ups, downs = after((last_sent, ups, downs), (ups, downs))
            if m == 0:
                received = (to_experts(last_sent), 0, upstream_slots, 0)
            else:
                both = to_experts(last_sent)
                received = (both, 0, both, 1)
            state.append(
                dict(
                    saved=saved,
                    info=info,
                    attention=attention,
                    residual=residual,
                    moe_in=moe_in,
                    gates=gates,
                    table=table,
                    up_rows=up_rows,
                    received=received,
                )
            )

        own_expert = jnp.stack([e_idx, h_idx]).astype(jnp.int32)
        held, earlier = None, (None, None)
        for m in micros:
            s = state[m]
            rows, row_part, cots, cot_part = s["received"]
            if m == 0:
                rows = after(rows, last_sent)
            held, copies, *work = run_expert(
                own_expert,
                rows,
                row_part,
                cots,
                cot_part,
                router_t,
                ups,
                downs,
                held,
                m,
                micro_count,
            )
            if m < micro_count - 1:
                earlier = (
                    weight_grad(work[0], work[3], nh, earlier[0]),
                    weight_grad(work[1], work[2], nh, earlier[1]),
                )
                s["copies_back"] = to_experts(after(copies, earlier))
            else:
                s["copies_back"] = to_experts(copies)
                works = work
        small = None
        copies_back = [s["copies_back"] for s in state]
        copies_back[:-1], works = after((copies_back[:-1], works), copies)
        for m in micros:
            s = state[m]
            last = m == micro_count - 1
            if m == micro_count - 1:
                works = after(works, grad_low)
                first = weight_grad(works[0], works[3], nh, earlier[0])
                works, state[0]["resid_all"] = after(
                    (works, state[0]["resid_all"]), (first, state[0]["resid_all"])
                )
                slabs = (
                    first,
                    weight_grad(works[1], works[2], nh, earlier[1]),
                )
                copies_back[1:] = after(copies_back[1:], slabs)
                got = [swap(send, "hidden", 1) for _, send in slabs]
                halves = [
                    jnp.stack(
                        [
                            (keep[p].astype(F32) + other[p].astype(F32)).astype(BF)
                            for (keep, _), other in zip(slabs, got)
                        ]
                    )
                    for p in range(nh // 2)
                ]
            grad_low, small = token_back(
                copies_back[m],
                s["table"],
                s["gates"],
                router_t,
                s["moe_in"],
                s["residual"],
                s["up_rows"],
                norm2_gain,
                small,
                last,
            )
            s["resid_all"] = gather_quarters(grad_low)

        firsts = halves
        gathers = [s["resid_all"] for s in state]

        def finish(part):
            bit = 2
            while bit < nh:
                got = [swap(slab, "hidden", bit) for slab in part[1::2]]
                part = [
                    (mine.astype(F32) + other.astype(F32)).astype(BF)
                    for mine, other in zip(part[0::2], got)
                ]
                bit *= 2
            rows = part[0].reshape(2, ne, width // ne, -1).transpose(1, 0, 2, 3)
            return rows.reshape(ne, 2 * width // ne, -1)

        owned = finish(after(halves, gathers))

        flag = jnp.full((1,), h_idx % 2, jnp.int32)
        pack_sums = None
        input_grads, norm1_sums = None, 0.0
        out_back = to_experts(after(held, copies_back[-1]))
        terms, resids = [], []
        state[0]["resid_all"] = after(state[0]["resid_all"], (firsts, grad_low))
        for m in micros:
            s = state[m]
            term, resid, pack_sums = attend_backward(
                s["resid_all"],
                s["info"],
                s["saved"],
                qkv_t,
                out_weight,
                pack_sums,
                m == micro_count - 1,
            )
            terms.append(term)
            resids.append(resid)
        terms[:-1] = after(terms[:-1], terms[-1])
        terms[-1] = jnp.concatenate([terms[-1], small], 0)
        begun = [begin_sum(term) for term in terms]

        share = pack_sums.reshape(ne, -1, width)
        bit = 1
        while bit < ne:
            side = (e_idx // bit) % 2
            if bit == 2:
                share, out_back, begun = after((share, out_back, begun), (out_back, begun))
                begun = [(kept, swap(kept, "hidden", nh // 2)) for kept in begun]
            if bit == ne // 2:
                share, owned, begun[:1] = after((share, owned, begun[:1]), (owned, begun[:1]))
            pairs = share.reshape(share.shape[0] // 2, 2, -1, width)
            kept = lax.dynamic_index_in_dim(pairs, side, 1, False)
            sent = lax.dynamic_index_in_dim(pairs, 1 - side, 1, False)
            share = (kept.astype(F32) + swap(sent, "expert", bit).astype(F32)).astype(BF)
            bit *= 2
        share = share[0]

        for m in micros:
            s = state[m]
            resid = resids[m]
            mine, other = end_sum(*after(begun[m], share))
            input_grads, sums = place_rows(
                [flag, mine, other, tokens, resid, norm1_gain[None]],
                input_grad_body(row_count, mine.shape[0]),
                "input_grad",
                (input_grads, tokens.shape[1:]),
                m,
                micro_count,
                [jax.ShapeDtypeStruct((8, width), F32)],
                1,
            )
            norm1_sums = norm1_sums + sums


        half = small.shape[0]
        kept = terms[-1].shape[0] // 2
        small = jnp.where(flag == 0, other[kept - half :], mine[kept - half :]).astype(F32)
        small = jnp.concatenate([norm1_sums[:2], small[: 2 + expert_count]], 0)
        small = jnp.pad(small, ((0, round_up(small.shape[0], 8) - small.shape[0]), (0, 0)))
        bit = 1
        while bit < ne:
            small = small + swap(small, "expert", bit)
            bit *= 2
        outputs = None
        for m in micros:
            s = state[m]
            delta = mix(out_back, m, s["table"], s["gates"], s["attention"])
            blocks = gather_quarters(delta)
            (outputs,) = place_rows(
                [*blocks, tokens, s["info"]],
                output_body(len(blocks)),
                "output",
                (outputs, tokens.shape[1:]),
                m,
                micro_count,
            )
        gathered = share[None]
        bit = ne // 2
        while bit >= 1:
            if bit == 1:
                parts = to_experts(after(owned, (out_back, gathered, begun)))[ne // 2 :].astype(F32)
                gathered, outputs = after((gathered, outputs), outputs)
            gathered = jnp.concatenate([gathered, swap(gathered, "expert", bit)], 0)
            bit //= 2
        bits = []
        bit = ne // 2
        found = [0]
        while bit >= 1:
            found = found + [r ^ bit for r in found]
            bit //= 2
        where = jnp.zeros((ne,), jnp.int32)
        slots = jnp.array([found.index(r) for r in range(ne)], jnp.int32)
        where = slots[jnp.arange(ne, dtype=jnp.int32) ^ e_idx]
        flat = gathered[where].astype(F32).reshape(4, -1, width)
        return (
            outputs,
            input_grads,
            small[0],
            small[1],
            flat[:3].transpose(0, 2, 1),
            flat[3],
            small[2],
            small[3],
            small[4 : 4 + expert_count].T,
            parts[:, : width // ne],
            parts[:, width // ne :],
        )

    return shards


def solution(mesh):
    placed = (
        P(None, "expert", None),
        P(None, "expert", None),
        P(None, "expert"),
        P(),
        P(),
        P(None, None, "hidden"),
        P("hidden", None),
        P(),
        P(),
        P(),
        P(None, "expert", None),
        P("expert", None, "hidden"),
        P("expert", None, "hidden"),
        P(None, "expert", None),
    )
    return jax.shard_map(
        make_shards(mesh.shape["expert"], mesh.shape["hidden"]),
        mesh=mesh,
        in_specs=placed,
        out_specs=(
            P(None, "expert", None),
            P(None, "expert", None),
            P(),
            P(),
            P(None, None, "hidden"),
            P("hidden", None),
            P(),
            P(),
            P(),
            P(None, "expert", "hidden"),
            P(None, "expert", "hidden"),
        ),
        check_vma=False,
    )
```

```python
import jax
import jax.numpy as jnp
from jax import lax
from jax.experimental import pallas as pl
from jax.experimental.pallas import tpu as pltpu
from jax.sharding import PartitionSpec as P

HEAD_DIM = 64
EPSILON = 1e-05
PRECISE = lax.Precision.HIGHEST
MASKED = -1e30
TILE = 16
LONGEST = 384
BLOCK = 256
BF = jnp.bfloat16
F32 = jnp.float32


def round_up(value, step):
    return -(-value // step) * step


def swap(values, axis, bit):
    size = lax.axis_size(axis)
    return lax.ppermute(values, axis, [(i, i ^ bit) for i in range(size)])


def normalize(values):
    centre = values - jnp.mean(values, -1, keepdims=True)
    spread = jnp.mean(centre * centre, -1, keepdims=True)
    scale = lax.rsqrt(spread + EPSILON)
    return centre * scale, scale


def normalize_pull(normed, scale, gain, grad):
    wide = grad * gain
    return scale * (
        wide
        - jnp.mean(wide, -1, keepdims=True)
        - normed * jnp.mean(wide * normed, -1, keepdims=True)
    )


def gelu_pair(v):
    c0 = 0.7978845608028654
    inner = c0 * (v + 0.044715 * v * v * v)
    t = jnp.tanh(inner)
    act = 0.5 * v * (1.0 + t)
    slope = 0.5 * (1.0 + t) + 0.5 * v * (1.0 - t * t) * (c0 * (1.0 + 3 * 0.044715 * v * v))
    return act, slope


def after(values, *others):
    return lax.optimization_barrier((values, others))[0]


def diagonal(count):
    return lax.broadcasted_iota(jnp.int32, (count, count), 0) == lax.broadcasted_iota(
        jnp.int32, (count, count), 1
    )


def expert_body(slices, packs, cap, width, aliased):
    rows_n = packs * cap

    def body(own_ref, rows_ref, cot_ref, router_ref, *refs):
        ups, downs = refs[:2]
        refs = refs[2 + (1 if aliased else 0) :]
        (out_ref, copies_ref, rows_all, grads_all, act_all, pre_all) = refs[:6]
        up_v, down_v, grad_rows, acc_out, acc_copies, sems = refs[6:]
        i, s = pl.program_id(0), pl.program_id(1)

        def fetch(r):
            return (
                pltpu.make_async_copy(ups.at[own_ref[1] ^ r], up_v.at[r], sems.at[0, r]),
                pltpu.make_async_copy(downs.at[own_ref[1] ^ r], down_v.at[r], sems.at[1, r]),
            )

        @pl.when((i == 0) & (s == 0))
        def _():
            for r in range(slices):
                for copy in fetch(r):
                    copy.start()

        for r in range(slices):

            @pl.when((i == 0) & (s == r))
            def _():
                for copy in fetch(r):
                    copy.wait()

        @pl.when(s == 0)
        def _():
            rows = rows_ref[...].reshape(rows_n, width)
            rows_all[...] = rows
            logits = mm(rows, router_ref[...], ALONG)
            ordinals = lax.broadcasted_iota(jnp.int32, logits.shape, 1).astype(F32)
            eye = diagonal(cap)
            other = []
            for p in range(packs):
                line = cot_ref[p, cap - TILE :, :][TILE - 1 :, :cap].astype(F32)
                other.append(jnp.sum(jnp.where(eye, line, 0.0), 1, keepdims=True))
            other = jnp.concatenate(other, 0)
            own = own_ref[0].astype(F32)
            picks = jnp.where(ordinals == own, 1.0, 0.0) - jnp.where(ordinals == other, 1.0, 0.0)
            gate = jax.nn.sigmoid(jnp.sum(logits * picks, -1, keepdims=True))
            cot = cot_ref[...].reshape(rows_n, width).astype(F32)
            low = (gate * cot).astype(BF)
            grad_rows[...] = low
            grads_all[...] = low

        up, down = up_v[s], down_v[s]
        pre = jnp.dot(rows_ref[...].reshape(rows_n, width), up, preferred_element_type=F32)
        act_grad = jnp.dot(grad_rows[...], down, preferred_element_type=F32)
        act, slope = gelu_pair(pre)
        act = act.astype(BF)
        act_all[...] = act
        pre_grad = (act_grad * slope).astype(BF)
        pre_all[...] = pre_grad
        along = (((1,), (1,)), ((), ()))
        out = lax.dot_general(act, down, along, preferred_element_type=F32)
        copies = lax.dot_general(pre_grad, up, along, preferred_element_type=F32)

        @pl.when(s == 0)
        def _():
            acc_out[...] = out
            acc_copies[...] = copies

        @pl.when(s > 0)
        def _():
            acc_out[...] += out
            acc_copies[...] += copies

        @pl.when(s == slices - 1)
        def _():
            low = acc_out[...].astype(BF)
            out_ref[...] = low.reshape(packs, cap, width)
            copies_ref[...] = acc_copies[...].astype(BF).reshape(packs, cap, width)
            cot = cot_ref[...].reshape(rows_n, width).astype(F32)
            gate_grad = jnp.sum(cot * low.astype(F32), -1, keepdims=True)
            eye = diagonal(cap)
            index = lax.broadcasted_iota(jnp.int32, (TILE, width), 0)
            for p in range(packs):
                column = gate_grad[p * cap : (p + 1) * cap]
                line = jnp.sum(jnp.where(eye, column, 0.0), 0, keepdims=True)
                line = jnp.concatenate([line, jnp.zeros((1, width - cap), F32)], 1)
                coarse = line.astype(BF).astype(F32)
                tail = copies_ref[p, cap - TILE :, :].astype(F32)
                tail = jnp.where(index == TILE - 1, coarse, tail)
                tail = jnp.where(index == TILE - 2, line - coarse, tail)
                copies_ref[p, cap - TILE :, :] = tail.astype(BF)

    return body


def run_expert(own, rows, row_part, cots, cot_part, router, ups, downs, held, m, micro_count):
    blocks, width = rows.shape[0], rows.shape[2]
    cap = cots.shape[1] // (cot_part + 1)
    slices, _, hidden = ups.shape
    packs = max(p for p in range(1, blocks + 1) if blocks % p == 0 and p * cap <= 448)
    steps = blocks // packs
    total = blocks * cap
    aliased = held is not None
    rows_n = packs * cap

    def block(part):
        return pl.BlockSpec((packs, cap, width), lambda i, s: (i, part, 0))

    any_spec = pl.BlockSpec(memory_space=pl.ANY)
    whole_rows = pl.BlockSpec((rows_n, width), lambda i, s: (i, 0))
    whole_hidden = pl.BlockSpec((rows_n, hidden), lambda i, s: (i, s))
    inputs = [own, rows, cots, router, ups, downs]
    in_specs = [
        pl.BlockSpec(memory_space=pltpu.SMEM),
        block(row_part),
        block(cot_part),
        pl.BlockSpec(router.shape, lambda i, s: (0, 0)),
    ] + [any_spec] * 2
    aliases = {}
    if aliased:
        aliases = {len(inputs): 0}
        inputs.append(held)
        in_specs.append(any_spec)
    return pl.pallas_call(
        expert_body(slices, packs, cap, width, aliased),
        grid=(steps, slices),
        in_specs=in_specs,
        out_specs=[block(m), block(0), whole_rows, whole_rows, whole_hidden, whole_hidden],
        out_shape=[
            jax.ShapeDtypeStruct((blocks, micro_count * cap, width), BF),
            jax.ShapeDtypeStruct((blocks, cap, width), BF),
            jax.ShapeDtypeStruct((total, width), BF),
            jax.ShapeDtypeStruct((total, width), BF),
            jax.ShapeDtypeStruct((total, slices * hidden), BF),
            jax.ShapeDtypeStruct((total, slices * hidden), BF),
        ],
        scratch_shapes=[
            pltpu.VMEM(ups.shape, BF),
            pltpu.VMEM(downs.shape, BF),
            pltpu.VMEM((rows_n, width), BF),
            pltpu.VMEM((rows_n, width), F32),
            pltpu.VMEM((rows_n, width), F32),
            pltpu.SemaphoreType.DMA((2, slices)),
        ],
        input_output_aliases=aliases,
        compiler_params=pltpu.CompilerParams(vmem_limit_bytes=48 * 1024 * 1024),
        cost_estimate=CHEAP,
        name="expert",
    )(*inputs)


CHEAP = pl.CostEstimate(flops=1, bytes_accessed=1, transcendentals=0)
ALONG = (((1,), (1,)), ((), ()))
DOWN = (((0,), (0,)), ((), ()))


def mm(left, right, dims=None):
    if dims is None:
        return jnp.dot(left, right, preferred_element_type=F32)
    return lax.dot_general(left, right, dims, preferred_element_type=F32)


def windows(total_rows):
    for q0 in range(0, total_rows, BLOCK):
        q1 = min(q0 + BLOCK, total_rows)
        yield q0, q1, max(0, (q0 - LONGEST + 1) // 128 * 128)


def visible(info, info_t, q0, q1, k0):
    shape = (q1 - k0, q1 - q0)
    key_pos = lax.broadcasted_iota(jnp.int32, shape, 0) + k0
    query_pos = lax.broadcasted_iota(jnp.int32, shape, 1) + q0
    same_doc = info_t[k0:q1, 0:1] == info[0:1, q0:q1]
    is_real = (info_t[k0:q1, 1:2] == 1.0) | (query_pos == key_pos)
    return (key_pos <= query_pos) & same_doc & is_real


def attend_forward_body(
    tokens_ref, info_ref, gain_ref, bias_ref, qkv_w_ref, out_w_ref,
    keep_ref, send_ref, attn_in_ref, qkv_ref, heads_ref, log_ref,
):
    total_rows = tokens_ref.shape[1]
    local = qkv_w_ref.shape[1]
    info = info_ref[...]
    info_t = info.T
    normed, _ = normalize(tokens_ref[0].astype(F32))
    attn_in = (normed * gain_ref[...] + bias_ref[...]).astype(BF)
    attn_in_ref[...] = attn_in
    for c in range(3):
        qkv_ref[c] = mm(attn_in, qkv_w_ref[c], ALONG).astype(BF)
    for q0, q1, k0 in windows(total_rows):
        allowed = visible(info, info_t, q0, q1, k0)
        for h in range(local // HEAD_DIM):
            part = slice(h * HEAD_DIM, (h + 1) * HEAD_DIM)
            scores = mm(qkv_ref[1, k0:q1, part], qkv_ref[0, q0:q1, part], ALONG)
            scores = jnp.where(allowed, scores * HEAD_DIM**-0.5, MASKED)
            peak = jnp.max(scores, 0, keepdims=True)
            exponent = jnp.exp(scores - peak)
            total = jnp.sum(exponent, 0, keepdims=True)
            weights = (exponent * (1.0 / total)).astype(BF)
            output = mm(qkv_ref[2, k0:q1, part], weights, DOWN)
            heads_ref[q0:q1, part] = output.T.astype(BF)
            log_ref[h : h + 1, q0:q1] = peak + jnp.log(total)
    perm = jnp.where(info_t[:, 3:4] == info[2:3, :], 1.0, 0.0).astype(BF)
    arranged = mm(perm, heads_ref[...]).astype(BF)
    term = mm(arranged, out_w_ref[...]).astype(BF)
    keep_ref[...] = term[: total_rows // 2]
    send_ref[...] = term[total_rows // 2 :]


def attend_forward(m, tokens, info, gain, bias, qkv_weight, out_weight):
    total_rows, width = tokens.shape[1:]
    local = out_weight.shape[0]
    shape = jax.ShapeDtypeStruct
    inputs = [tokens, info, gain[None], bias[None], qkv_weight, out_weight]
    out_shape = [
        shape((total_rows // 2, width), BF),
        shape((total_rows // 2, width), BF),
        shape((total_rows, width), BF),
        shape((3, total_rows, local), BF),
        shape((total_rows, local), BF),
        shape((8, total_rows), F32),
    ]
    return kernel(
        attend_forward_body,
        out_shape,
        "attend_forward",
        grid=(1,),
        in_specs=[picked(x, m) if k == 0 else whole(x.shape) for k, x in enumerate(inputs)],
        out_specs=[whole(x.shape) for x in out_shape],
    )(*inputs)


def attend_backward_body(adds, count):
    def body(*refs):
        blocks, refs = refs[:count], refs[count:]
        info_ref, attn_in_ref, qkv_ref, heads_ref, log_ref, qkv_w_ref, out_w_ref = refs[:7]
        refs = refs[7:]
        if adds:
            earlier_ref, refs = refs[0], refs[1:]
        term_ref, resid_out, sums_ref, grads, key_sum, value_sum = refs
        total_rows = attn_in_ref.shape[0]
        local = out_w_ref.shape[0]
        scale = HEAD_DIM**-0.5
        info = info_ref[...]
        info_t = info.T
        unperm = jnp.where(info_t[:, 2:3] == info[3:4, :], 1.0, 0.0).astype(BF)
        resid = jnp.concatenate([block[...] for block in blocks], 0)
        resid = mm(unperm, resid).astype(BF)
        resid_out[...] = resid
        heads_grad = mm(resid, out_w_ref[...], ALONG).astype(BF)
        key_sum[...] = jnp.zeros(key_sum.shape, F32)
        value_sum[...] = jnp.zeros(value_sum.shape, F32)
        for q0, q1, k0 in windows(total_rows):
            allowed = visible(info, info_t, q0, q1, k0)
            for h in range(local // HEAD_DIM):
                part = slice(h * HEAD_DIM, (h + 1) * HEAD_DIM)
                query, key = qkv_ref[0, q0:q1, part], qkv_ref[1, k0:q1, part]
                value, out_grad = qkv_ref[2, k0:q1, part], heads_grad[q0:q1, part]
                scores = mm(key, query, ALONG) * scale
                scores = jnp.where(allowed, scores, MASKED)
                weights = jnp.exp(scores - log_ref[h : h + 1, q0:q1])
                weight_grad = mm(value, out_grad, ALONG)
                delta = jnp.sum(weights * weight_grad, 0, keepdims=True)
                score_grad = (weights * (weight_grad - delta)).astype(BF)
                grads[0, q0:q1, part] = (scale * mm(key, score_grad, DOWN)).T.astype(BF)
                key_sum[h, k0:q1] += mm(score_grad, query)
                value_sum[h, k0:q1] += mm(weights.astype(BF), out_grad)
        for h in range(local // HEAD_DIM):
            part = slice(h * HEAD_DIM, (h + 1) * HEAD_DIM)
            grads[1, :, part] = (scale * key_sum[h]).astype(BF)
            grads[2, :, part] = value_sum[h].astype(BF)
        term = mm(grads[0], qkv_w_ref[0])
        for c in (1, 2):
            term = term + mm(grads[c], qkv_w_ref[c])
        term_ref[...] = term.astype(BF)
        attn_in = attn_in_ref[...]
        for c in range(4):
            rows = slice(c * local, (c + 1) * local)
            if c < 3:
                found = mm(grads[c], attn_in, DOWN)
            else:
                found = mm(heads_ref[...], resid, DOWN)
            if adds:
                found = found + earlier_ref[rows, :]
            sums_ref[rows, :] = found.astype(sums_ref.dtype)

    return body


def attend_backward(blocks, info, saved, qkv_weight, out_weight, earlier, last):
    attn_in, qkv, heads, log_total = saved
    total_rows, width = attn_in.shape
    local = out_weight.shape[0]
    shape = jax.ShapeDtypeStruct
    inputs = [*blocks, info, attn_in, qkv, heads, log_total, qkv_weight, out_weight]
    if earlier is not None:
        inputs.append(earlier)
    return pl.pallas_call(
        attend_backward_body(earlier is not None, len(blocks)),
        out_shape=[
            shape((total_rows, width), BF),
            shape((total_rows, width), BF),
            shape((4 * local, width), BF if last else F32),
        ],
        scratch_shapes=[
            pltpu.VMEM((3, total_rows, local), BF),
            pltpu.VMEM((local // HEAD_DIM, total_rows, HEAD_DIM), F32),
            pltpu.VMEM((local // HEAD_DIM, total_rows, HEAD_DIM), F32),
        ],
        compiler_params=pltpu.CompilerParams(vmem_limit_bytes=48 * 1024 * 1024),
        cost_estimate=CHEAP,
        name="attend_backward",
    )(*inputs)


def chosen(info, info_t, count):
    return jnp.where(info_t[:count, 3:4] == info[2:3, :], 1.0, 0.0).astype(BF)


def kernel(body, out_shape, name, mebibytes=40, **options):
    return pl.pallas_call(
        body,
        out_shape=out_shape,
        compiler_params=pltpu.CompilerParams(vmem_limit_bytes=mebibytes * 1024 * 1024),
        cost_estimate=CHEAP,
        name=name,
        **options,
    )


def route_body(m, order):
    def body(hid_ref, doc_ref, pad_ref, routes_ref, cot_ref, *outs):
        route_pack(m, order, hid_ref, doc_ref, pad_ref, routes_ref, cot_ref, *outs)

    return body


def route_pack(m, order, hid_ref, doc_ref, pad_ref, routes_ref, cot_ref, info_out, member_ref, table_ref, rows_ref, sent_ref):
    experts, cap, quarter = table_ref.shape
    total_rows, width = cot_ref.shape[1:]
    dealt = lax.broadcasted_iota(jnp.int32, (1, quarter), 1) * len(order)
    deal = jnp.concatenate([dealt + (hid_ref[0] ^ r) for r in order], 1).astype(F32)
    info = jnp.zeros(info_out.shape, F32)
    line = lax.broadcasted_iota(jnp.int32, info.shape, 0)
    routes = routes_ref[m].astype(F32)
    known = (doc_ref[m].astype(F32), pad_ref[m : m + 1, :].astype(F32), None, deal, routes[:1], routes[1:])
    for k, row in enumerate(known):
        if row is not None:
            info = jnp.where(line == k, row, info)
    low = jnp.minimum(info[4:5], info[5:6])
    high = jnp.maximum(info[4:5], info[5:6])
    place = lax.broadcasted_iota(jnp.int32, (1, total_rows), 1).astype(F32)
    key = (low * experts + high) * total_rows + place
    key_t = jnp.where(line == 6, key, info).T
    rank = jnp.sum(jnp.where(key_t[:, 6:7] < key, 1.0, 0.0), 0, keepdims=True)
    info = jnp.where(line == 2, rank, info)
    info_out[...] = info
    perm = chosen(info, info.T, quarter)
    mine = mm(info.astype(BF), perm, ALONG)
    first, second = mine[4:5], mine[5:6]
    names = lax.broadcasted_iota(jnp.int32, (experts, quarter), 0).astype(F32)
    member = jnp.where((first == names) | (second == names), 1.0, 0.0)
    member_ref[...] = member
    shape = (quarter, quarter)
    before = lax.broadcasted_iota(jnp.int32, shape, 0) < lax.broadcasted_iota(jnp.int32, shape, 1)
    place = mm(member.astype(BF), jnp.where(before, 1.0, 0.0).astype(BF))
    rows = mm(perm, cot_ref[0]).astype(BF)
    rows_ref[...] = rows
    slot = lax.broadcasted_iota(jnp.int32, (cap, quarter), 0).astype(F32)
    last = lax.broadcasted_iota(jnp.int32, (cap, width), 0) == cap - 1
    for e in range(experts):
        match = (slot == place[e : e + 1]) & (member[e : e + 1] > 0.5)
        table = jnp.where(match, 1.0, 0.0).astype(BF)
        table_ref[e] = table
        others = jnp.broadcast_to(first + second - e, (8, quarter)).astype(BF)
        other = mm(others, table, ALONG)[:1]
        other = jnp.concatenate([other, jnp.zeros((1, width - cap), F32)], 1)
        sent_ref[e] = jnp.where(last, other, mm(table, rows)).astype(BF)


def whole(shape):
    return pl.BlockSpec(shape, lambda i: (0,) * len(shape))


def picked(values, m):
    return pl.BlockSpec((1,) + values.shape[1:], lambda i: (m, 0, 0))


def route_tokens(m, hid, doc_ids, pad_mask, routes, cotangent, experts, cap, order):
    total_rows, width = cotangent.shape[1:]
    quarter = total_rows // len(order)
    out_shape = [
        jax.ShapeDtypeStruct((8, total_rows), F32),
        jax.ShapeDtypeStruct((experts, quarter), F32),
        jax.ShapeDtypeStruct((experts, cap, quarter), BF),
        jax.ShapeDtypeStruct((quarter, width), BF),
        jax.ShapeDtypeStruct((experts, cap, width), BF),
    ]
    return kernel(
        route_body(m, order),
        out_shape,
        "route",
        grid=(1,),
        in_specs=[
            pl.BlockSpec(memory_space=pltpu.SMEM),
            whole(doc_ids.shape),
            whole(pad_mask.shape),
            whole(routes.shape),
            picked(cotangent, m),
        ],
        out_specs=[whole(x.shape) for x in out_shape],
    )(hid, doc_ids, pad_mask, routes, cotangent)


def middle_body(joined):
    def body(mine_ref, got_ref, tokens_ref, info_ref, member_ref, table_ref, gain_ref, bias_ref, router_ref, *refs):
        if joined:
            cots_ref, refs = refs[0], refs[1:]
        sent_ref, moe_ref, attention_ref, residual_ref, gates_ref = refs
        experts, cap, quarter = table_ref.shape
        info = info_ref[...]
        perm = chosen(info, info.T, quarter)
        attention = mine_ref[...].astype(F32) + got_ref[...].astype(F32)
        attention_ref[...] = attention.astype(BF)
        residual = mm(perm, tokens_ref[0]) + attention
        residual_ref[...] = residual
        normed, _ = normalize(residual)
        moe_in = (normed * gain_ref[...] + bias_ref[...]).astype(BF)
        moe_ref[...] = moe_in
        logits = mm(router_ref[...], moe_in, ALONG)
        member = member_ref[...] > 0.5
        masked = jnp.where(member, logits, MASKED)
        raised = jnp.where(member, jnp.exp(masked - jnp.max(masked, 0, keepdims=True)), 0.0)
        gates_ref[...] = raised / jnp.sum(raised, 0, keepdims=True)
        for e in range(experts):
            sent_ref[e, :cap] = mm(table_ref[e], moe_in).astype(BF)
            if joined:
                sent_ref[e, cap:] = cots_ref[e]

    return body


def middle(m, mine, got, tokens, info, member, table, gain, bias, router_t, cots):
    experts, cap, quarter = table.shape
    width = tokens.shape[2]
    shape = jax.ShapeDtypeStruct
    inputs = [mine, got, tokens, info, member, table, gain[None], bias[None], router_t]
    if cots is not None:
        inputs.append(cots)
    out_shape = [
        shape((experts, cap if cots is None else 2 * cap, width), BF),
        shape((quarter, width), BF),
        shape((quarter, width), BF),
        shape((quarter, width), F32),
        shape((experts, quarter), F32),
    ]
    return kernel(
        middle_body(cots is not None),
        out_shape,
        "middle",
        grid=(1,),
        in_specs=[picked(x, m) if k == 2 else whole(x.shape) for k, x in enumerate(inputs)],
        out_specs=[whole(x.shape) for x in out_shape],
    )(*inputs)


def token_back_body(adds):
    def body(back_ref, table_ref, gates_ref, router_ref, moe_ref, residual_ref, rows_ref, gain_ref, *refs):
        if adds:
            earlier_ref, refs = refs[0], refs[1:]
        grad_ref, small_ref = refs
        experts, cap, quarter = table_ref.shape
        width = moe_ref.shape[1]
        table = table_ref[...].reshape(experts * cap, quarter)
        copies = mm(table, back_ref[...].reshape(experts * cap, width), DOWN)
        lines = []
        for e in range(experts):
            both = mm(back_ref[e, cap - TILE :, :][:, :cap], table_ref[e])
            lines.append(both[TILE - 2 : TILE - 1] + both[TILE - 1 :])
        gate_grad = jnp.concatenate(lines, 0)
        gates = gates_ref[...]
        logit_grad = gates * (gate_grad - jnp.sum(gates * gate_grad, 0, keepdims=True))
        coarse = logit_grad.astype(BF)
        fine = (logit_grad - coarse.astype(F32)).astype(BF)
        router = router_ref[...]
        normed2_grad = copies + mm(coarse, router, DOWN) + mm(fine, router, DOWN)
        normed, scale = normalize(residual_ref[...])
        grad_router = mm(coarse, moe_ref[...]) + mm(fine, moe_ref[...])
        small = [
            jnp.sum(normed2_grad * normed, 0, keepdims=True),
            jnp.sum(normed2_grad, 0, keepdims=True),
            grad_router,
        ]
        spare = small_ref.shape[0] - 2 - experts
        small = jnp.concatenate(small + [jnp.zeros((spare, width), F32)], 0)
        if adds:
            small = small + earlier_ref[...]
        small_ref[...] = small.astype(small_ref.dtype)
        pull = normalize_pull(normed, scale, gain_ref[...], normed2_grad)
        grad_ref[...] = (rows_ref[...].astype(F32) + pull).astype(BF)

    return body


def token_back(back, table, gates, router_t, moe_in, residual, rows, gain, earlier, last):
    quarter, width = moe_in.shape
    small_rows = round_up(2 + table.shape[0], 2 * TILE)
    shape = jax.ShapeDtypeStruct
    inputs = [back, table, gates, router_t, moe_in, residual, rows, gain[None]]
    if earlier is not None:
        inputs.append(earlier)
    out_shape = [shape((quarter, width), BF), shape((small_rows, width), BF if last else F32)]
    return kernel(token_back_body(earlier is not None), out_shape, "token_back")(*inputs)


def weight_body(adds, hidden):
    def body(left_ref, right_ref, *refs):
        if adds:
            earlier, refs = refs[:2], refs[2:]
        outs, turned = refs[:2], refs[2]

        @pl.when(pl.program_id(0) == 0)
        def _():
            turned[...] = left_ref[...].T

        for k in range(2):
            found = mm(turned[...], right_ref[:, k * hidden : (k + 1) * hidden])
            if adds:
                found = found + earlier[k][0].astype(F32)
            outs[k][0] = found.astype(BF)

    return body


def weight_grad(left, right, slices, earlier):
    total, width = left.shape
    hidden = right.shape[1] // slices
    pair = pl.BlockSpec((1, width, hidden), lambda p: (p, 0, 0))
    inputs = [left, right]
    in_specs = [
        pl.BlockSpec((total, width), lambda p: (0, 0)),
        pl.BlockSpec((total, 2 * hidden), lambda p: (0, p)),
    ]
    if earlier is not None:
        inputs += list(earlier)
        in_specs += [pair, pair]
    return kernel(
        weight_body(earlier is not None, hidden),
        [jax.ShapeDtypeStruct((slices // 2, width, hidden), BF)] * 2,
        "weight_grad",
        56,
        grid=(slices // 2,),
        in_specs=in_specs,
        out_specs=[pair, pair],
        scratch_shapes=[pltpu.VMEM((width, total), BF)],
    )(*inputs)


def mix_body(back_ref, table_ref, gates_ref, attention_ref, delta_ref):
    experts, cap, quarter = table_ref.shape
    width = back_ref.shape[2]
    weighted = []
    for e in range(experts):
        weighted.append((table_ref[e].astype(F32) * gates_ref[e : e + 1, :]).astype(BF))
    weighted = jnp.concatenate(weighted, 0)
    mixture = mm(weighted, back_ref[...].reshape(experts * cap, width), DOWN)
    delta_ref[...] = (attention_ref[...].astype(F32) + mixture).astype(BF)


def mix(back, part, table, gates, attention):
    experts, cap, quarter = table.shape
    width = attention.shape[1]
    return kernel(
        mix_body,
        jax.ShapeDtypeStruct((quarter, width), BF),
        "mix",
        grid=(1,),
        in_specs=[
            pl.BlockSpec((experts, cap, width), lambda i: (0, part, 0)),
            pl.BlockSpec((experts, cap, quarter), lambda i: (0, 0, 0)),
            pl.BlockSpec((experts, quarter), lambda i: (0, 0)),
            pl.BlockSpec((quarter, width), lambda i: (0, 0)),
        ],
        out_specs=pl.BlockSpec((quarter, width), lambda i: (0, 0)),
    )(back, table, gates, attention)


def output_body(count):
    def body(*refs):
        blocks, (tokens_ref, info_ref) = refs[:count], refs[count : count + 2]
        out_ref = refs[-1]
        info = info_ref[...]
        info_t = info.T
        unperm = jnp.where(info_t[:, 2:3] == info[3:4, :], 1.0, 0.0).astype(BF)
        delta = jnp.concatenate([block[...] for block in blocks], 0)
        out_ref[0] = tokens_ref[0].astype(F32) + mm(unperm, delta)

    return body


def place_rows(inputs, body, name, held, m, micro_count, more_out=(), smem=0):
    total_rows, width = held[1]
    first = pl.BlockSpec((1, total_rows, width), lambda i: (m, 0, 0))

    in_specs = [picked(x, m) if x.ndim == 3 else whole(x.shape) for x in inputs]
    in_specs[:smem] = [pl.BlockSpec(memory_space=pltpu.SMEM)] * smem
    aliases = {}
    inputs = list(inputs)
    if held[0] is not None:
        aliases = {len(inputs): 0}
        inputs.append(held[0])
        in_specs.append(pl.BlockSpec(memory_space=pl.ANY))
    return kernel(
        body,
        [jax.ShapeDtypeStruct((micro_count, total_rows, width), F32)] + list(more_out),
        name,
        grid=(1,),
        in_specs=in_specs,
        out_specs=[first] + [whole(x.shape) for x in more_out],
        input_output_aliases=aliases,
    )(*inputs)


def input_grad_body(total_rows, half):
    def body(flag_ref, mine_ref, other_ref, tokens_ref, resid_ref, gain_ref, *refs):
        grad_ref, sums_ref = refs[-2:]
        mine, other = mine_ref[...].astype(F32), other_ref[...].astype(F32)
        zero = flag_ref[0] == 0
        low = jnp.where(zero, mine, other)
        high = jnp.where(zero, other, mine)
        grad = jnp.concatenate([low, high], 0)[:total_rows]
        normed, scale = normalize(tokens_ref[0].astype(F32))
        sums = [jnp.sum(grad * normed, 0, keepdims=True), jnp.sum(grad, 0, keepdims=True)]
        sums_ref[...] = jnp.concatenate(sums + [jnp.zeros((6, grad.shape[1]), F32)], 0)
        grad_ref[0] = resid_ref[...].astype(F32) + normalize_pull(normed, scale, gain_ref[...], grad)

    return body


def make_shards(ne, nh):
    def to_experts(blocks):
        return lax.all_to_all(blocks, "expert", split_axis=0, concat_axis=0, tiled=True)

    def reduce_quarters(keep, send):
        bit = 1
        while bit < nh // 2:
            got = swap(send, "hidden", bit)
            half = keep.shape[0] // 2
            send = (keep[half:].astype(F32) + got[half:].astype(F32)).astype(BF)
            keep = (keep[:half].astype(F32) + got[:half].astype(F32)).astype(BF)
            bit *= 2
        return keep, swap(send, "hidden", bit)

    def gather_quarters(rows):
        blocks = [rows]
        bit = nh // 2
        while bit >= 1:
            blocks = blocks + [swap(block, "hidden", bit) for block in blocks]
            bit //= 2
        return blocks

    def quarter_order():
        order = [0]
        bit = nh // 2
        while bit >= 1:
            order = order + [r ^ bit for r in order]
            bit //= 2
        return order

    def begin_sum(rows):
        h = lax.axis_index("hidden")
        count = rows.shape[0] // 2
        flag = h % 2
        kept = lax.dynamic_slice_in_dim(rows, flag * count, count, 0)
        sent = lax.dynamic_slice_in_dim(rows, (1 - flag) * count, count, 0)
        kept = (kept.astype(F32) + swap(sent, "hidden", 1).astype(F32)).astype(BF)
        bit = 2
        while bit < nh // 2:
            kept = (kept.astype(F32) + swap(kept, "hidden", bit).astype(F32)).astype(BF)
            bit *= 2
        return kept

    def end_sum(kept, got):
        kept = (kept.astype(F32) + got.astype(F32)).astype(BF)
        return kept, swap(kept, "hidden", 1)

    def shards(
        tokens,
        doc_ids,
        pad_mask,
        norm1_gain,
        norm1_bias,
        qkv_weight,
        out_weight,
        norm2_gain,
        norm2_bias,
        router,
        routes,
        up_weight,
        down_weight,
        cotangent,
    ):
        micro_count, row_count, width = tokens.shape
        expert_count = router.shape[1]
        top_count = routes.shape[2]
        pack_cap = 2 * row_count * top_count // expert_count
        quarter = row_count // nh
        cap = round_up((pack_cap + (nh - 1) * (expert_count - 1)) // nh + 2, TILE)
        order = quarter_order()
        e_idx = lax.axis_index("expert")
        h_idx = lax.axis_index("hidden")
        micros = range(micro_count)

        ups = lax.all_gather(up_weight[0], "hidden")
        downs = lax.all_gather(down_weight[0], "hidden")

        router_t = router.T
        hid = jnp.full((1,), h_idx, jnp.int32)
        routes_t = routes.transpose(0, 2, 1)
        qkv_t = qkv_weight.transpose(0, 2, 1)

        def route(m):
            return route_tokens(
                m, hid, doc_ids, pad_mask, routes_t, cotangent, expert_count, cap, order
            )

        state = []
        for m in micros:
            if m == 0:
                info, member, table, up_rows, up_sent = route(m)
                upstream_slots = to_experts(up_sent)
                earlier = up_sent
            else:
                info, member, table, up_rows, up_sent = following
                earlier = last_sent
            mine_tokens = after(tokens, earlier)
            keep, send, *saved = attend_forward(
                m, mine_tokens, info, norm1_gain, norm1_bias, qkv_t, out_weight
            )
            mine, got = reduce_quarters(keep, send)
            if m + 1 < micro_count:
                following = route(m + 1)
                got, following = after((got, following), following)
            last_sent, moe_in, attention, residual, gates = middle(
                m,
                mine,
                got,
                mine_tokens,
                info,
                member,
                table,
                norm2_gain,
                norm2_bias,
                router_t,
                None if m == 0 else up_sent,
            )
            if m == micro_count - 1:
                last_sent, ups, downs = after((last_sent, ups, downs), (ups, downs))
            if m == 0:
                received = (to_experts(last_sent), 0, upstream_slots, 0)
            else:
                both = to_experts(last_sent)
                received = (both, 0, both, 1)
            state.append(
                dict(
                    saved=saved,
                    info=info,
                    attention=attention,
                    residual=residual,
                    moe_in=moe_in,
                    gates=gates,
                    table=table,
                    up_rows=up_rows,
                    received=received,
                )
            )

        own_expert = jnp.stack([e_idx, h_idx]).astype(jnp.int32)
        held, earlier = None, (None, None)
        for m in micros:
            s = state[m]
            rows, row_part, cots, cot_part = s["received"]
            if m == 0:
                rows = after(rows, last_sent)
            held, copies, *work = run_expert(
                own_expert,
                rows,
                row_part,
                cots,
                cot_part,
                router_t,
                ups,
                downs,
                held,
                m,
                micro_count,
            )
            if m < micro_count - 1:
                earlier = (
                    weight_grad(work[0], work[3], nh, earlier[0]),
                    weight_grad(work[1], work[2], nh, earlier[1]),
                )
                s["copies_back"] = to_experts(after(copies, earlier))
            else:
                s["copies_back"] = to_experts(copies)
                works = work
        small = None
        copies_back = [s["copies_back"] for s in state]
        copies_back[:-1], works = after((copies_back[:-1], works), copies)
        for m in micros:
            s = state[m]
            last = m == micro_count - 1
            if m == micro_count - 1:
                works = after(works, grad_low)
                first = weight_grad(works[0], works[3], nh, earlier[0])
                works, state[0]["resid_all"] = after(
                    (works, state[0]["resid_all"]), (first, state[0]["resid_all"])
                )
                slabs = (
                    first,
                    weight_grad(works[1], works[2], nh, earlier[1]),
                )
                copies_back[1:] = after(copies_back[1:], slabs)
                got = [swap(send, "hidden", 1) for _, send in slabs]
                halves = [
                    jnp.stack(
                        [
                            (keep[p].astype(F32) + other[p].astype(F32)).astype(BF)
                            for (keep, _), other in zip(slabs, got)
                        ]
                    )
                    for p in range(nh // 2)
                ]
            grad_low, small = token_back(
                copies_back[m],
                s["table"],
                s["gates"],
                router_t,
                s["moe_in"],
                s["residual"],
                s["up_rows"],
                norm2_gain,
                small,
                last,
            )
            s["resid_all"] = gather_quarters(grad_low)

        firsts = halves
        gathers = [s["resid_all"] for s in state]

        def finish(part):
            bit = 2
            while bit < nh:
                got = [swap(slab, "hidden", bit) for slab in part[1::2]]
                part = [
                    (mine.astype(F32) + other.astype(F32)).astype(BF)
                    for mine, other in zip(part[0::2], got)
                ]
                bit *= 2
            rows = part[0].reshape(2, ne, width // ne, -1).transpose(1, 0, 2, 3)
            return rows.reshape(ne, 2 * width // ne, -1)

        owned = finish(after(halves, gathers))

        flag = jnp.full((1,), h_idx % 2, jnp.int32)
        pack_sums = None
        input_grads, norm1_sums = None, 0.0
        out_back = to_experts(after(held, copies_back[-1]))
        terms, resids = [], []
        state[0]["resid_all"] = after(state[0]["resid_all"], (firsts, grad_low))
        for m in micros:
            s = state[m]
            term, resid, pack_sums = attend_backward(
                s["resid_all"],
                s["info"],
                s["saved"],
                qkv_t,
                out_weight,
                pack_sums,
                m == micro_count - 1,
            )
            terms.append(term)
            resids.append(resid)
        terms[:-1] = after(terms[:-1], terms[-1])
        terms[-1] = jnp.concatenate([terms[-1], small], 0)
        begun = [begin_sum(term) for term in terms]

        share = pack_sums.reshape(ne, -1, width)
        bit = 1
        while bit < ne:
            side = (e_idx // bit) % 2
            if bit == 2:
                share, out_back, begun = after((share, out_back, begun), (out_back, begun))
                begun = [(kept, swap(kept, "hidden", nh // 2)) for kept in begun]
            if bit == ne // 2:
                deltas = [
                    mix(out_back, m, s["table"], s["gates"], s["attention"])
                    for m, s in enumerate(state)
                ]
                needed = (share, owned, begun[:1], deltas)
                share, owned, begun[:1], deltas = lax.optimization_barrier(needed)
            pairs = share.reshape(share.shape[0] // 2, 2, -1, width)
            kept = lax.dynamic_index_in_dim(pairs, side, 1, False)
            sent = lax.dynamic_index_in_dim(pairs, 1 - side, 1, False)
            share = (kept.astype(F32) + swap(sent, "expert", bit).astype(F32)).astype(BF)
            bit *= 2
        share = share[0]

        for m in micros:
            s = state[m]
            resid = resids[m]
            mine, other = end_sum(*after(begun[m], share))
            input_grads, sums = place_rows(
                [flag, mine, other, tokens, resid, norm1_gain[None]],
                input_grad_body(row_count, mine.shape[0]),
                "input_grad",
                (input_grads, tokens.shape[1:]),
                m,
                micro_count,
                [jax.ShapeDtypeStruct((8, width), F32)],
                1,
            )
            norm1_sums = norm1_sums + sums


        half = small.shape[0]
        kept = terms[-1].shape[0] // 2
        small = jnp.where(flag == 0, other[kept - half :], mine[kept - half :]).astype(F32)
        small = jnp.concatenate([norm1_sums[:2], small[: 2 + expert_count]], 0)
        small = jnp.pad(small, ((0, round_up(small.shape[0], 8) - small.shape[0]), (0, 0)))
        bit = 1
        while bit < ne:
            small = small + swap(small, "expert", bit)
            bit *= 2
        outputs = None
        for m in micros:
            s = state[m]
            blocks = after(gather_quarters(deltas[m]), norm1_sums)
            (outputs,) = place_rows(
                [*blocks, tokens, s["info"]],
                output_body(len(blocks)),
                "output",
                (outputs, tokens.shape[1:]),
                m,
                micro_count,
            )
        gathered = share[None]
        bit = ne // 2
        while bit >= 1:
            if bit == 1:
                parts = to_experts(after(owned, (out_back, gathered, begun)))[ne // 2 :].astype(F32)
                gathered, outputs = after((gathered, outputs), outputs)
            gathered = jnp.concatenate([gathered, swap(gathered, "expert", bit)], 0)
            bit //= 2
        bits = []
        bit = ne // 2
        found = [0]
        while bit >= 1:
            found = found + [r ^ bit for r in found]
            bit //= 2
        where = jnp.zeros((ne,), jnp.int32)
        slots = jnp.array([found.index(r) for r in range(ne)], jnp.int32)
        where = slots[jnp.arange(ne, dtype=jnp.int32) ^ e_idx]
        flat = gathered[where].astype(F32).reshape(4, -1, width)
        return (
            outputs,
            input_grads,
            small[0],
            small[1],
            flat[:3].transpose(0, 2, 1),
            flat[3],
            small[2],
            small[3],
            small[4 : 4 + expert_count].T,
            parts[:, : width // ne],
            parts[:, width // ne :],
        )

    return shards


def solution(mesh):
    placed = (
        P(None, "expert", None),
        P(None, "expert", None),
        P(None, "expert"),
        P(),
        P(),
        P(None, None, "hidden"),
        P("hidden", None),
        P(),
        P(),
        P(),
        P(None, "expert", None),
        P("expert", None, "hidden"),
        P("expert", None, "hidden"),
        P(None, "expert", None),
    )
    return jax.shard_map(
        make_shards(mesh.shape["expert"], mesh.shape["hidden"]),
        mesh=mesh,
        in_specs=placed,
        out_specs=(
            P(None, "expert", None),
            P(None, "expert", None),
            P(),
            P(),
            P(None, None, "hidden"),
            P("hidden", None),
            P(),
            P(),
            P(),
            P(None, "expert", "hidden"),
            P(None, "expert", "hidden"),
        ),
        check_vma=False,
    )
```

```python
import jax
import jax.numpy as jnp
from jax import lax
from jax.experimental import pallas as pl
from jax.experimental.pallas import tpu as pltpu
from jax.sharding import PartitionSpec as P

HEAD_DIM = 64
EPSILON = 1e-05
PRECISE = lax.Precision.HIGHEST
MASKED = -1e30
TILE = 16
LONGEST = 384
BLOCK = 256
BF = jnp.bfloat16
F32 = jnp.float32


def round_up(value, step):
    return -(-value // step) * step


def swap(values, axis, bit):
    size = lax.axis_size(axis)
    return lax.ppermute(values, axis, [(i, i ^ bit) for i in range(size)])


def normalize(values):
    centre = values - jnp.mean(values, -1, keepdims=True)
    spread = jnp.mean(centre * centre, -1, keepdims=True)
    scale = lax.rsqrt(spread + EPSILON)
    return centre * scale, scale


def normalize_pull(normed, scale, gain, grad):
    wide = grad * gain
    return scale * (
        wide
        - jnp.mean(wide, -1, keepdims=True)
        - normed * jnp.mean(wide * normed, -1, keepdims=True)
    )


def gelu_pair(v):
    c0 = 0.7978845608028654
    inner = c0 * (v + 0.044715 * v * v * v)
    t = jnp.tanh(inner)
    act = 0.5 * v * (1.0 + t)
    slope = 0.5 * (1.0 + t) + 0.5 * v * (1.0 - t * t) * (c0 * (1.0 + 3 * 0.044715 * v * v))
    return act, slope


def after(values, *others):
    return lax.optimization_barrier((values, others))[0]


def diagonal(count):
    return lax.broadcasted_iota(jnp.int32, (count, count), 0) == lax.broadcasted_iota(
        jnp.int32, (count, count), 1
    )


def expert_body(slices, packs, cap, width, aliased):
    rows_n = packs * cap

    def body(own_ref, rows_ref, cot_ref, router_ref, *refs):
        ups, downs = refs[:2]
        refs = refs[2 + (1 if aliased else 0) :]
        (out_ref, copies_ref, rows_all, grads_all, act_all, pre_all) = refs[:6]
        up_v, down_v, grad_rows, acc_out, acc_copies, sems = refs[6:]
        i, s = pl.program_id(0), pl.program_id(1)

        def fetch(r):
            return (
                pltpu.make_async_copy(ups.at[own_ref[1] ^ r], up_v.at[r], sems.at[0, r]),
                pltpu.make_async_copy(downs.at[own_ref[1] ^ r], down_v.at[r], sems.at[1, r]),
            )

        @pl.when((i == 0) & (s == 0))
        def _():
            for r in range(slices):
                for copy in fetch(r):
                    copy.start()

        for r in range(slices):

            @pl.when((i == 0) & (s == r))
            def _():
                for copy in fetch(r):
                    copy.wait()

        @pl.when(s == 0)
        def _():
            rows = rows_ref[...].reshape(rows_n, width)
            rows_all[...] = rows
            logits = mm(rows, router_ref[...], ALONG)
            ordinals = lax.broadcasted_iota(jnp.int32, logits.shape, 1).astype(F32)
            eye = diagonal(cap)
            other = []
            for p in range(packs):
                line = cot_ref[p, cap - TILE :, :][TILE - 1 :, :cap].astype(F32)
                other.append(jnp.sum(jnp.where(eye, line, 0.0), 1, keepdims=True))
            other = jnp.concatenate(other, 0)
            own = own_ref[0].astype(F32)
            picks = jnp.where(ordinals == own, 1.0, 0.0) - jnp.where(ordinals == other, 1.0, 0.0)
            gate = jax.nn.sigmoid(jnp.sum(logits * picks, -1, keepdims=True))
            cot = cot_ref[...].reshape(rows_n, width).astype(F32)
            low = (gate * cot).astype(BF)
            grad_rows[...] = low
            grads_all[...] = low

        up, down = up_v[s], down_v[s]
        pre = jnp.dot(rows_ref[...].reshape(rows_n, width), up, preferred_element_type=F32)
        act_grad = jnp.dot(grad_rows[...], down, preferred_element_type=F32)
        act, slope = gelu_pair(pre)
        act = act.astype(BF)
        act_all[...] = act
        pre_grad = (act_grad * slope).astype(BF)
        pre_all[...] = pre_grad
        along = (((1,), (1,)), ((), ()))
        out = lax.dot_general(act, down, along, preferred_element_type=F32)
        copies = lax.dot_general(pre_grad, up, along, preferred_element_type=F32)

        @pl.when(s == 0)
        def _():
            acc_out[...] = out
            acc_copies[...] = copies

        @pl.when(s > 0)
        def _():
            acc_out[...] += out
            acc_copies[...] += copies

        @pl.when(s == slices - 1)
        def _():
            low = acc_out[...].astype(BF)
            out_ref[...] = low.reshape(packs, cap, width)
            copies_ref[...] = acc_copies[...].astype(BF).reshape(packs, cap, width)
            cot = cot_ref[...].reshape(rows_n, width).astype(F32)
            gate_grad = jnp.sum(cot * low.astype(F32), -1, keepdims=True)
            eye = diagonal(cap)
            index = lax.broadcasted_iota(jnp.int32, (TILE, width), 0)
            for p in range(packs):
                column = gate_grad[p * cap : (p + 1) * cap]
                line = jnp.sum(jnp.where(eye, column, 0.0), 0, keepdims=True)
                line = jnp.concatenate([line, jnp.zeros((1, width - cap), F32)], 1)
                coarse = line.astype(BF).astype(F32)
                tail = copies_ref[p, cap - TILE :, :].astype(F32)
                tail = jnp.where(index == TILE - 1, coarse, tail)
                tail = jnp.where(index == TILE - 2, line - coarse, tail)
                copies_ref[p, cap - TILE :, :] = tail.astype(BF)

    return body


def run_expert(own, rows, row_part, cots, cot_part, router, ups, downs, held, m, micro_count):
    blocks, width = rows.shape[0], rows.shape[2]
    cap = cots.shape[1] // (cot_part + 1)
    slices, _, hidden = ups.shape
    packs = max(p for p in range(1, blocks + 1) if blocks % p == 0 and p * cap <= 896)
    steps = blocks // packs
    total = blocks * cap
    aliased = held is not None
    rows_n = packs * cap

    def block(part):
        return pl.BlockSpec((packs, cap, width), lambda i, s: (i, part, 0))

    any_spec = pl.BlockSpec(memory_space=pl.ANY)
    whole_rows = pl.BlockSpec((rows_n, width), lambda i, s: (i, 0))
    whole_hidden = pl.BlockSpec((rows_n, hidden), lambda i, s: (i, s))
    inputs = [own, rows, cots, router, ups, downs]
    in_specs = [
        pl.BlockSpec(memory_space=pltpu.SMEM),
        block(row_part),
        block(cot_part),
        pl.BlockSpec(router.shape, lambda i, s: (0, 0)),
    ] + [any_spec] * 2
    aliases = {}
    if aliased:
        aliases = {len(inputs): 0}
        inputs.append(held)
        in_specs.append(any_spec)
    return pl.pallas_call(
        expert_body(slices, packs, cap, width, aliased),
        grid=(steps, slices),
        in_specs=in_specs,
        out_specs=[block(m), block(0), whole_rows, whole_rows, whole_hidden, whole_hidden],
        out_shape=[
            jax.ShapeDtypeStruct((blocks, micro_count * cap, width), BF),
            jax.ShapeDtypeStruct((blocks, cap, width), BF),
            jax.ShapeDtypeStruct((total, width), BF),
            jax.ShapeDtypeStruct((total, width), BF),
            jax.ShapeDtypeStruct((total, slices * hidden), BF),
            jax.ShapeDtypeStruct((total, slices * hidden), BF),
        ],
        scratch_shapes=[
            pltpu.VMEM(ups.shape, BF),
            pltpu.VMEM(downs.shape, BF),
            pltpu.VMEM((rows_n, width), BF),
            pltpu.VMEM((rows_n, width), F32),
            pltpu.VMEM((rows_n, width), F32),
            pltpu.SemaphoreType.DMA((2, slices)),
        ],
        input_output_aliases=aliases,
        compiler_params=pltpu.CompilerParams(vmem_limit_bytes=48 * 1024 * 1024),
        cost_estimate=CHEAP,
        name="expert",
    )(*inputs)


CHEAP = pl.CostEstimate(flops=1, bytes_accessed=1, transcendentals=0)
ALONG = (((1,), (1,)), ((), ()))
DOWN = (((0,), (0,)), ((), ()))


def mm(left, right, dims=None):
    if dims is None:
        return jnp.dot(left, right, preferred_element_type=F32)
    return lax.dot_general(left, right, dims, preferred_element_type=F32)


def windows(total_rows):
    for q0 in range(0, total_rows, BLOCK):
        q1 = min(q0 + BLOCK, total_rows)
        yield q0, q1, max(0, (q0 - LONGEST + 1) // 128 * 128)


def visible(info, info_t, q0, q1, k0):
    shape = (q1 - k0, q1 - q0)
    key_pos = lax.broadcasted_iota(jnp.int32, shape, 0) + k0
    query_pos = lax.broadcasted_iota(jnp.int32, shape, 1) + q0
    same_doc = info_t[k0:q1, 0:1] == info[0:1, q0:q1]
    is_real = (info_t[k0:q1, 1:2] == 1.0) | (query_pos == key_pos)
    return (key_pos <= query_pos) & same_doc & is_real


def attend_forward_body(
    tokens_ref, info_ref, gain_ref, bias_ref, qkv_w_ref, out_w_ref,
    keep_ref, send_ref, attn_in_ref, qkv_ref, heads_ref, log_ref,
):
    total_rows = tokens_ref.shape[1]
    local = qkv_w_ref.shape[1]
    info = info_ref[...]
    info_t = info.T
    normed, _ = normalize(tokens_ref[0].astype(F32))
    attn_in = (normed * gain_ref[...] + bias_ref[...]).astype(BF)
    attn_in_ref[...] = attn_in
    for c in range(3):
        qkv_ref[c] = mm(attn_in, qkv_w_ref[c], ALONG).astype(BF)
    for q0, q1, k0 in windows(total_rows):
        allowed = visible(info, info_t, q0, q1, k0)
        for h in range(local // HEAD_DIM):
            part = slice(h * HEAD_DIM, (h + 1) * HEAD_DIM)
            scores = mm(qkv_ref[1, k0:q1, part], qkv_ref[0, q0:q1, part], ALONG)
            scores = jnp.where(allowed, scores * HEAD_DIM**-0.5, MASKED)
            peak = jnp.max(scores, 0, keepdims=True)
            exponent = jnp.exp(scores - peak)
            total = jnp.sum(exponent, 0, keepdims=True)
            weights = (exponent * (1.0 / total)).astype(BF)
            output = mm(qkv_ref[2, k0:q1, part], weights, DOWN)
            heads_ref[q0:q1, part] = output.T.astype(BF)
            log_ref[h : h + 1, q0:q1] = peak + jnp.log(total)
    perm = jnp.where(info_t[:, 3:4] == info[2:3, :], 1.0, 0.0).astype(BF)
    arranged = mm(perm, heads_ref[...]).astype(BF)
    term = mm(arranged, out_w_ref[...]).astype(BF)
    keep_ref[...] = term[: total_rows // 2]
    send_ref[...] = term[total_rows // 2 :]


def attend_forward(m, tokens, info, gain, bias, qkv_weight, out_weight):
    total_rows, width = tokens.shape[1:]
    local = out_weight.shape[0]
    shape = jax.ShapeDtypeStruct
    inputs = [tokens, info, gain[None], bias[None], qkv_weight, out_weight]
    out_shape = [
        shape((total_rows // 2, width), BF),
        shape((total_rows // 2, width), BF),
        shape((total_rows, width), BF),
        shape((3, total_rows, local), BF),
        shape((total_rows, local), BF),
        shape((8, total_rows), F32),
    ]
    return kernel(
        attend_forward_body,
        out_shape,
        "attend_forward",
        grid=(1,),
        in_specs=[picked(x, m) if k == 0 else whole(x.shape) for k, x in enumerate(inputs)],
        out_specs=[whole(x.shape) for x in out_shape],
    )(*inputs)


def attend_backward_body(adds, count):
    def body(*refs):
        blocks, refs = refs[:count], refs[count:]
        info_ref, attn_in_ref, qkv_ref, heads_ref, log_ref, qkv_w_ref, out_w_ref = refs[:7]
        refs = refs[7:]
        if adds:
            earlier_ref, refs = refs[0], refs[1:]
        term_ref, resid_out, sums_ref, grads, key_sum, value_sum = refs
        total_rows = attn_in_ref.shape[0]
        local = out_w_ref.shape[0]
        scale = HEAD_DIM**-0.5
        info = info_ref[...]
        info_t = info.T
        unperm = jnp.where(info_t[:, 2:3] == info[3:4, :], 1.0, 0.0).astype(BF)
        resid = jnp.concatenate([block[...] for block in blocks], 0)
        resid = mm(unperm, resid).astype(BF)
        resid_out[...] = resid
        heads_grad = mm(resid, out_w_ref[...], ALONG).astype(BF)
        key_sum[...] = jnp.zeros(key_sum.shape, F32)
        value_sum[...] = jnp.zeros(value_sum.shape, F32)
        for q0, q1, k0 in windows(total_rows):
            allowed = visible(info, info_t, q0, q1, k0)
            for h in range(local // HEAD_DIM):
                part = slice(h * HEAD_DIM, (h + 1) * HEAD_DIM)
                query, key = qkv_ref[0, q0:q1, part], qkv_ref[1, k0:q1, part]
                value, out_grad = qkv_ref[2, k0:q1, part], heads_grad[q0:q1, part]
                scores = mm(key, query, ALONG) * scale
                scores = jnp.where(allowed, scores, MASKED)
                weights = jnp.exp(scores - log_ref[h : h + 1, q0:q1])
                weight_grad = mm(value, out_grad, ALONG)
                delta = jnp.sum(weights * weight_grad, 0, keepdims=True)
                score_grad = (weights * (weight_grad - delta)).astype(BF)
                grads[0, q0:q1, part] = (scale * mm(key, score_grad, DOWN)).T.astype(BF)
                key_sum[h, k0:q1] += mm(score_grad, query)
                value_sum[h, k0:q1] += mm(weights.astype(BF), out_grad)
        for h in range(local // HEAD_DIM):
            part = slice(h * HEAD_DIM, (h + 1) * HEAD_DIM)
            grads[1, :, part] = (scale * key_sum[h]).astype(BF)
            grads[2, :, part] = value_sum[h].astype(BF)
        term = mm(grads[0], qkv_w_ref[0])
        for c in (1, 2):
            term = term + mm(grads[c], qkv_w_ref[c])
        term_ref[...] = term.astype(BF)
        attn_in = attn_in_ref[...]
        for c in range(4):
            rows = slice(c * local, (c + 1) * local)
            if c < 3:
                found = mm(grads[c], attn_in, DOWN)
            else:
                found = mm(heads_ref[...], resid, DOWN)
            if adds:
                found = found + earlier_ref[rows, :]
            sums_ref[rows, :] = found.astype(sums_ref.dtype)

    return body


def attend_backward(blocks, info, saved, qkv_weight, out_weight, earlier, last):
    attn_in, qkv, heads, log_total = saved
    total_rows, width = attn_in.shape
    local = out_weight.shape[0]
    shape = jax.ShapeDtypeStruct
    inputs = [*blocks, info, attn_in, qkv, heads, log_total, qkv_weight, out_weight]
    if earlier is not None:
        inputs.append(earlier)
    return pl.pallas_call(
        attend_backward_body(earlier is not None, len(blocks)),
        out_shape=[
            shape((total_rows, width), BF),
            shape((total_rows, width), BF),
            shape((4 * local, width), BF if last else F32),
        ],
        scratch_shapes=[
            pltpu.VMEM((3, total_rows, local), BF),
            pltpu.VMEM((local // HEAD_DIM, total_rows, HEAD_DIM), F32),
            pltpu.VMEM((local // HEAD_DIM, total_rows, HEAD_DIM), F32),
        ],
        compiler_params=pltpu.CompilerParams(vmem_limit_bytes=48 * 1024 * 1024),
        cost_estimate=CHEAP,
        name="attend_backward",
    )(*inputs)


def chosen(info, info_t, count):
    return jnp.where(info_t[:count, 3:4] == info[2:3, :], 1.0, 0.0).astype(BF)


def kernel(body, out_shape, name, mebibytes=40, **options):
    return pl.pallas_call(
        body,
        out_shape=out_shape,
        compiler_params=pltpu.CompilerParams(vmem_limit_bytes=mebibytes * 1024 * 1024),
        cost_estimate=CHEAP,
        name=name,
        **options,
    )


def route_body(m, order):
    def body(hid_ref, doc_ref, pad_ref, routes_ref, cot_ref, *outs):
        route_pack(m, order, hid_ref, doc_ref, pad_ref, routes_ref, cot_ref, *outs)

    return body


def route_pack(m, order, hid_ref, doc_ref, pad_ref, routes_ref, cot_ref, info_out, member_ref, table_ref, rows_ref, sent_ref):
    experts, cap, quarter = table_ref.shape
    total_rows, width = cot_ref.shape[1:]
    dealt = lax.broadcasted_iota(jnp.int32, (1, quarter), 1) * len(order)
    deal = jnp.concatenate([dealt + (hid_ref[0] ^ r) for r in order], 1).astype(F32)
    info = jnp.zeros(info_out.shape, F32)
    line = lax.broadcasted_iota(jnp.int32, info.shape, 0)
    routes = routes_ref[m].astype(F32)
    known = (doc_ref[m].astype(F32), pad_ref[m : m + 1, :].astype(F32), None, deal, routes[:1], routes[1:])
    for k, row in enumerate(known):
        if row is not None:
            info = jnp.where(line == k, row, info)
    low = jnp.minimum(info[4:5], info[5:6])
    high = jnp.maximum(info[4:5], info[5:6])
    place = lax.broadcasted_iota(jnp.int32, (1, total_rows), 1).astype(F32)
    key = (low * experts + high) * total_rows + place
    key_t = jnp.where(line == 6, key, info).T
    rank = jnp.sum(jnp.where(key_t[:, 6:7] < key, 1.0, 0.0), 0, keepdims=True)
    info = jnp.where(line == 2, rank, info)
    info_out[...] = info
    perm = chosen(info, info.T, quarter)
    mine = mm(info.astype(BF), perm, ALONG)
    first, second = mine[4:5], mine[5:6]
    names = lax.broadcasted_iota(jnp.int32, (experts, quarter), 0).astype(F32)
    member = jnp.where((first == names) | (second == names), 1.0, 0.0)
    member_ref[...] = member
    shape = (quarter, quarter)
    before = lax.broadcasted_iota(jnp.int32, shape, 0) < lax.broadcasted_iota(jnp.int32, shape, 1)
    place = mm(member.astype(BF), jnp.where(before, 1.0, 0.0).astype(BF))
    rows = mm(perm, cot_ref[0]).astype(BF)
    rows_ref[...] = rows
    slot = lax.broadcasted_iota(jnp.int32, (cap, quarter), 0).astype(F32)
    last = lax.broadcasted_iota(jnp.int32, (cap, width), 0) == cap - 1
    for e in range(experts):
        match = (slot == place[e : e + 1]) & (member[e : e + 1] > 0.5)
        table = jnp.where(match, 1.0, 0.0).astype(BF)
        table_ref[e] = table
        others = jnp.broadcast_to(first + second - e, (8, quarter)).astype(BF)
        other = mm(others, table, ALONG)[:1]
        other = jnp.concatenate([other, jnp.zeros((1, width - cap), F32)], 1)
        sent_ref[e] = jnp.where(last, other, mm(table, rows)).astype(BF)


def whole(shape):
    return pl.BlockSpec(shape, lambda i: (0,) * len(shape))


def picked(values, m):
    return pl.BlockSpec((1,) + values.shape[1:], lambda i: (m, 0, 0))


def route_tokens(m, hid, doc_ids, pad_mask, routes, cotangent, experts, cap, order):
    total_rows, width = cotangent.shape[1:]
    quarter = total_rows // len(order)
    out_shape = [
        jax.ShapeDtypeStruct((8, total_rows), F32),
        jax.ShapeDtypeStruct((experts, quarter), F32),
        jax.ShapeDtypeStruct((experts, cap, quarter), BF),
        jax.ShapeDtypeStruct((quarter, width), BF),
        jax.ShapeDtypeStruct((experts, cap, width), BF),
    ]
    return kernel(
        route_body(m, order),
        out_shape,
        "route",
        grid=(1,),
        in_specs=[
            pl.BlockSpec(memory_space=pltpu.SMEM),
            whole(doc_ids.shape),
            whole(pad_mask.shape),
            whole(routes.shape),
            picked(cotangent, m),
        ],
        out_specs=[whole(x.shape) for x in out_shape],
    )(hid, doc_ids, pad_mask, routes, cotangent)


def middle_body(joined):
    def body(mine_ref, got_ref, tokens_ref, info_ref, member_ref, table_ref, gain_ref, bias_ref, router_ref, *refs):
        if joined:
            cots_ref, refs = refs[0], refs[1:]
        sent_ref, moe_ref, attention_ref, residual_ref, gates_ref = refs
        experts, cap, quarter = table_ref.shape
        info = info_ref[...]
        perm = chosen(info, info.T, quarter)
        attention = mine_ref[...].astype(F32) + got_ref[...].astype(F32)
        attention_ref[...] = attention.astype(BF)
        residual = mm(perm, tokens_ref[0]) + attention
        residual_ref[...] = residual
        normed, _ = normalize(residual)
        moe_in = (normed * gain_ref[...] + bias_ref[...]).astype(BF)
        moe_ref[...] = moe_in
        logits = mm(router_ref[...], moe_in, ALONG)
        member = member_ref[...] > 0.5
        masked = jnp.where(member, logits, MASKED)
        raised = jnp.where(member, jnp.exp(masked - jnp.max(masked, 0, keepdims=True)), 0.0)
        gates_ref[...] = raised / jnp.sum(raised, 0, keepdims=True)
        for e in range(experts):
            sent_ref[e, :cap] = mm(table_ref[e], moe_in).astype(BF)
            if joined:
                sent_ref[e, cap:] = cots_ref[e]

    return body


def middle(m, mine, got, tokens, info, member, table, gain, bias, router_t, cots):
    experts, cap, quarter = table.shape
    width = tokens.shape[2]
    shape = jax.ShapeDtypeStruct
    inputs = [mine, got, tokens, info, member, table, gain[None], bias[None], router_t]
    if cots is not None:
        inputs.append(cots)
    out_shape = [
        shape((experts, cap if cots is None else 2 * cap, width), BF),
        shape((quarter, width), BF),
        shape((quarter, width), BF),
        shape((quarter, width), F32),
        shape((experts, quarter), F32),
    ]
    return kernel(
        middle_body(cots is not None),
        out_shape,
        "middle",
        grid=(1,),
        in_specs=[picked(x, m) if k == 2 else whole(x.shape) for k, x in enumerate(inputs)],
        out_specs=[whole(x.shape) for x in out_shape],
    )(*inputs)


def token_back_body(adds):
    def body(back_ref, table_ref, gates_ref, router_ref, moe_ref, residual_ref, rows_ref, gain_ref, *refs):
        if adds:
            earlier_ref, refs = refs[0], refs[1:]
        grad_ref, small_ref = refs
        experts, cap, quarter = table_ref.shape
        width = moe_ref.shape[1]
        table = table_ref[...].reshape(experts * cap, quarter)
        copies = mm(table, back_ref[...].reshape(experts * cap, width), DOWN)
        lines = []
        for e in range(experts):
            both = mm(back_ref[e, cap - TILE :, :][:, :cap], table_ref[e])
            lines.append(both[TILE - 2 : TILE - 1] + both[TILE - 1 :])
        gate_grad = jnp.concatenate(lines, 0)
        gates = gates_ref[...]
        logit_grad = gates * (gate_grad - jnp.sum(gates * gate_grad, 0, keepdims=True))
        coarse = logit_grad.astype(BF)
        fine = (logit_grad - coarse.astype(F32)).astype(BF)
        router = router_ref[...]
        normed2_grad = copies + mm(coarse, router, DOWN) + mm(fine, router, DOWN)
        normed, scale = normalize(residual_ref[...])
        grad_router = mm(coarse, moe_ref[...]) + mm(fine, moe_ref[...])
        small = [
            jnp.sum(normed2_grad * normed, 0, keepdims=True),
            jnp.sum(normed2_grad, 0, keepdims=True),
            grad_router,
        ]
        spare = small_ref.shape[0] - 2 - experts
        small = jnp.concatenate(small + [jnp.zeros((spare, width), F32)], 0)
        if adds:
            small = small + earlier_ref[...]
        small_ref[...] = small.astype(small_ref.dtype)
        pull = normalize_pull(normed, scale, gain_ref[...], normed2_grad)
        grad_ref[...] = (rows_ref[...].astype(F32) + pull).astype(BF)

    return body


def token_back(back, table, gates, router_t, moe_in, residual, rows, gain, earlier, last):
    quarter, width = moe_in.shape
    small_rows = round_up(2 + table.shape[0], 2 * TILE)
    shape = jax.ShapeDtypeStruct
    inputs = [back, table, gates, router_t, moe_in, residual, rows, gain[None]]
    if earlier is not None:
        inputs.append(earlier)
    out_shape = [shape((quarter, width), BF), shape((small_rows, width), BF if last else F32)]
    return kernel(token_back_body(earlier is not None), out_shape, "token_back")(*inputs)


def weight_body(adds, hidden):
    def body(left_ref, right_ref, *refs):
        if adds:
            earlier, refs = refs[:2], refs[2:]
        outs, turned = refs[:2], refs[2]

        @pl.when(pl.program_id(0) == 0)
        def _():
            turned[...] = left_ref[...].T

        for k in range(2):
            found = mm(turned[...], right_ref[:, k * hidden : (k + 1) * hidden])
            if adds:
                found = found + earlier[k][0].astype(F32)
            outs[k][0] = found.astype(BF)

    return body


def weight_grad(left, right, slices, earlier):
    total, width = left.shape
    hidden = right.shape[1] // slices
    pair = pl.BlockSpec((1, width, hidden), lambda p: (p, 0, 0))
    inputs = [left, right]
    in_specs = [
        pl.BlockSpec((total, width), lambda p: (0, 0)),
        pl.BlockSpec((total, 2 * hidden), lambda p: (0, p)),
    ]
    if earlier is not None:
        inputs += list(earlier)
        in_specs += [pair, pair]
    return kernel(
        weight_body(earlier is not None, hidden),
        [jax.ShapeDtypeStruct((slices // 2, width, hidden), BF)] * 2,
        "weight_grad",
        56,
        grid=(slices // 2,),
        in_specs=in_specs,
        out_specs=[pair, pair],
        scratch_shapes=[pltpu.VMEM((width, total), BF)],
    )(*inputs)


def mix_body(back_ref, table_ref, gates_ref, attention_ref, delta_ref):
    experts, cap, quarter = table_ref.shape
    width = back_ref.shape[2]
    weighted = []
    for e in range(experts):
        weighted.append((table_ref[e].astype(F32) * gates_ref[e : e + 1, :]).astype(BF))
    weighted = jnp.concatenate(weighted, 0)
    mixture = mm(weighted, back_ref[...].reshape(experts * cap, width), DOWN)
    delta_ref[...] = (attention_ref[...].astype(F32) + mixture).astype(BF)


def mix(back, part, table, gates, attention):
    experts, cap, quarter = table.shape
    width = attention.shape[1]
    return kernel(
        mix_body,
        jax.ShapeDtypeStruct((quarter, width), BF),
        "mix",
        grid=(1,),
        in_specs=[
            pl.BlockSpec((experts, cap, width), lambda i: (0, part, 0)),
            pl.BlockSpec((experts, cap, quarter), lambda i: (0, 0, 0)),
            pl.BlockSpec((experts, quarter), lambda i: (0, 0)),
            pl.BlockSpec((quarter, width), lambda i: (0, 0)),
        ],
        out_specs=pl.BlockSpec((quarter, width), lambda i: (0, 0)),
    )(back, table, gates, attention)


def output_body(count):
    def body(*refs):
        blocks, (tokens_ref, info_ref) = refs[:count], refs[count : count + 2]
        out_ref = refs[-1]
        info = info_ref[...]
        info_t = info.T
        unperm = jnp.where(info_t[:, 2:3] == info[3:4, :], 1.0, 0.0).astype(BF)
        delta = jnp.concatenate([block[...] for block in blocks], 0)
        out_ref[0] = tokens_ref[0].astype(F32) + mm(unperm, delta)

    return body


def place_rows(inputs, body, name, held, m, micro_count, more_out=(), smem=0):
    total_rows, width = held[1]
    first = pl.BlockSpec((1, total_rows, width), lambda i: (m, 0, 0))

    in_specs = [picked(x, m) if x.ndim == 3 else whole(x.shape) for x in inputs]
    in_specs[:smem] = [pl.BlockSpec(memory_space=pltpu.SMEM)] * smem
    aliases = {}
    inputs = list(inputs)
    if held[0] is not None:
        aliases = {len(inputs): 0}
        inputs.append(held[0])
        in_specs.append(pl.BlockSpec(memory_space=pl.ANY))
    return kernel(
        body,
        [jax.ShapeDtypeStruct((micro_count, total_rows, width), F32)] + list(more_out),
        name,
        grid=(1,),
        in_specs=in_specs,
        out_specs=[first] + [whole(x.shape) for x in more_out],
        input_output_aliases=aliases,
    )(*inputs)


def input_grad_body(total_rows, half):
    def body(flag_ref, mine_ref, other_ref, tokens_ref, resid_ref, gain_ref, *refs):
        grad_ref, sums_ref = refs[-2:]
        mine, other = mine_ref[...].astype(F32), other_ref[...].astype(F32)
        zero = flag_ref[0] == 0
        low = jnp.where(zero, mine, other)
        high = jnp.where(zero, other, mine)
        grad = jnp.concatenate([low, high], 0)[:total_rows]
        normed, scale = normalize(tokens_ref[0].astype(F32))
        sums = [jnp.sum(grad * normed, 0, keepdims=True), jnp.sum(grad, 0, keepdims=True)]
        sums_ref[...] = jnp.concatenate(sums + [jnp.zeros((6, grad.shape[1]), F32)], 0)
        grad_ref[0] = resid_ref[...].astype(F32) + normalize_pull(normed, scale, gain_ref[...], grad)

    return body


def make_shards(ne, nh):
    def to_experts(blocks):
        return lax.all_to_all(blocks, "expert", split_axis=0, concat_axis=0, tiled=True)

    def reduce_quarters(keep, send):
        bit = 1
        while bit < nh // 2:
            got = swap(send, "hidden", bit)
            half = keep.shape[0] // 2
            send = (keep[half:].astype(F32) + got[half:].astype(F32)).astype(BF)
            keep = (keep[:half].astype(F32) + got[:half].astype(F32)).astype(BF)
            bit *= 2
        return keep, swap(send, "hidden", bit)

    def gather_quarters(rows):
        blocks = [rows]
        bit = nh // 2
        while bit >= 1:
            blocks = blocks + [swap(block, "hidden", bit) for block in blocks]
            bit //= 2
        return blocks

    def quarter_order():
        order = [0]
        bit = nh // 2
        while bit >= 1:
            order = order + [r ^ bit for r in order]
            bit //= 2
        return order

    def begin_sum(rows):
        h = lax.axis_index("hidden")
        count = rows.shape[0] // 2
        flag = h % 2
        kept = lax.dynamic_slice_in_dim(rows, flag * count, count, 0)
        sent = lax.dynamic_slice_in_dim(rows, (1 - flag) * count, count, 0)
        kept = (kept.astype(F32) + swap(sent, "hidden", 1).astype(F32)).astype(BF)
        bit = 2
        while bit < nh // 2:
            kept = (kept.astype(F32) + swap(kept, "hidden", bit).astype(F32)).astype(BF)
            bit *= 2
        return kept

    def end_sum(kept, got):
        kept = (kept.astype(F32) + got.astype(F32)).astype(BF)
        return kept, swap(kept, "hidden", 1)

    def shards(
        tokens,
        doc_ids,
        pad_mask,
        norm1_gain,
        norm1_bias,
        qkv_weight,
        out_weight,
        norm2_gain,
        norm2_bias,
        router,
        routes,
        up_weight,
        down_weight,
        cotangent,
    ):
        micro_count, row_count, width = tokens.shape
        expert_count = router.shape[1]
        top_count = routes.shape[2]
        pack_cap = 2 * row_count * top_count // expert_count
        quarter = row_count // nh
        cap = round_up((pack_cap + (nh - 1) * (expert_count - 1)) // nh + 2, TILE)
        order = quarter_order()
        e_idx = lax.axis_index("expert")
        h_idx = lax.axis_index("hidden")
        micros = range(micro_count)

        ups = lax.all_gather(up_weight[0], "hidden")
        downs = lax.all_gather(down_weight[0], "hidden")

        router_t = router.T
        hid = jnp.full((1,), h_idx, jnp.int32)
        routes_t = routes.transpose(0, 2, 1)
        qkv_t = qkv_weight.transpose(0, 2, 1)

        def route(m):
            return route_tokens(
                m, hid, doc_ids, pad_mask, routes_t, cotangent, expert_count, cap, order
            )

        state = []
        for m in micros:
            if m == 0:
                info, member, table, up_rows, up_sent = route(m)
                upstream_slots = to_experts(up_sent)
                earlier = up_sent
            else:
                info, member, table, up_rows, up_sent = following
                earlier = last_sent
            mine_tokens = after(tokens, earlier)
            keep, send, *saved = attend_forward(
                m, mine_tokens, info, norm1_gain, norm1_bias, qkv_t, out_weight
            )
            mine, got = reduce_quarters(keep, send)
            if m + 1 < micro_count:
                following = route(m + 1)
                got, following = after((got, following), following)
            last_sent, moe_in, attention, residual, gates = middle(
                m,
                mine,
                got,
                mine_tokens,
                info,
                member,
                table,
                norm2_gain,
                norm2_bias,
                router_t,
                None if m == 0 else up_sent,
            )
            if m == micro_count - 1:
                last_sent, ups, downs = after((last_sent, ups, downs), (ups, downs))
            if m == 0:
                received = (to_experts(last_sent), 0, upstream_slots, 0)
            else:
                both = to_experts(last_sent)
                received = (both, 0, both, 1)
            state.append(
                dict(
                    saved=saved,
                    info=info,
                    attention=attention,
                    residual=residual,
                    moe_in=moe_in,
                    gates=gates,
                    table=table,
                    up_rows=up_rows,
                    received=received,
                )
            )

        own_expert = jnp.stack([e_idx, h_idx]).astype(jnp.int32)
        held, earlier = None, (None, None)
        for m in micros:
            s = state[m]
            rows, row_part, cots, cot_part = s["received"]
            if m == 0:
                rows = after(rows, last_sent)
            held, copies, *work = run_expert(
                own_expert,
                rows,
                row_part,
                cots,
                cot_part,
                router_t,
                ups,
                downs,
                held,
                m,
                micro_count,
            )
            if m < micro_count - 1:
                earlier = (
                    weight_grad(work[0], work[3], nh, earlier[0]),
                    weight_grad(work[1], work[2], nh, earlier[1]),
                )
                s["copies_back"] = to_experts(after(copies, earlier))
            else:
                s["copies_back"] = to_experts(copies)
                works = work
        small = None
        copies_back = [s["copies_back"] for s in state]
        copies_back[:-1], works = after((copies_back[:-1], works), copies)
        for m in micros:
            s = state[m]
            last = m == micro_count - 1
            if m == micro_count - 1:
                works = after(works, grad_low)
                first = weight_grad(works[0], works[3], nh, earlier[0])
                works, state[0]["resid_all"] = after(
                    (works, state[0]["resid_all"]), (first, state[0]["resid_all"])
                )
                slabs = (
                    first,
                    weight_grad(works[1], works[2], nh, earlier[1]),
                )
                copies_back[1:] = after(copies_back[1:], slabs)
                got = [swap(send, "hidden", 1) for _, send in slabs]
                halves = [
                    jnp.stack(
                        [
                            (keep[p].astype(F32) + other[p].astype(F32)).astype(BF)
                            for (keep, _), other in zip(slabs, got)
                        ]
                    )
                    for p in range(nh // 2)
                ]
            grad_low, small = token_back(
                copies_back[m],
                s["table"],
                s["gates"],
                router_t,
                s["moe_in"],
                s["residual"],
                s["up_rows"],
                norm2_gain,
                small,
                last,
            )
            s["resid_all"] = gather_quarters(grad_low)

        firsts = halves
        gathers = [s["resid_all"] for s in state]

        def finish(part):
            bit = 2
            while bit < nh:
                got = [swap(slab, "hidden", bit) for slab in part[1::2]]
                part = [
                    (mine.astype(F32) + other.astype(F32)).astype(BF)
                    for mine, other in zip(part[0::2], got)
                ]
                bit *= 2
            rows = part[0].reshape(2, ne, width // ne, -1).transpose(1, 0, 2, 3)
            return rows.reshape(ne, 2 * width // ne, -1)

        owned = finish(after(halves, gathers))

        flag = jnp.full((1,), h_idx % 2, jnp.int32)
        pack_sums = None
        input_grads, norm1_sums = None, 0.0
        out_back = to_experts(after(held, copies_back[-1]))
        terms, resids = [], []
        state[0]["resid_all"] = after(state[0]["resid_all"], (firsts, grad_low))
        for m in micros:
            s = state[m]
            term, resid, pack_sums = attend_backward(
                s["resid_all"],
                s["info"],
                s["saved"],
                qkv_t,
                out_weight,
                pack_sums,
                m == micro_count - 1,
            )
            terms.append(term)
            resids.append(resid)
        terms[:-1] = after(terms[:-1], terms[-1])
        terms[-1] = jnp.concatenate([terms[-1], small], 0)
        begun = [begin_sum(term) for term in terms]

        share = pack_sums.reshape(ne, -1, width)
        bit = 1
        while bit < ne:
            side = (e_idx // bit) % 2
            if bit == 2:
                share, out_back, begun = after((share, out_back, begun), (out_back, begun))
                begun = [(kept, swap(kept, "hidden", nh // 2)) for kept in begun]
            if bit == ne // 2:
                deltas = [
                    mix(out_back, m, s["table"], s["gates"], s["attention"])
                    for m, s in enumerate(state)
                ]
                needed = (share, owned, begun[:1], deltas)
                share, owned, begun[:1], deltas = lax.optimization_barrier(needed)
            pairs = share.reshape(share.shape[0] // 2, 2, -1, width)
            kept = lax.dynamic_index_in_dim(pairs, side, 1, False)
            sent = lax.dynamic_index_in_dim(pairs, 1 - side, 1, False)
            share = (kept.astype(F32) + swap(sent, "expert", bit).astype(F32)).astype(BF)
            bit *= 2
        share = share[0]

        for m in micros:
            s = state[m]
            resid = resids[m]
            mine, other = end_sum(*after(begun[m], share))
            input_grads, sums = place_rows(
                [flag, mine, other, tokens, resid, norm1_gain[None]],
                input_grad_body(row_count, mine.shape[0]),
                "input_grad",
                (input_grads, tokens.shape[1:]),
                m,
                micro_count,
                [jax.ShapeDtypeStruct((8, width), F32)],
                1,
            )
            norm1_sums = norm1_sums + sums


        half = small.shape[0]
        kept = terms[-1].shape[0] // 2
        small = jnp.where(flag == 0, other[kept - half :], mine[kept - half :]).astype(F32)
        small = jnp.concatenate([norm1_sums[:2], small[: 2 + expert_count]], 0)
        small = jnp.pad(small, ((0, round_up(small.shape[0], 8) - small.shape[0]), (0, 0)))
        bit = 1
        while bit < ne:
            small = small + swap(small, "expert", bit)
            bit *= 2
        outputs = None
        for m in micros:
            s = state[m]
            blocks = after(gather_quarters(deltas[m]), norm1_sums)
            (outputs,) = place_rows(
                [*blocks, tokens, s["info"]],
                output_body(len(blocks)),
                "output",
                (outputs, tokens.shape[1:]),
                m,
                micro_count,
            )
        gathered = share[None]
        bit = ne // 2
        while bit >= 1:
            if bit == 1:
                parts = to_experts(after(owned, (out_back, gathered, begun)))[ne // 2 :].astype(F32)
                gathered, outputs = after((gathered, outputs), outputs)
            gathered = jnp.concatenate([gathered, swap(gathered, "expert", bit)], 0)
            bit //= 2
        bits = []
        bit = ne // 2
        found = [0]
        while bit >= 1:
            found = found + [r ^ bit for r in found]
            bit //= 2
        where = jnp.zeros((ne,), jnp.int32)
        slots = jnp.array([found.index(r) for r in range(ne)], jnp.int32)
        where = slots[jnp.arange(ne, dtype=jnp.int32) ^ e_idx]
        flat = gathered[where].astype(F32).reshape(4, -1, width)
        return (
            outputs,
            input_grads,
            small[0],
            small[1],
            flat[:3].transpose(0, 2, 1),
            flat[3],
            small[2],
            small[3],
            small[4 : 4 + expert_count].T,
            parts[:, : width // ne],
            parts[:, width // ne :],
        )

    return shards


def solution(mesh):
    placed = (
        P(None, "expert", None),
        P(None, "expert", None),
        P(None, "expert"),
        P(),
        P(),
        P(None, None, "hidden"),
        P("hidden", None),
        P(),
        P(),
        P(),
        P(None, "expert", None),
        P("expert", None, "hidden"),
        P("expert", None, "hidden"),
        P(None, "expert", None),
    )
    return jax.shard_map(
        make_shards(mesh.shape["expert"], mesh.shape["hidden"]),
        mesh=mesh,
        in_specs=placed,
        out_specs=(
            P(None, "expert", None),
            P(None, "expert", None),
            P(),
            P(),
            P(None, None, "hidden"),
            P("hidden", None),
            P(),
            P(),
            P(),
            P(None, "expert", "hidden"),
            P(None, "expert", "hidden"),
        ),
        check_vma=False,
    )
```
